32 devices in a mesh: dp: 16 (over z, y, x), tensor: 2 (over core).
Axes of the slice: x: 2, y: 2, z: 4, core: 2. Of those that a mesh axis runs over, the one named last changes fastest.
Arguments:
- tokens: bfloat16 [16384, 768], P(('dp', 'tensor')), may hold values from -6 to 6
- cotangent: bfloat16 [16384, 768], P(('dp', 'tensor')), may hold values from -6 to 6
- segment_ids: int32 [16384], P('dp'), may hold values from 0 to 17, as said below
- norm1_gain: float32 [768], replicated, may hold values from 0.5 to 1.5
- w_query: float32 [768, 768], P('dp', 'tensor'), may hold values from -0.21875 to 0.21875
- w_key: float32 [768, 768], P('dp', 'tensor'), may hold values from -0.21875 to 0.21875
- w_value: float32 [768, 768], P('dp', 'tensor'), may hold values from -0.21875 to 0.21875
- pre_mix: float32 [12, 12], replicated, may hold values from -1.75 to 1.75
- post_mix: float32 [12, 12], replicated, may hold values from -1.75 to 1.75
- w_output: float32 [768, 768], P('tensor', 'dp'), may hold values from -1.25 to 1.25
- norm2_gain: float32 [768], replicated, may hold values from 0.5 to 1.5
- w_in: float32 [768, 3072], P('dp', 'tensor'), may hold values from -0.21875 to 0.21875
- w_out: float32 [3072, 768], P('tensor', 'dp'), may hold values from -0.109375 to 0.109375
Outputs:
- output: bfloat16 [16384, 768], P(('dp', 'tensor'))
- grad_tokens: bfloat16 [16384, 768], P(('dp', 'tensor'))
- grad_norm1_gain: float32 [768], replicated
- grad_w_query: float32 [768, 768], P('dp', 'tensor')
- grad_w_key: float32 [768, 768], P('dp', 'tensor')
- grad_w_value: float32 [768, 768], P('dp', 'tensor')
- grad_pre_mix: float32 [12, 12], replicated
- grad_post_mix: float32 [12, 12], replicated
- grad_w_output: float32 [768, 768], P('tensor', 'dp')
- grad_norm2_gain: float32 [768], replicated
- grad_w_in: float32 [768, 3072], P('dp', 'tensor')
- grad_w_out: float32 [3072, 768], P('tensor', 'dp')
The draws below stay inside these ranges and needn't reach their ends.
Inputs may be any that keep to these rules, and one draw needn't show every extreme that they name: `segment_ids`: within each sequence of 1024 tokens the ids start at 0 and rise by one at each document boundary; documents hold 60 to 800 tokens, the last of a sequence cut at its end; no boundary lies at position 512.
All inputs are finite; a program needn't handle non-finite values.
Results may differ from the reference program's by a relative error of at most 0.02.
Values may be sent and summed in bfloat16 or wider, within the bound.
No kernel may reach another device: no remote copies, remote signals or barrier semaphores. Data moves between devices by JAX's collectives and lax.ppermute only.
A program may use at most 384 MiB of HBM per device.

```python
import jax
import jax.numpy as jnp
from jax import lax

D = 768
FF = 3072
HEADS = 12
HEAD_DIM = 64
SEQ = 1024
INNER = 768
SEQUENCES = 16
TOKENS = 16384


def document_ids(key):
    base = jax.random.fold_in(key, 4711)
    sizes = jax.random.randint(base, (SEQUENCES, SEQ // 60 + 2), 61, 800)
    sizes = sizes.at[0].set(60)
    ends = jnp.cumsum(sizes, axis=1)
    ends = ends + (ends == SEQ // 2).astype(jnp.int32)
    position = jnp.arange(SEQ)
    return jnp.sum((ends[:, None, :] <= position[None, :, None]).astype(jnp.int32), axis=2)


def draw_segment_ids(key, part):
    return document_ids(key).reshape(TOKENS).astype(jnp.int32)


def levels(key, dims, split, smallest, top_value):
    def one(dim, blocks):
        draws = jax.random.uniform(jax.random.fold_in(jax.random.fold_in(key, 6), dim), (blocks,), jnp.float32, smallest / len(split), top_value / len(split))
        return jnp.repeat(jnp.exp(draws), dims[dim] // blocks).reshape((-1,) + (1,) * (len(dims) - dim - 1))

    level = one(*split[0])
    for cut in split[1:]:
        level = level * one(*cut)
    return level


def normal_values(stream_key, extent, deviation, limit, shards=(), held_as=jnp.bfloat16):
    level = levels(stream_key, extent, shards, -0.22, 0.18) if shards else 1.0
    array = jax.random.normal(stream_key, extent, jnp.float32) * deviation * level
    return jnp.minimum(jnp.maximum(array, -limit), limit).astype(held_as)


def setup_inputs(seed: int = 0) -> dict:
    splits = jax.random.split(jax.random.key(seed), 14)
    tokens = normal_values(splits[0], (TOKENS, D), 1.0, 6.0, ((0, 32),))
    cotangent = normal_values(splits[1], (TOKENS, D), 1.0, 6.0, ((0, 32),))
    segment_ids = draw_segment_ids(jax.random.fold_in(splits[13], 71), 0)
    norm1_gain = jnp.clip(1.0 + 0.1 * jax.random.normal(splits[3], (D,), jnp.float32), 0.5, 1.5)
    w_query = normal_values(splits[4], (D, INNER), D ** -0.5, 0.21875, ((0, 16), (1, 2)), jnp.float32)
    w_key = normal_values(splits[5], (D, INNER), D ** -0.5, 0.21875, ((0, 16), (1, 2)), jnp.float32)
    w_value = normal_values(splits[6], (D, INNER), D ** -0.5, 0.21875, ((0, 16), (1, 2)), jnp.float32)
    pre_mix = normal_values(splits[7], (HEADS, HEADS), HEADS ** -0.5, 1.75, (), jnp.float32)
    post_mix = normal_values(splits[8], (HEADS, HEADS), HEADS ** -0.5, 1.75, (), jnp.float32)
    w_output = normal_values(splits[9], (INNER, D), (D // 32) ** -0.5, 1.25, ((0, 2), (1, 16)), jnp.float32)
    norm2_gain = jnp.clip(1.0 + 0.1 * jax.random.normal(splits[10], (D,), jnp.float32), 0.5, 1.5)
    w_in = normal_values(splits[11], (D, FF), D ** -0.5, 0.21875, ((0, 16), (1, 2)), jnp.float32)
    w_out = normal_values(splits[12], (FF, D), FF ** -0.5, 0.109375, ((0, 2), (1, 16)), jnp.float32)
    return {"tokens": tokens, "cotangent": cotangent, "segment_ids": segment_ids, "norm1_gain": norm1_gain, "w_query": w_query, "w_key": w_key, "w_value": w_value, "pre_mix": pre_mix, "post_mix": post_mix, "w_output": w_output, "norm2_gain": norm2_gain, "w_in": w_in, "w_out": w_out}


HIGH = lax.Precision.HIGHEST

@jax.custom_vjp
def low(v):
    return lax.optimization_barrier(v.astype(jnp.bfloat16)).astype(jnp.float32)

@jax.custom_vjp
def low_back(v):
    return v

def low_keep(v):
    return (low(v), None)

def low_pass(kept, grad):
    return (grad,)

def back_keep(v):
    return (v, None)

def back_low(kept, grad):
    return (low(grad),)
low.defvjp(low_keep, low_pass)
low_back.defvjp(back_keep, back_low)

def both_ways(value):
    return low(low_back(value))

def matmul(left, right):
    return jnp.dot(left, right, precision=HIGH)

def rms_norm(values, gain):
    return values * lax.rsqrt(lax.optimization_barrier(jnp.mean(values * values, axis=-1, keepdims=True)) + 1e-06) * gain

def layer(inputs, gain_one, w_query, w_key, w_value, pre_mix, post_mix, w_output, gain_two, w_in, w_out, segment_ids):
    query_low = low(w_query)
    key_low = low(w_key)
    value_low = low(w_value)
    output_low = low(w_output)
    in_low = low(w_in)
    out_low = low(w_out)
    position = jnp.arange(SEQ)

    def one_sequence(pieces):
        rows_in, seg_row = pieces
        act_one = low(rms_norm(rows_in, gain_one))
        query = both_ways(matmul(act_one, query_low)).reshape(SEQ, HEADS, HEAD_DIM)
        key = both_ways(matmul(act_one, key_low)).reshape(SEQ, HEADS, HEAD_DIM)
        value = both_ways(matmul(act_one, value_low)).reshape(SEQ, HEADS, HEAD_DIM)
        scores = low_back(0.125 * jnp.einsum('qhd,khd->hqk', query, key, precision=HIGH))
        logits = low_back(jnp.einsum('hg,gqk->hqk', pre_mix, scores, precision=HIGH))
        allowed = (position[None, :] <= position[:, None]) & (seg_row[:, None] == seg_row[None, :])
        probs = jax.nn.softmax(jnp.where(allowed[None], logits, -1e+30), axis=-1)
        mixed = both_ways(jnp.einsum('kh,hqj->kqj', post_mix, probs, precision=HIGH))
        attended = jnp.einsum('kqj,jkd->qkd', mixed, value, precision=HIGH).reshape(SEQ, INNER)
        heads_out = both_ways(attended)
        middle = rows_in + low_back(matmul(heads_out, output_low))
        act_two = low(rms_norm(middle, gain_two))
        pre_act = low_back(matmul(act_two, in_low))
        hidden = both_ways(jax.nn.gelu(pre_act, approximate=True))
        return middle + matmul(hidden, out_low)
    result = lax.map(jax.checkpoint(one_sequence), (inputs.reshape(SEQUENCES, SEQ, D), segment_ids.reshape(SEQUENCES, SEQ)))
    return result.reshape(TOKENS, D)

def reference(tokens, cotangent, segment_ids, norm1_gain, w_query, w_key, w_value, pre_mix, post_mix, w_output, norm2_gain, w_in, w_out):

    def forward(inputs, gain_one, query_w, key_w, value_w, pre_w, post_w, output_w, gain_two, in_w, out_w):
        return layer(inputs, gain_one, query_w, key_w, value_w, pre_w, post_w, output_w, gain_two, in_w, out_w, segment_ids)
    output, pullback = jax.vjp(forward, tokens.astype(jnp.float32), norm1_gain, w_query, w_key, w_value, pre_mix, post_mix, w_output, norm2_gain, w_in, w_out)
    grads = pullback(cotangent.astype(jnp.float32))
    return (output.astype(jnp.bfloat16), grads[0].astype(jnp.bfloat16), grads[1], grads[2], grads[3], grads[4], grads[5], grads[6], grads[7], grads[8], grads[9], grads[10])
```

```python
import jax, jax.numpy as jnp
from jax import lax
from jax.experimental import pallas as pl
from jax.experimental.pallas import tpu as pltpu

HEADS=12; HD=64; INNER=768; SEQ=1024; BLK=256
LOG2E=1.4426950408889634
BF=jnp.bfloat16; F32=jnp.float32

def chunks(c):
    return (1,4) if c==0 else (3,2)

def blocks_of(c):
    return (0,3) if c==0 else (2,1)

def dot(a,b): return jnp.dot(a,b,preferred_element_type=F32)

def k1_body(core_ref, pre_ref, segc_ref, segr_ref, k_ref, qT_ref, pT_ref, mask_ref):
    h=pl.program_id(0)
    def run(c):
        nj=chunks(c); bl=blocks_of(c)
        base=(0,nj[0]*BLK)
        @pl.when(h==0)
        def _():
            for b in range(2):
                qpos=lax.broadcasted_iota(jnp.int32,(BLK,BLK),1)+bl[b]*BLK
                qseg=segr_ref[:,b*BLK:(b+1)*BLK]
                for j in range(nj[b]):
                    kpos=lax.broadcasted_iota(jnp.int32,(BLK,BLK),0)+j*BLK
                    kseg=segc_ref[j*BLK:(j+1)*BLK,:]
                    ok=(kpos<=qpos)&(kseg==qseg)
                    mask_ref[base[b]+j*BLK:base[b]+(j+1)*BLK,:]=jnp.where(ok,0.0,-1e30)
        for b in range(2):
            n=nj[b]*BLK
            qs=jnp.concatenate([(qT_ref[g*HD:(g+1)*HD,b*BLK:(b+1)*BLK].astype(F32)*pre_ref[h,g]).astype(BF) for g in range(HEADS)],axis=0)
            s=dot(k_ref[:n,:],qs)+mask_ref[base[b]:base[b]+n,:]
            m=jnp.max(s,axis=0,keepdims=True)
            e=jnp.exp2(s-m)
            inv=1.0/jnp.sum(e,axis=0,keepdims=True)
            pT_ref[base[b]:base[b]+n,:]=(e*inv).astype(BF)
    for c in range(2):
        pl.when(core_ref[0]==c)(lambda c=c: run(c))

def smem(): return pl.BlockSpec(memory_space=pltpu.SMEM)
def full(s): return pl.BlockSpec(s,lambda h:(0,)*len(s))
PAR=pltpu.CompilerParams(vmem_limit_bytes=56*1024*1024)

def k1(core,pre,segc,segr,k,qT):
    return pl.pallas_call(k1_body, grid=(HEADS,),
        in_specs=[smem(),smem(),full((SEQ,1)),full((1,512)),full((SEQ,INNER)),full((INNER,512))],
        out_specs=pl.BlockSpec((5*BLK,BLK),lambda h:(0,h)),
        out_shape=jax.ShapeDtypeStruct((5*BLK,HEADS*BLK),BF),
        scratch_shapes=[pltpu.VMEM((5*BLK,BLK),F32)],
        compiler_params=PAR, name="logits_softmax")(core,pre,segc,segr,k,qT)

def k2_body(core_ref, post_ref, vT_ref, pT_ref, uT_ref, hT_ref, acc_ref):
    h=pl.program_id(0)
    def run(c):
        nj=chunks(c); base=(0,nj[0]*BLK)
        for b in range(2):
            n=nj[b]*BLK
            u=dot(vT_ref[:,:n],pT_ref[base[b]:base[b]+n,:])
            cs=slice(b*BLK,(b+1)*BLK)
            uT_ref[:,cs]=u.astype(BF)
            for k in range(HEADS):
                rs=slice(k*HD,(k+1)*HD)
                acc_ref[rs,cs]+=u[rs,:]*post_ref[k,h]
    @pl.when(h==0)
    def _(): acc_ref[...]=jnp.zeros_like(acc_ref)
    for c in range(2):
        pl.when(core_ref[0]==c)(lambda c=c: run(c))
    @pl.when(h==HEADS-1)
    def _(): hT_ref[...]=acc_ref[...].astype(BF)

def k2(core,post,vT,pT):
    return pl.pallas_call(k2_body, grid=(HEADS,),
        in_specs=[smem(),smem(),full((INNER,SEQ)),pl.BlockSpec((5*BLK,BLK),lambda h:(0,h))],
        out_specs=[pl.BlockSpec((INNER,512),lambda h:(h,0)),full((INNER,512))],
        out_shape=[jax.ShapeDtypeStruct((HEADS*INNER,512),BF),jax.ShapeDtypeStruct((INNER,512),BF)],
        scratch_shapes=[pltpu.VMEM((INNER,512),F32)],
        compiler_params=PAR, name="attend")(core,post,vT,pT)

def b1_body(core_ref, post_ref, prep_ref, v_ref, ghT_ref, gh_ref, pT_ref, uT_ref, gL_ref, gV_ref, gpost_ref, acc_ref):
    h=pl.program_id(0)
    def run(c):
        nj=chunks(c); base=(0,nj[0]*BLK)
        for b in range(2):
            n=nj[b]*BLK
            cs=slice(b*BLK,(b+1)*BLK)
            r=jnp.zeros((1,BLK),F32)
            parts=[]
            for k in range(HEADS):
                rs=slice(k*HD,(k+1)*HD)
                gk=ghT_ref[rs,cs].astype(F32)
                G=jnp.sum(gk*uT_ref[rs,cs].astype(F32),axis=0,keepdims=True)
                w=post_ref[k,h]
                gpost_ref[k:k+1,cs]=G
                r=r+G*w
                parts.append((gk*w).astype(BF))
            gs=jnp.concatenate(parts,axis=0)
            gP=dot(v_ref[:n,:],gs)
            p=pT_ref[base[b]:base[b]+n,:]
            gL_ref[base[b]:base[b]+n,:]=(p.astype(F32)*(gP-r)).astype(BF)
            g2=(gh_ref[cs,:].astype(F32)*prep_ref[0]).astype(BF)
            acc_ref[:n,:]+=dot(p,g2)
    @pl.when(h==0)
    def _(): acc_ref[...]=jnp.zeros_like(acc_ref)
    for c in range(2):
        pl.when(core_ref[0]==c)(lambda c=c: run(c))
    @pl.when(h==HEADS-1)
    def _(): gV_ref[...]=acc_ref[...].astype(BF)

def b1(core,post,post_rep,v,ghT,gh,pT,uT):
    return pl.pallas_call(b1_body, grid=(HEADS,),
        in_specs=[smem(),smem(),pl.BlockSpec((1,1,INNER),lambda h:(h,0,0)),full((SEQ,INNER)),full((INNER,512)),full((512,INNER)),
                  pl.BlockSpec((5*BLK,BLK),lambda h:(0,h)),pl.BlockSpec((INNER,512),lambda h:(h,0))],
        out_specs=[pl.BlockSpec((5*BLK,BLK),lambda h:(0,h)),full((SEQ,INNER)),pl.BlockSpec((None,HEADS,512),lambda h:(h,0,0))],
        out_shape=[jax.ShapeDtypeStruct((5*BLK,HEADS*BLK),BF),jax.ShapeDtypeStruct((SEQ,INNER),BF),jax.ShapeDtypeStruct((HEADS,HEADS,512),F32)],
        scratch_shapes=[pltpu.VMEM((SEQ,INNER),F32)],
        compiler_params=PAR, name="attend_back")(core,post,post_rep,v,ghT,gh,pT,uT)

def b2_body(core_ref, pre_ref, prep_ref, kT_ref, qT_ref, q_ref, gL_ref, gQ_ref, gK_ref, gpre_ref, accq_ref, acck_ref):
    h=pl.program_id(0)
    def run(c):
        nj=chunks(c); base=(0,nj[0]*BLK)
        for b in range(2):
            n=nj[b]*BLK
            cs=slice(b*BLK,(b+1)*BLK)
            g=gL_ref[base[b]:base[b]+n,:]
            w=dot(kT_ref[:,:n],g)
            for k in range(HEADS):
                rs=slice(k*HD,(k+1)*HD)
                wk=w[rs,:]
                gpre_ref[k:k+1,cs]=jnp.sum(qT_ref[rs,cs].astype(F32)*wk,axis=0,keepdims=True)
                accq_ref[rs,cs]+=wk*pre_ref[h,k]
            q2=(q_ref[cs,:].astype(F32)*prep_ref[0]).astype(BF)
            acck_ref[:n,:]+=dot(g,q2)
    @pl.when(h==0)
    def _():
        accq_ref[...]=jnp.zeros_like(accq_ref)
        acck_ref[...]=jnp.zeros_like(acck_ref)
    for c in range(2):
        pl.when(core_ref[0]==c)(lambda c=c: run(c))
    @pl.when(h==HEADS-1)
    def _():
        gQ_ref[...]=accq_ref[...].astype(BF)
        gK_ref[...]=acck_ref[...].astype(BF)

def b2(core,pre,pre_rep,kT,qT,q,gL):
    return pl.pallas_call(b2_body, grid=(HEADS,),
        in_specs=[smem(),smem(),pl.BlockSpec((1,1,INNER),lambda h:(h,0,0)),full((INNER,SEQ)),full((INNER,512)),full((512,INNER)),
                  pl.BlockSpec((5*BLK,BLK),lambda h:(0,h))],
        out_specs=[full((INNER,512)),full((SEQ,INNER)),pl.BlockSpec((None,HEADS,512),lambda h:(h,0,0))],
        out_shape=[jax.ShapeDtypeStruct((INNER,512),BF),jax.ShapeDtypeStruct((SEQ,INNER),BF),jax.ShapeDtypeStruct((HEADS,HEADS,512),F32)],
        scratch_shapes=[pltpu.VMEM((INNER,512),F32),pltpu.VMEM((SEQ,INNER),F32)],
        compiler_params=PAR, name="scores_back")(core,pre,pre_rep,kT,qT,q,gL)


from jax.sharding import PartitionSpec as P

EPSILON=1e-06
HALF=SEQ//2


def gelu(v):
    return jax.nn.gelu(v,approximate=True)

def rms_forward(v):
    inv=lax.rsqrt(jnp.mean(v*v,axis=-1,keepdims=True)+EPSILON)
    return v*inv,inv

def rms_backward(grad,normed,inv,gain):
    scaled=grad*gain
    back=inv*(scaled-normed*jnp.mean(scaled*normed,axis=-1,keepdims=True))
    return back,jnp.sum(grad*normed,axis=0)

def dg(a,b,ca,cb):
    return lax.dot_general(a,b,(((ca,),(cb,)),((),())),preferred_element_type=F32)

def swap(v):
    return lax.ppermute(v,"tensor",[(0,1),(1,0)])

def hop(v,mask):
    n=lax.axis_size("dp")
    return lax.ppermute(v,"dp",[(i,i^mask) for i in range(n)])

def place_body(me_ref,*refs):
    ins,out,sems=refs[:4],refs[4],refs[5]
    me=me_ref[0]
    nz,r,h=ins[0].shape[1:]
    copies=[]
    for t,ref in enumerate(ins):
        w=ref.shape[3]
        col=0 if t<2 else h
        for i in range(2):
            for j in range(nz):
                e=4*j+((2*i+t) if t<2 else (i+2*(t-2)))
                row=pl.multiple_of(lax.bitwise_xor(me,e)*r,16)
                cp=pltpu.make_async_copy(ref.at[i,j],out.at[pl.ds(row,r),pl.ds(col,w)],sems.at[len(copies)])
                cp.start()
                copies.append(cp)
    for cp in copies:
        cp.wait()

def place(me,parts):
    two,nz,r,h=parts[0].shape
    total=h+parts[2].shape[3]
    if r%16:
        a=jnp.stack([parts[0],parts[1]],axis=0)
        b=jnp.stack([parts[2],parts[3]],axis=1)
        whole=jnp.concatenate([a,b],axis=-1)
        whole=whole.transpose(2,1,0,3,4).reshape(4*nz,r,total)
        order=lax.bitwise_xor(lax.iota(jnp.int32,4*nz),me)
        return jnp.take(whole,order,axis=0).reshape(4*nz*r,total)
    return pl.pallas_call(
        place_body,
        in_specs=[pl.BlockSpec(memory_space=pltpu.SMEM)]+[pl.BlockSpec(memory_space=pl.ANY)]*4,
        out_specs=pl.BlockSpec(memory_space=pl.ANY),
        out_shape=jax.ShapeDtypeStruct((4*nz*r,total),BF),
        scratch_shapes=[pltpu.SemaphoreType.DMA((8*nz,))],
        name="place")(me.reshape(1),*parts)

def gather_rows(shard):
    n=lax.axis_size("dp")
    me=lax.axis_index("dp")
    nz=n//4
    if nz==4:
        z=jnp.stack([shard]+[hop(shard,4*e) for e in range(1,nz)],axis=0)
    else:
        z=shard[None]
        bit=1
        while bit<nz:
            z=jnp.concatenate([z,hop(z,4*bit)],axis=0)
            bit*=2
    h=shard.shape[1]//2
    a,b=z[:,:,:h],z[:,:,h:]
    a2=jnp.stack([a,hop(a,2)],axis=0)
    b2=jnp.stack([b,hop(b,1)],axis=0)
    ax=hop(a2,1)
    by=hop(b2,2)
    return place(me,(a2,ax,b2,by))

def pick(v,i,axis):
    return lax.dynamic_index_in_dim(v,i,axis,keepdims=False)

def scatter_rows(g):
    n=lax.axis_size("dp")
    me=lax.axis_index("dp")
    nz=n//4
    mx,my,mz=me&1,(me>>1)&1,me>>2
    rows,cols=g.shape
    v=g.reshape(nz,2,2,rows//n,cols)
    h=cols//2
    a,b=v[...,:h],v[...,h:]
    add=lambda p,q: (p.astype(F32)+q.astype(F32)).astype(BF)
    a=add(pick(a,mx,2),hop(pick(a,1-mx,2),1))
    b=add(pick(b,my,1),hop(pick(b,1-my,1),2))
    a=add(pick(a,my,1),hop(pick(a,1-my,1),2))
    b=add(pick(b,mx,1),hop(pick(b,1-mx,1),1))
    z=jnp.concatenate([a,b],axis=-1)
    if nz==4:
        total=pick(z,mz,0).astype(F32)
        for e in range(1,nz):
            total=total+hop(pick(z,mz^e,0),4*e).astype(F32)
        return total
    bit=nz//2
    while bit:
        w=z.reshape(2,bit,z.shape[1],z.shape[2])
        mb=(mz&bit)//bit
        z=add(pick(w,mb,0),hop(pick(w,1-mb,0),4*bit))
        bit//=2
    return z[0].astype(F32)

def sum_all(v):
    n=lax.axis_size("dp")
    v=v+swap(v)
    v=v+(hop(v,1)+hop(v,2)+hop(v,3))
    if n==16:
        return v+(hop(v,4)+hop(v,8)+hop(v,12))
    bit=4
    while bit<n:
        v=v+hop(v,bit)
        bit*=2
    return v

def on_device(tokens,cotangent,segment_ids,norm1_gain,w_query,w_key,w_value,pre_mix,post_mix,w_output,norm2_gain,w_in,w_out):
    core=lax.axis_index("tensor")
    first=core==0
    cat=lambda *a: jnp.concatenate(a,axis=0)
    cols=lambda *a: jnp.concatenate(a,axis=1)
    low=lambda v: v.astype(BF)
    natural=lambda mine,other: cat(jnp.where(first,mine,other),jnp.where(first,other,mine))
    rel=lambda m,axis: jnp.where(first,m,jnp.roll(m,HEADS//2,axis=axis))
    HI=INNER//2

    qk=gather_rows(cols(low(w_query),low(w_key)))
    qk_o=swap(qk)
    vo=gather_rows(cols(low(w_value),low(w_output.T)))
    vo_o=swap(vo)
    win=gather_rows(low(w_in))
    woutT=gather_rows(low(w_out.T))
    wq=cols(qk[:,:HI],qk_o[:,:HI])
    wk=cols(qk[:,HI:],qk_o[:,HI:])
    wv=cols(vo[:,:HI],vo_o[:,:HI])
    woT=cols(vo[:,HI:],vo_o[:,HI:])

    x_loc,x_oth=tokens,swap(tokens)
    cot_oth=swap(cotangent)
    normed_loc,inv_loc=rms_forward(x_loc.astype(F32))
    act_loc=low(normed_loc*norm1_gain)
    act_oth=low(rms_forward(x_oth.astype(F32))[0]*norm1_gain)
    act_nat=natural(act_loc,act_oth)
    act_own=cat(act_loc[:BLK],act_oth[BLK:])
    x_own=cat(x_loc[:BLK],x_oth[BLK:]).astype(F32)
    cot_own=cat(cotangent[:BLK],cot_oth[BLK:])
    cot_grp=cat(cot_own,cot_oth[:BLK],cotangent[BLK:])

    coreid=core.reshape(1).astype(jnp.int32)
    pre_r=rel(pre_mix,1)
    post_r=rel(post_mix,0)
    pre_s=pre_r*0.125
    pre_rep=jnp.repeat(pre_s,HD,axis=1).reshape(HEADS,1,INNER)
    post_rep=jnp.repeat(post_r.T,HD,axis=1).reshape(HEADS,1,INNER)
    segc=segment_ids.reshape(SEQ,1)
    sb=segment_ids.reshape(4,1,BLK)
    segr=cols(jnp.where(first,sb[0],sb[2]),jnp.where(first,sb[3],sb[1]))

    qT=low(dg(wq,act_own,0,1))
    k=low(dg(act_nat,wk,1,0))
    pT=k1(coreid,pre_s*LOG2E,segc,segr,k,qT)
    vT=low(dg(wv,act_nat,0,1))
    uT,hT=k2(coreid,post_r,vT,pT)

    middle=x_own+dg(hT,woT,0,1)
    normed2,inv2=rms_forward(middle)
    act2=low(normed2*norm2_gain)
    grp=cat(act2,swap(act2))
    pre_act=dg(grp,win,1,0)
    hidden=low(gelu(pre_act))
    grad_woutT=scatter_rows(low(dg(cot_grp,hidden,0,0)))
    out_part=dg(hidden,woutT,1,1)
    out_own=low(middle+out_part[:HALF]+swap(low(out_part[HALF:])).astype(F32))
    output=cat(out_own[:BLK],swap(out_own[BLK:]))
    grad_hidden=low(dg(cot_grp,woutT,1,0))
    grad_pre=low(jax.vjp(gelu,pre_act)[1](grad_hidden.astype(F32))[0])
    grad_win=scatter_rows(low(dg(grp,grad_pre,0,0)))
    ga2=dg(grad_pre,win,1,1)
    ga2=ga2[:HALF]+swap(low(ga2[HALF:])).astype(F32)
    back2,gain2=rms_backward(ga2,normed2,inv2,norm2_gain)
    grad_middle=cot_own.astype(F32)+back2
    grad_attn=low(grad_middle)
    gm_loc=cat(grad_middle[:BLK],swap(grad_middle[BLK:]))

    ghT=low(dg(woT,grad_attn,0,1))
    gh=low(dg(grad_attn,woT,1,0))
    g_woT=low(dg(grad_attn,hT,0,1))
    v=low(dg(act_nat,wv,1,0))
    gL,gV,gpost=b1(coreid,post_r,post_rep,v,ghT,gh,pT,uT)
    g_wv=low(dg(act_nat,gV,0,0))
    mine=lambda g: low(g[:,:HI].astype(F32)+swap(g[:,HI:]).astype(F32))
    grad_vo=scatter_rows(cols(mine(g_wv),mine(g_woT)))
    kT=low(dg(wk,act_nat,0,1))
    q=low(dg(act_own,wq,1,0))
    gQT,gK,gpre=b2(coreid,pre_s,pre_rep,kT,qT,q,gL)
    g_wq=low(dg(act_own,gQT,0,1))
    g_wk=low(dg(act_nat,gK,0,0))
    grad_qk=scatter_rows(cols(mine(g_wq),mine(g_wk)))

    ga_kv=dg(gK,wk,1,1)+dg(gV,wv,1,1)
    ga_q=dg(gQT,wq,0,1)
    ga_loc=lax.dynamic_slice_in_dim(ga_kv,core*HALF,HALF,0)
    ga_oth=lax.dynamic_slice_in_dim(ga_kv,(1-core)*HALF,HALF,0)
    sent=low(cat(ga_oth[:BLK],ga_oth[BLK:]+ga_q[BLK:]))
    ga1=cat(ga_loc[:BLK]+ga_q[:BLK],ga_loc[BLK:])+swap(sent).astype(F32)
    back1,gain1=rms_backward(ga1,normed_loc,inv_loc,norm1_gain)
    grad_tokens=low(gm_loc+back1)

    gpost_m=rel(jnp.sum(gpost,axis=-1).T,0)
    gpre_m=rel(jnp.sum(gpre,axis=-1)*0.125,1)
    small=cat(gain1,gain2,gpre_m.reshape(-1),gpost_m.reshape(-1),jnp.zeros((96,),F32)).reshape(15,128)
    small=sum_all(small).reshape(-1)
    D=norm1_gain.shape[0]
    m=HEADS*HEADS
    return (output,grad_tokens,small[:D],grad_qk[:,:HI],grad_qk[:,HI:],grad_vo[:,:HI],
            small[2*D:2*D+m].reshape(HEADS,HEADS),small[2*D+m:2*D+2*m].reshape(HEADS,HEADS),
            grad_vo[:,HI:].T,small[D:2*D],grad_win,grad_woutT.T)


def solution(mesh):
    rows=P(("dp","tensor"),None)
    w=P("dp","tensor")
    wt=P("tensor","dp")
    return jax.shard_map(on_device,mesh=mesh,
        in_specs=(rows,rows,P("dp"),P(),w,w,w,P(),P(),wt,P(),w,wt),
        out_specs=(rows,rows,P(),w,w,w,P(),P(),wt,P(),w,wt),
        check_vma=False)
```

```python
import jax
import jax.numpy as jnp
from jax import lax
from jax.experimental import pallas as pl
from jax.experimental.pallas import tpu as pltpu
from jax.sharding import PartitionSpec as P

HEADS = 12
HD = 64
INNER = 768
HI = INNER // 2
SEQ = 1024
HALF = SEQ // 2
BLK = 256
EPSILON = 1e-06
LOG2E = 1.4426950408889634
BF = jnp.bfloat16
F32 = jnp.float32
HB1, HB2, HB3, HB4 = 3, 3, 2, 3
FT = 512


def dot(a, b):
    return jnp.dot(a, b, preferred_element_type=F32)


def dot_nt(a, b):
    return lax.dot_general(a, b, (((1,), (1,)), ((), ())), preferred_element_type=F32)


def smem():
    return pl.BlockSpec(memory_space=pltpu.SMEM)


def whole():
    return pl.BlockSpec(memory_space=pltpu.VMEM)


def full(s):
    return pl.BlockSpec(s, lambda *i: (0,) * len(s))


def params():
    return pltpu.CompilerParams(vmem_limit_bytes=56 * 1024 * 1024)


def cost(flops, moved, exps=0):
    return pl.CostEstimate(flops=int(flops), bytes_accessed=int(moved), transcendentals=int(exps))


def sds(shape, dtype=BF):
    return jax.ShapeDtypeStruct(shape, dtype)


def once(body, outs, args, name, scalars=1, scratch=(), flops=0):
    moved = sum(a.size * a.dtype.itemsize for a in args) + sum(
        o.size * o.dtype.itemsize for o in outs
    )
    return pl.pallas_call(
        body,
        in_specs=[smem()] * scalars + [whole()] * (len(args) - scalars),
        out_specs=[whole()] * len(outs),
        out_shape=list(outs),
        scratch_shapes=list(scratch),
        compiler_params=params(),
        cost_estimate=cost(flops, moved),
        name=name,
    )(*args)


def per_core(ids_ref, run):
    for c in range(2):
        pl.when(ids_ref[0] == c)(lambda c=c: run(c))


def chunks(c):
    return (1, 4) if c == 0 else (3, 2)


def blocks_of(c):
    return (0, 3) if c == 0 else (2, 1)


def logits_body(ids_ref, pre_ref, segc_ref, segr_ref, k_ref, qT_ref, pT_ref, mask_ref):
    step = pl.program_id(0)

    def run(c):
        nj, bl = chunks(c), blocks_of(c)
        base = (0, nj[0] * BLK)

        @pl.when(step == 0)
        def _():
            for b in range(2):
                qpos = lax.broadcasted_iota(jnp.int32, (BLK, BLK), 1) + bl[b] * BLK
                qseg = segr_ref[:, b * BLK : (b + 1) * BLK]
                for j in range(nj[b]):
                    kpos = lax.broadcasted_iota(jnp.int32, (BLK, BLK), 0) + j * BLK
                    kseg = segc_ref[j * BLK : (j + 1) * BLK, :]
                    ok = (kpos <= qpos) & (kseg == qseg)
                    at = base[b] + j * BLK
                    mask_ref[at : at + BLK, :] = jnp.where(ok, 0.0, -1e30)

        for hh in range(HB1):
            h = step * HB1 + hh
            for b in range(2):
                n = nj[b] * BLK
                qs = jnp.concatenate(
                    [
                        (
                            qT_ref[g * HD : (g + 1) * HD, b * BLK : (b + 1) * BLK].astype(F32)
                            * pre_ref[h, g]
                        ).astype(BF)
                        for g in range(HEADS)
                    ],
                    axis=0,
                )
                s = dot(k_ref[:n, :], qs) + mask_ref[base[b] : base[b] + n, :]
                m = jnp.max(s, axis=0, keepdims=True)
                e = jnp.exp2(s - m)
                inv = 1.0 / jnp.sum(e, axis=0, keepdims=True)
                pT_ref[base[b] : base[b] + n, hh * BLK : (hh + 1) * BLK] = (e * inv).astype(BF)

    per_core(ids_ref, run)


def logits_softmax(ids, pre, segc, segr, k, qT):
    return pl.pallas_call(
        logits_body,
        grid=(HEADS // HB1,),
        in_specs=[smem(), smem(), full((SEQ, 1)), full((1, HALF)), full((SEQ, INNER)), full((INNER, HALF))],
        out_specs=pl.BlockSpec((5 * BLK, HB1 * BLK), lambda h: (0, h)),
        out_shape=sds((5 * BLK, HEADS * BLK)),
        scratch_shapes=[pltpu.VMEM((5 * BLK, BLK), F32)],
        compiler_params=params(),
        cost_estimate=cost(6.04e9, 10e6, 4e6),
        name="logits_softmax",
    )(ids, pre, segc, segr, k, qT)


def attend_body(ids_ref, post_ref, vT_ref, pT_ref, uT_ref, h_ref, acc_ref):
    step = pl.program_id(0)

    def run(c):
        nj = chunks(c)
        base = (0, nj[0] * BLK)
        for b in range(2):
            n = nj[b] * BLK
            cs = slice(b * BLK, (b + 1) * BLK)
            us = []
            for hh in range(HB2):
                u = dot(vT_ref[:, :n], pT_ref[base[b] : base[b] + n, hh * BLK : (hh + 1) * BLK])
                uT_ref[hh * INNER : (hh + 1) * INNER, cs] = u.astype(BF)
                us.append(u)
            for k in range(HEADS):
                rs = slice(k * HD, (k + 1) * HD)
                t = us[0][rs, :] * post_ref[k, step * HB2]
                for hh in range(1, HB2):
                    t = t + us[hh][rs, :] * post_ref[k, step * HB2 + hh]
                acc_ref[rs, cs] += t

    @pl.when(step == 0)
    def _():
        acc_ref[...] = jnp.zeros_like(acc_ref)

    per_core(ids_ref, run)

    @pl.when(step == HEADS // HB2 - 1)
    def _():
        h_ref[...] = acc_ref[...].T.astype(BF)


def attend(ids, post, vT, pT):
    return pl.pallas_call(
        attend_body,
        grid=(HEADS // HB2,),
        in_specs=[smem(), smem(), full((INNER, SEQ)), pl.BlockSpec((5 * BLK, HB2 * BLK), lambda h: (0, h))],
        out_specs=[pl.BlockSpec((HB2 * INNER, HALF), lambda h: (h, 0)), full((HALF, INNER))],
        out_shape=[sds((HEADS * INNER, HALF)), sds((HALF, INNER))],
        scratch_shapes=[pltpu.VMEM((INNER, HALF), F32)],
        compiler_params=params(),
        cost_estimate=cost(6.04e9, 20e6),
        name="attend",
    )(ids, post, vT, pT)


def split_rows(c, acc_ref, own_ref, oth_ref):
    for d in range(2):
        src = slice((c ^ d) * HALF, (c ^ d) * HALF + HALF)
        dst = slice(d * HALF, (d + 1) * HALF)
        own_ref[dst, :] = acc_ref[src, :HI].astype(BF)
        oth_ref[dst, :] = acc_ref[src, HI:].astype(BF)


def attend_back_body(
    ids_ref, post_ref, rep_ref, v_ref, ghT_ref, gh_ref, pT_ref, uT_ref,
    gL_ref, own_ref, oth_ref, gpost_ref, acc_ref,
):
    step = pl.program_id(0)

    def run(c):
        nj = chunks(c)
        base = (0, nj[0] * BLK)
        for b in range(2):
            n = nj[b] * BLK
            cs = slice(b * BLK, (b + 1) * BLK)
            g2s = []
            for hh in range(HB3):
                h = step * HB3 + hh
                hs = slice(hh * BLK, (hh + 1) * BLK)
                r = jnp.zeros((1, BLK), F32)
                parts = []
                for k in range(HEADS):
                    gk = ghT_ref[k * HD : (k + 1) * HD, cs].astype(F32)
                    u = uT_ref[hh * INNER + k * HD : hh * INNER + (k + 1) * HD, cs].astype(F32)
                    g = jnp.sum(gk * u, axis=0, keepdims=True)
                    w = post_ref[k, h]
                    gpost_ref[hh, k : k + 1, cs] = g
                    r = r + g * w
                    parts.append((gk * w).astype(BF))
                gP = dot(v_ref[:n, :], jnp.concatenate(parts, axis=0))
                p = pT_ref[base[b] : base[b] + n, hs]
                gL_ref[base[b] : base[b] + n, hs] = (p.astype(F32) * (gP - r)).astype(BF)
                g2s.append((gh_ref[cs, :].astype(F32) * rep_ref[hh]).astype(BF))
            acc_ref[:n, :] += dot(pT_ref[base[b] : base[b] + n, :], jnp.concatenate(g2s, axis=0))

        @pl.when(step == HEADS // HB3 - 1)
        def _():
            split_rows(c, acc_ref, own_ref, oth_ref)

    @pl.when(step == 0)
    def _():
        acc_ref[...] = jnp.zeros_like(acc_ref)

    per_core(ids_ref, run)


def attend_back(ids, post, post_rep, v, ghT, gh, pT, uT):
    return pl.pallas_call(
        attend_back_body,
        grid=(HEADS // HB3,),
        in_specs=[
            smem(), smem(), pl.BlockSpec((HB3, 1, INNER), lambda h: (h, 0, 0)),
            full((SEQ, INNER)), full((INNER, HALF)), full((HALF, INNER)),
            pl.BlockSpec((5 * BLK, HB3 * BLK), lambda h: (0, h)),
            pl.BlockSpec((HB3 * INNER, HALF), lambda h: (h, 0)),
        ],
        out_specs=[
            pl.BlockSpec((5 * BLK, HB3 * BLK), lambda h: (0, h)),
            full((SEQ, HI)), full((SEQ, HI)),
            pl.BlockSpec((HB3, HEADS, HALF), lambda h: (h, 0, 0)),
        ],
        out_shape=[
            sds((5 * BLK, HEADS * BLK)), sds((SEQ, HI)), sds((SEQ, HI)),
            sds((HEADS, HEADS, HALF), F32),
        ],
        scratch_shapes=[pltpu.VMEM((SEQ, INNER), F32)],
        compiler_params=params(),
        cost_estimate=cost(12.1e9, 30e6),
        name="attend_back",
    )(ids, post, post_rep, v, ghT, gh, pT, uT)


def scores_back_body(
    ids_ref, pre_ref, rep_ref, kT_ref, qT_ref, q_ref, gL_ref,
    gqa_ref, gqb_ref, own_ref, oth_ref, gpre_ref, accq_ref, acck_ref,
):
    step = pl.program_id(0)

    def run(c):
        nj = chunks(c)
        base = (0, nj[0] * BLK)
        for b in range(2):
            n = nj[b] * BLK
            cs = slice(b * BLK, (b + 1) * BLK)
            ws, q2s = [], []
            for hh in range(HB4):
                ws.append(dot(kT_ref[:, :n], gL_ref[base[b] : base[b] + n, hh * BLK : (hh + 1) * BLK]))
                q2s.append((q_ref[cs, :].astype(F32) * rep_ref[hh]).astype(BF))
            for k in range(HEADS):
                rs = slice(k * HD, (k + 1) * HD)
                qk = qT_ref[rs, cs].astype(F32)
                t = None
                for hh in range(HB4):
                    w = ws[hh][rs, :]
                    gpre_ref[hh, k : k + 1, cs] = jnp.sum(qk * w, axis=0, keepdims=True)
                    u = w * pre_ref[step * HB4 + hh, k]
                    t = u if t is None else t + u
                accq_ref[rs, cs] += t
            acck_ref[:n, :] += dot(gL_ref[base[b] : base[b] + n, :], jnp.concatenate(q2s, axis=0))

        @pl.when(step == HEADS // HB4 - 1)
        def _():
            split_rows(c, acck_ref, own_ref, oth_ref)

    @pl.when(step == 0)
    def _():
        accq_ref[...] = jnp.zeros_like(accq_ref)
        acck_ref[...] = jnp.zeros_like(acck_ref)

    per_core(ids_ref, run)

    @pl.when(step == HEADS // HB4 - 1)
    def _():
        gqa_ref[...] = accq_ref[:HI, :].T.astype(BF)
        gqb_ref[...] = accq_ref[HI:, :].T.astype(BF)


def scores_back(ids, pre, pre_rep, kT, qT, q, gL):
    return pl.pallas_call(
        scores_back_body,
        grid=(HEADS // HB4,),
        in_specs=[
            smem(), smem(), pl.BlockSpec((HB4, 1, INNER), lambda h: (h, 0, 0)),
            full((INNER, SEQ)), full((INNER, HALF)), full((HALF, INNER)),
            pl.BlockSpec((5 * BLK, HB4 * BLK), lambda h: (0, h)),
        ],
        out_specs=[
            full((HALF, HI)), full((HALF, HI)), full((SEQ, HI)), full((SEQ, HI)),
            pl.BlockSpec((HB4, HEADS, HALF), lambda h: (h, 0, 0)),
        ],
        out_shape=[
            sds((HALF, HI)), sds((HALF, HI)), sds((SEQ, HI)), sds((SEQ, HI)),
            sds((HEADS, HEADS, HALF), F32),
        ],
        scratch_shapes=[pltpu.VMEM((INNER, HALF), F32), pltpu.VMEM((SEQ, INNER), F32)],
        compiler_params=params(),
        cost_estimate=cost(12.1e9, 14e6),
        name="scores_back",
    )(ids, pre, pre_rep, kT, qT, q, gL)


def own_rows(loc, oth):
    return jnp.concatenate([loc[:BLK], oth[BLK:]], axis=0)


def project_body(with_q, ids_ref, loc_ref, oth_ref, *refs):
    if with_q:
        qa, qb, wa, wb, q_ref, qT_ref, k_ref, kT_ref = refs
        own = own_rows(loc_ref[...], oth_ref[...])
        for i, w in enumerate((qa, qb)):
            t = dot(own, w[...])
            cs = slice(i * HI, (i + 1) * HI)
            q_ref[:, cs] = t.astype(BF)
            qT_ref[cs, :] = t.T.astype(BF)
    else:
        wa, wb, k_ref, kT_ref = refs

    def run(c):
        for d, rows in enumerate((loc_ref, oth_ref)):
            rs = slice((c ^ d) * HALF, (c ^ d) * HALF + HALF)
            for i, w in enumerate((wa, wb)):
                t = dot(rows[...], w[...])
                cs = slice(i * HI, (i + 1) * HI)
                k_ref[rs, cs] = t.astype(BF)
                kT_ref[cs, rs] = t.T.astype(BF)

    per_core(ids_ref, run)


def project_qk(ids, loc, oth, qa, qb, ka, kb):
    outs = (sds((HALF, INNER)), sds((INNER, HALF)), sds((SEQ, INNER)), sds((INNER, SEQ)))
    body = lambda *r: project_body(True, *r)
    return once(body, outs, (ids, loc, oth, qa, qb, ka, kb), "project_qk", flops=1.8e9)


def project_v(ids, loc, oth, va, vb):
    outs = (sds((SEQ, INNER)), sds((INNER, SEQ)))
    body = lambda *r: project_body(False, *r)
    return once(body, outs, (ids, loc, oth, va, vb), "project_v", flops=1.2e9)


def norm(v):
    inv = lax.rsqrt(jnp.mean(v * v, axis=-1, keepdims=True) + EPSILON)
    return v * inv, inv


def middle_body(x_ref, h_ref, wa_ref, wb_ref, gain_ref, mid_ref, act_ref, actT_ref):
    mid = x_ref[...].astype(F32) + dot_nt(h_ref[:, :HI], wa_ref[...]) + dot_nt(h_ref[:, HI:], wb_ref[...])
    act = norm(mid)[0] * gain_ref[...]
    mid_ref[...] = mid
    act_ref[...] = act.astype(BF)
    actT_ref[...] = act.T.astype(BF)


def emit(me, scr_ref, cols, keep_ref, send_ref, outer_x):
    for e in range(16):
        x, y, z = e & 1, (e >> 1) & 1, e >> 2
        if me is None:
            ref, at, row = (keep_ref, send_ref)[e >> 3], e & 7, e * 48
        else:
            first, second = (x, y) if outer_x else (y, x)
            ref, at = (keep_ref, send_ref)[first], second * 4 + z
            row = pl.multiple_of(lax.bitwise_xor(me, e) * 48, 16)
        ref[at, :, cols] = scr_ref[pl.ds(row, 48), cols].astype(BF)


def ffn_body(
    xor, ids_ref, aown_ref, aoth_ref, aTown_ref, aToth_ref, cown_ref, coth_ref, cT_ref,
    win_ref, wout_ref, outa_ref, outb_ref, gaa_ref, gab_ref, ka_ref, sa_ref, kb_ref, sb_ref,
    acco_ref, accg_ref, scr_ref,
):
    step = pl.program_id(0)
    last = pl.num_programs(0) - 1
    me = ids_ref[1] if xor else None

    @pl.when(step == 0)
    def _():
        acco_ref[...] = jnp.zeros_like(acco_ref)
        accg_ref[...] = jnp.zeros_like(accg_ref)

    win, wout = win_ref[...], wout_ref[...]
    hid, gpre = [], []
    for a_ref, c_ref, rs in ((aown_ref, cown_ref, slice(0, HALF)), (aoth_ref, coth_ref, slice(HALF, SEQ))):
        v = dot(a_ref[...], win)
        sq = v * v
        t = jnp.tanh(0.7978845608028654 * v * (1.0 + 0.044715 * sq))
        hidden = (0.5 * v * (1.0 + t)).astype(BF)
        slope = 0.5 * (1.0 + t) + 0.5 * v * (1.0 - t * t) * (
            0.7978845608028654 * (1.0 + 0.134145 * sq)
        )
        gh = dot(c_ref[...], wout).astype(BF).astype(F32)
        gp = (gh * slope).astype(BF)
        acco_ref[rs, :] += dot_nt(hidden, wout)
        accg_ref[rs, :] += dot_nt(gp, win)
        hid.append(hidden)
        gpre.append(gp)
    scr_ref[...] = dot(cT_ref[:, :HALF], hid[0]) + dot(cT_ref[:, HALF:], hid[1])
    emit(me, scr_ref, slice(0, FT), ka_ref, sa_ref, True)
    scr_ref[...] = dot(aTown_ref[...], gpre[0]) + dot(aToth_ref[...], gpre[1])
    emit(me, scr_ref, slice(0, FT), kb_ref, sb_ref, False)

    @pl.when(step == last)
    def _():
        outa_ref[...] = acco_ref[:HALF, :]
        outb_ref[...] = acco_ref[HALF:, :].astype(BF)
        gaa_ref[...] = accg_ref[:HALF, :]
        gab_ref[...] = accg_ref[HALF:, :].astype(BF)


def ffn(xor, ids, aown, aoth, aTown, aToth, cown, coth, cT, win, woutT):
    width = win.shape[1]
    tile = pl.BlockSpec((INNER, FT), lambda t: (0, t))
    grad = pl.BlockSpec((8, 48, FT), lambda t: (0, 0, t))
    half, halfT = full((HALF, INNER)), full((INNER, HALF))
    return pl.pallas_call(
        lambda *r: ffn_body(xor, *r),
        grid=(width // FT,),
        in_specs=[smem(), half, half, halfT, halfT, half, half, full((INNER, SEQ)), tile, tile],
        out_specs=[half, half, half, half, grad, grad, grad, grad],
        out_shape=[
            sds((HALF, INNER), F32), sds((HALF, INNER)), sds((HALF, INNER), F32), sds((HALF, INNER)),
        ] + [sds((8, 48, width))] * 4,
        scratch_shapes=[
            pltpu.VMEM((SEQ, INNER), F32), pltpu.VMEM((SEQ, INNER), F32), pltpu.VMEM((INNER, FT), F32),
        ],
        compiler_params=params(),
        cost_estimate=cost(14.5e9, 20e6, 1.6e6),
        name="ffn",
    )(ids, aown, aoth, aTown, aToth, cown, coth, cT, win, woutT)


def middle_back_body(
    ga_ref, gr_ref, mid_ref, cot_ref, gain_ref, h_ref, wa_ref, wb_ref,
    stay_ref, sent_ref, gh_ref, ghT_ref, gain_out, gwa_ref, gwb_ref,
):
    ga = ga_ref[...] + gr_ref[...].astype(F32)
    normed, inv = norm(mid_ref[...])
    scaled = ga * gain_ref[...]
    gm = cot_ref[...].astype(F32) + inv * (
        scaled - normed * jnp.mean(scaled * normed, axis=-1, keepdims=True)
    )
    gain_out[...] = jnp.sum(ga * normed, axis=0, keepdims=True)
    stay_ref[...] = gm[:BLK]
    sent_ref[...] = gm[BLK:]
    grad = gm.astype(BF)
    gT = gm.T.astype(BF)
    for i, (w, gw) in enumerate(((wa_ref, gwa_ref), (wb_ref, gwb_ref))):
        cs = slice(i * HI, (i + 1) * HI)
        t = dot(grad, w[...])
        gh_ref[:, cs] = t.astype(BF)
        ghT_ref[cs, :] = t.T.astype(BF)
        gw[...] = dot(gT, h_ref[:, cs]).astype(BF)


def joined(own, got):
    a, b = own.astype(F32), got.astype(F32)
    return jnp.concatenate([a[:HALF] + b[HALF:], a[HALF:] + b[:HALF]], axis=0).astype(BF)


def grad_vo_body(xor, ids_ref, aT_ref, gv_ref, rv_ref, go_ref, ro_ref, gv_out, ka, sa, kb, sb, scr):
    me = ids_ref[1] if xor else None
    gv = joined(gv_ref[...], rv_ref[...])
    gv_out[...] = gv
    scr[...] = dot(aT_ref[...], gv)
    emit(me, scr, slice(0, HI), ka, sa, True)
    scr[...] = go_ref[...].astype(F32) + ro_ref[...].astype(F32)
    emit(me, scr, slice(0, HI), kb, sb, False)


def grad_qk_body(xor, ids_ref, aT_ref, gq_ref, rq_ref, gk_ref, rk_ref, gq_out, gk_out, ka, sa, kb, sb, scr):
    me = ids_ref[1] if xor else None
    gq, rq = gq_ref[...], rq_ref[...]
    gq = jnp.concatenate([gq[:BLK], rq[BLK:], rq[:BLK], gq[BLK:]], axis=0)
    gq_out[...] = gq
    scr[...] = dot(aT_ref[...], gq)
    emit(me, scr, slice(0, HI), ka, sa, True)
    gk = joined(gk_ref[...], rk_ref[...])
    gk_out[...] = gk
    scr[...] = dot(aT_ref[...], gk)
    emit(me, scr, slice(0, HI), kb, sb, False)


def act_back_body(gq_ref, gk_ref, gv_ref, wq_ref, wk_ref, wv_ref, loc_ref, oth_ref):
    for rs, ref in ((slice(0, HALF), loc_ref), (slice(HALF, SEQ), oth_ref)):
        t = dot_nt(gq_ref[rs, :], wq_ref[...]) + dot_nt(gk_ref[rs, :], wk_ref[...])
        ref[...] = (t + dot_nt(gv_ref[rs, :], wv_ref[...])).astype(ref.dtype)


def tokens_back_body(ga_ref, gr_ref, x_ref, gain_ref, stay_ref, got_ref, out_ref, gain_out):
    ga = ga_ref[...] + gr_ref[...].astype(F32)
    normed, inv = norm(x_ref[...].astype(F32))
    scaled = ga * gain_ref[...]
    back = inv * (scaled - normed * jnp.mean(scaled * normed, axis=-1, keepdims=True))
    gain_out[...] = jnp.sum(ga * normed, axis=0, keepdims=True)
    out_ref[:BLK, :] = (stay_ref[...] + back[:BLK]).astype(BF)
    out_ref[BLK:, :] = (got_ref[...] + back[BLK:]).astype(BF)


def swap(v):
    return lax.ppermute(v, "tensor", [(0, 1), (1, 0)])


def hop(v, mask):
    n = lax.axis_size("dp")
    return lax.ppermute(v, "dp", [(i, i ^ mask) for i in range(n)])


def after(v, *done):
    return lax.optimization_barrier((v, *done))[0]


def place_body(ids_ref, *refs):
    ins, outs = refs[:4], refs[4:]
    me = ids_ref[1]
    for t, ref in enumerate(ins):
        for i in range(2):
            for j in range(4):
                e = 4 * j + ((2 * i + t) if t < 2 else (i + 2 * (t - 2)))
                row = pl.multiple_of(lax.bitwise_xor(me, e) * 48, 16)
                outs[t // 2][pl.ds(row, 48), :] = ref[i, j]


def gather_pair(ids, a, b, wait=(), wait2=()):
    if lax.axis_size("dp") != 16:
        return (
            lax.all_gather(a, "dp", axis=0, tiled=True),
            lax.all_gather(b, "dp", axis=0, tiled=True),
            (), (),
        )
    ca = a.shape[1]
    shard = after(jnp.concatenate([a, b], axis=1), *wait)
    got = [hop(shard, 4 * e) for e in range(1, 4)]
    z = jnp.stack([shard] + got, axis=0)
    az, bz = z[:, :, :ca], z[:, :, ca:]
    if wait2:
        az, bz = lax.optimization_barrier((az, bz, *wait2))[:2]
    a2 = jnp.stack([az, hop(az, 2)], axis=0)
    b2 = jnp.stack([bz, hop(bz, 1)], axis=0)
    ax, by = hop(a2, 1), hop(b2, 2)
    wa, wb = once(
        place_body, (sds((768, ca)), sds((768, b.shape[1]))), (ids, a2, ax, b2, by), "place"
    )
    return wa, wb, (got[2],), (ax, by)


def fold_one_body(ka, ra, kb, rb, oka, osa, okb, osb):
    for k, r, keep, send in ((ka, ra, oka, osa), (kb, rb, okb, osb)):
        t = (k[...].astype(F32) + r[...].astype(F32)).astype(BF)
        keep[...] = t[:4]
        send[...] = t[4:]


def fold_two_body(ka, ra, kb, rb, own, *sends):
    w = ka.shape[2]
    for k, r, cs in ((ka, ra, slice(0, w)), (kb, rb, slice(w, 2 * w))):
        t = k[...].astype(F32) + r[...].astype(F32)
        own[:, cs] = t[0]
        for e in range(3):
            sends[e][:, cs] = t[e + 1].astype(BF)


def scatter_pair(ka, sa, kb, sb):
    w = ka.shape[2]
    if lax.axis_size("dp") != 16:
        flat = jnp.concatenate(
            [jnp.concatenate([k, s], axis=0).reshape(768, w) for k, s in ((ka, sa), (kb, sb))], axis=1
        )
        return lax.psum_scatter(flat.astype(F32), "dp", scatter_dimension=0, tiled=True)
    piece = sds((4, 48, w))
    ka, sa, kb, sb = once(
        fold_one_body, (piece,) * 4, (ka, hop(sa, 1), kb, hop(sb, 2)), "fold_one", scalars=0
    )
    own, *sends = once(
        fold_two_body, (sds((48, 2 * w), F32),) + (sds((48, 2 * w)),) * 3,
        (ka, hop(sa, 2), kb, hop(sb, 1)), "fold_two", scalars=0,
    )
    for e in range(3):
        own = own + hop(sends[e], 4 * (e + 1)).astype(F32)
    return own


def sum_all(v):
    n = lax.axis_size("dp")
    v = v + swap(v)
    v = v + (hop(v, 1) + hop(v, 2) + hop(v, 3))
    if n == 16:
        return v + (hop(v, 4) + hop(v, 8) + hop(v, 12))
    bit = 4
    while bit < n:
        v = v + hop(v, bit)
        bit *= 2
    return v


def on_device(
    tokens, cotangent, segment_ids, norm1_gain, w_query, w_key, w_value, pre_mix, post_mix,
    w_output, norm2_gain, w_in, w_out,
):
    core = lax.axis_index("tensor")
    ids = jnp.stack([core, lax.axis_index("dp")]).astype(jnp.int32)
    first = core == 0
    xor = lax.axis_size("dp") == 16
    cat = lambda *a: jnp.concatenate(a, axis=0)
    low = lambda v: v.astype(BF)
    rel = lambda m, axis: jnp.where(first, m, jnp.roll(m, HEADS // 2, axis=axis))
    D = norm1_gain.shape[0]

    wq, wk, z1, xy1 = gather_pair(ids, low(w_query), low(w_key))
    wv, woT, z2, xy2 = gather_pair(ids, low(w_value), low(w_output.T), z1, xy1)
    win, woutT, _, _ = gather_pair(ids, low(w_in), low(w_out.T), z2, xy2)
    wq_o, wk_o, wv_o, woT_o = swap(wq), swap(wk), swap(wv), swap(woT)

    x_oth, cot_oth = swap(tokens), swap(cotangent)
    gain1, gain2 = norm1_gain.reshape(1, D), norm2_gain.reshape(1, D)
    act_loc = low(norm(tokens.astype(F32))[0] * gain1)
    act_oth = low(norm(x_oth.astype(F32))[0] * gain1)
    actT = cat(act_loc, act_oth).T
    x_own = own_rows(tokens, x_oth)
    cot_own, cot_rest = own_rows(cotangent, cot_oth), own_rows(cot_oth, cotangent)
    cotT = cat(cot_own, cot_rest).T

    pre_r, post_r = rel(pre_mix, 1), rel(post_mix, 0)
    pre_s = pre_r * 0.125
    pre_rep = jnp.repeat(pre_s, HD, axis=1).reshape(HEADS, 1, INNER)
    post_rep = jnp.repeat(post_r.T, HD, axis=1).reshape(HEADS, 1, INNER)
    segc = segment_ids.reshape(SEQ, 1)
    sb = segment_ids.reshape(4, 1, BLK)
    segr = jnp.concatenate([jnp.where(first, sb[0], sb[2]), jnp.where(first, sb[3], sb[1])], axis=1)

    q, qT, k, kT = project_qk(ids, act_loc, act_oth, wq, wq_o, wk, wk_o)
    pT = logits_softmax(ids, pre_s * LOG2E, segc, segr, k, qT)
    v, vT = project_v(ids, act_loc, act_oth, wv, wv_o)
    uT, heads = attend(ids, post_r, vT, pT)
    mid, act2, act2T = once(
        middle_body, (sds((HALF, D), F32), sds((HALF, D)), sds((D, HALF))),
        (x_own, heads, woT, woT_o, gain2), "middle", scalars=0, flops=6e8,
    )
    out_own, out_oth, ga_own, ga_oth, ka, sa, kb, sb_ = ffn(
        xor, ids, act2, swap(act2), act2T, swap(act2T), cot_own, cot_rest, cotT, win, woutT
    )
    grad_ffn = scatter_pair(ka, sa, kb, sb_)
    out = low(mid + out_own + swap(out_oth).astype(F32))
    output = cat(out[:BLK], swap(out[BLK:]))

    stay, sent, gh, ghT, gain2_part, gwo, gwo_o = once(
        middle_back_body,
        (
            sds((BLK, D), F32), sds((BLK, D), F32), sds((HALF, INNER)), sds((INNER, HALF)),
            sds((1, D), F32), sds((D, HI)), sds((D, HI)),
        ),
        (ga_own, swap(ga_oth), mid, cot_own, gain2, heads, woT, woT_o),
        "middle_back", scalars=0, flops=1.2e9,
    )
    gL, gv, gv_o, gpost = attend_back(ids, post_r, post_rep, v, ghT, gh, pT, uT)
    grads = (sds((8, 48, HI)),) * 4
    gv, *vo = once(
        lambda *r: grad_vo_body(xor, *r), (sds((SEQ, HI)),) + grads,
        (ids, actT, gv, swap(gv_o), gwo, swap(gwo_o)), "grad_vo",
        scratch=[pltpu.VMEM((D, HI), F32)], flops=6e8,
    )
    grad_vo = scatter_pair(*vo)
    gq, gq_o, gk, gk_o, gpre = scores_back(ids, pre_s, pre_rep, kT, qT, q, gL)
    gq, gk, *qk = once(
        lambda *r: grad_qk_body(xor, *r), (sds((SEQ, HI)),) * 2 + grads,
        (ids, actT, gq, swap(gq_o), gk, swap(gk_o)), "grad_qk",
        scratch=[pltpu.VMEM((D, HI), F32)], flops=1.2e9,
    )
    grad_qk = scatter_pair(*qk)
    ga_loc, ga_oth = once(
        act_back_body, (sds((HALF, D), F32), sds((HALF, D))), (gq, gk, gv, wq, wk, wv),
        "act_back", scalars=0, flops=1.8e9,
    )
    grad_tokens, gain1_part = once(
        tokens_back_body, (sds((HALF, D)), sds((1, D), F32)),
        (ga_loc, swap(ga_oth), tokens, gain1, stay, swap(sent)), "tokens_back", scalars=0,
    )

    gpost_m = rel(jnp.sum(gpost, axis=-1).T, 0)
    gpre_m = rel(jnp.sum(gpre, axis=-1) * 0.125, 1)
    m = HEADS * HEADS
    small = cat(
        gain1_part.reshape(-1), gain2_part.reshape(-1), gpre_m.reshape(-1), gpost_m.reshape(-1),
        jnp.zeros((15 * 128 - 2 * D - 2 * m,), F32),
    ).reshape(15, 128)
    small = sum_all(small).reshape(-1)
    ff = w_in.shape[1]
    return (
        output, grad_tokens, small[:D], grad_qk[:, :HI], grad_qk[:, HI:], grad_vo[:, :HI],
        small[2 * D : 2 * D + m].reshape(HEADS, HEADS),
        small[2 * D + m : 2 * D + 2 * m].reshape(HEADS, HEADS),
        grad_vo[:, HI:].T, small[D : 2 * D], grad_ffn[:, ff:], grad_ffn[:, :ff].T,
    )


def solution(mesh):
    rows = P(("dp", "tensor"), None)
    w, wt = P("dp", "tensor"), P("tensor", "dp")
    return jax.shard_map(
        on_device,
        mesh=mesh,
        in_specs=(rows, rows, P("dp"), P(), w, w, w, P(), P(), wt, P(), w, wt),
        out_specs=(rows, rows, P(), w, w, w, P(), P(), wt, P(), w, wt),
        check_vma=False,
    )
```

```python
import math

import jax
import jax.numpy as jnp
from jax import lax
from jax.experimental import pallas as pl
from jax.experimental.pallas import tpu as pltpu
from jax.sharding import PartitionSpec as P

HEADS = 12
HD = 64
INNER = 768
HI = INNER // 2
SEQ = 1024
HALF = SEQ // 2
BLK = 256
EPSILON = 1e-06
LOG2E = 1.4426950408889634
BF = jnp.bfloat16
F32 = jnp.float32
HB1, HB2, HB3, HB4 = 3, 3, 2, 3
FT = 512


def dot(a, b):
    return jnp.dot(a, b, preferred_element_type=F32)


def dot_nt(a, b):
    return lax.dot_general(a, b, (((1,), (1,)), ((), ())), preferred_element_type=F32)


def smem():
    return pl.BlockSpec(memory_space=pltpu.SMEM)


def whole():
    return pl.BlockSpec(memory_space=pltpu.VMEM)


def full(s):
    return pl.BlockSpec(s, lambda *i: (0,) * len(s))


def params(mib=24):
    return pltpu.CompilerParams(vmem_limit_bytes=mib * 1024 * 1024)


def cost(flops, moved, exps=0):
    return pl.CostEstimate(flops=int(flops), bytes_accessed=int(moved), transcendentals=int(exps))


def sds(shape, dtype=BF):
    return jax.ShapeDtypeStruct(shape, dtype)


def once(body, outs, args, name, scalars=1, scratch=(), flops=0):
    moved = sum(math.prod(a.shape) * a.dtype.itemsize for a in (*args, *outs))
    return pl.pallas_call(
        body,
        in_specs=[smem()] * scalars + [whole()] * (len(args) - scalars),
        out_specs=[whole()] * len(outs),
        out_shape=list(outs),
        scratch_shapes=list(scratch),
        compiler_params=params(),
        cost_estimate=cost(flops, moved),
        name=name,
    )(*args)


def per_core(ids_ref, run):
    for c in range(2):
        pl.when(ids_ref[0] == c)(lambda c=c: run(c))


def head(c, i):
    return (i + c * (HEADS // 2)) % HEADS


def spread(rep_ref, row, values):
    for g, value in enumerate(values):
        rep_ref[row : row + 1, g * HD : (g + 1) * HD] = jnp.full((1, HD), value, F32)


def hbm(shape, dtype=BF):
    return pltpu.HBM(shape, dtype)


def far(v):
    return pltpu.with_memory_space_constraint(v, pltpu.HBM)


def chunks(c):
    return (1, 4) if c == 0 else (3, 2)


def blocks_of(c):
    return (0, 3) if c == 0 else (2, 1)


def logits_body(ids_ref, pre_ref, seg_ref, k_ref, qT_ref, pT_ref, mask_ref):
    step = pl.program_id(0)

    def run(c):
        nj, bl = chunks(c), blocks_of(c)
        base = (0, nj[0] * BLK)

        @pl.when(step == 0)
        def _():
            seg = seg_ref[...].astype(F32)
            down = jnp.broadcast_to(seg, (8, SEQ)).T[:, :1]
            for b in range(2):
                qpos = lax.broadcasted_iota(jnp.int32, (BLK, BLK), 1) + bl[b] * BLK
                qseg = seg[:, bl[b] * BLK : (bl[b] + 1) * BLK]
                for j in range(nj[b]):
                    kpos = lax.broadcasted_iota(jnp.int32, (BLK, BLK), 0) + j * BLK
                    ok = (kpos <= qpos) & (down[j * BLK : (j + 1) * BLK] == qseg)
                    at = base[b] + j * BLK
                    mask_ref[at : at + BLK, :] = jnp.where(ok, 0.0, -1e30)

        for hh in range(HB1):
            h = step * HB1 + hh
            scale = [pre_ref[h, head(c, g)] * (0.125 * LOG2E) for g in range(HEADS)]
            for b in range(2):
                n = nj[b] * BLK
                qs = jnp.concatenate(
                    [
                        (
                            qT_ref[g * HD : (g + 1) * HD, b * BLK : (b + 1) * BLK].astype(F32)
                            * scale[g]
                        ).astype(BF)
                        for g in range(HEADS)
                    ],
                    axis=0,
                )
                s = dot(k_ref[:n, :], qs) + mask_ref[base[b] : base[b] + n, :]
                m = jnp.max(s, axis=0, keepdims=True)
                e = jnp.exp2(s - m)
                inv = 1.0 / jnp.sum(e, axis=0, keepdims=True)
                pT_ref[base[b] : base[b] + n, hh * BLK : (hh + 1) * BLK] = (e * inv).astype(BF)

    per_core(ids_ref, run)


def logits_softmax(ids, pre, seg, k, qT):
    return pl.pallas_call(
        logits_body,
        grid=(HEADS // HB1,),
        in_specs=[smem(), smem(), full((1, SEQ)), full((SEQ, INNER)), full((INNER, HALF))],
        out_specs=pl.BlockSpec((5 * BLK, HB1 * BLK), lambda h: (0, h)),
        out_shape=hbm((5 * BLK, HEADS * BLK)),
        scratch_shapes=[pltpu.VMEM((5 * BLK, BLK), F32)],
        compiler_params=params(),
        cost_estimate=cost(6.04e9, 10e6, 4e6),
        name="logits_softmax",
    )(ids, pre, seg, k, qT)


def attend_body(ids_ref, post_ref, vT_ref, pT_ref, uT_ref, h_ref, acc_ref):
    step = pl.program_id(0)

    def run(c):
        nj = chunks(c)
        base = (0, nj[0] * BLK)
        for b in range(2):
            n = nj[b] * BLK
            cs = slice(b * BLK, (b + 1) * BLK)
            us = []
            for hh in range(HB2):
                u = dot(vT_ref[:, :n], pT_ref[base[b] : base[b] + n, hh * BLK : (hh + 1) * BLK])
                uT_ref[hh * INNER : (hh + 1) * INNER, cs] = u.astype(BF)
                us.append(u)
            for k in range(HEADS):
                rs = slice(k * HD, (k + 1) * HD)
                t = us[0][rs, :] * post_ref[head(c, k), step * HB2]
                for hh in range(1, HB2):
                    t = t + us[hh][rs, :] * post_ref[head(c, k), step * HB2 + hh]
                acc_ref[rs, cs] += t

    @pl.when(step == 0)
    def _():
        acc_ref[...] = jnp.zeros_like(acc_ref)

    per_core(ids_ref, run)

    @pl.when(step == HEADS // HB2 - 1)
    def _():
        h_ref[...] = acc_ref[...].T.astype(BF)


def attend(ids, post, vT, pT):
    return pl.pallas_call(
        attend_body,
        grid=(HEADS // HB2,),
        in_specs=[smem(), smem(), full((INNER, SEQ)), pl.BlockSpec((5 * BLK, HB2 * BLK), lambda h: (0, h))],
        out_specs=[pl.BlockSpec((HB2 * INNER, HALF), lambda h: (h, 0)), full((HALF, INNER))],
        out_shape=[hbm((HEADS * INNER, HALF)), sds((HALF, INNER))],
        scratch_shapes=[pltpu.VMEM((INNER, HALF), F32)],
        compiler_params=params(),
        cost_estimate=cost(6.04e9, 20e6),
        name="attend",
    )(ids, post, vT, far(pT))


def split_rows(c, acc_ref, own_ref, oth_ref):
    for d in range(2):
        src = slice((c ^ d) * HALF, (c ^ d) * HALF + HALF)
        dst = slice(d * HALF, (d + 1) * HALF)
        own_ref[dst, :] = acc_ref[src, :HI].astype(BF)
        oth_ref[dst, :] = acc_ref[src, HI:].astype(BF)


def keep_sum(ref, h, k, b, g):
    g = g[:, :128] + g[:, 128:]
    ref[h, k : k + 1, :] = g if b == 0 else ref[h, k : k + 1, :] + g


def attend_back_body(
    ids_ref, post_ref, v_ref, ghT_ref, gh_ref, pT_ref, uT_ref,
    gL_ref, own_ref, oth_ref, gpost_ref, acc_ref, rep_ref,
):
    step = pl.program_id(0)

    def run(c):
        nj = chunks(c)
        base = (0, nj[0] * BLK)
        for hh in range(HB3):
            spread(rep_ref, hh, [post_ref[head(c, k), step * HB3 + hh] for k in range(HEADS)])
        for b in range(2):
            n = nj[b] * BLK
            cs = slice(b * BLK, (b + 1) * BLK)
            g2s = []
            for hh in range(HB3):
                h = step * HB3 + hh
                hs = slice(hh * BLK, (hh + 1) * BLK)
                r = jnp.zeros((1, BLK), F32)
                parts = []
                for k in range(HEADS):
                    gk = ghT_ref[k * HD : (k + 1) * HD, cs].astype(F32)
                    u = uT_ref[hh * INNER + k * HD : hh * INNER + (k + 1) * HD, cs].astype(F32)
                    g = jnp.sum(gk * u, axis=0, keepdims=True)
                    w = post_ref[head(c, k), h]
                    keep_sum(gpost_ref, hh, head(c, k), b, g)
                    r = r + g * w
                    parts.append((gk * w).astype(BF))
                gP = dot(v_ref[:n, :], jnp.concatenate(parts, axis=0))
                p = pT_ref[base[b] : base[b] + n, hs]
                gL_ref[base[b] : base[b] + n, hs] = (p.astype(F32) * (gP - r)).astype(BF)
                g2s.append((gh_ref[cs, :].astype(F32) * rep_ref[hh : hh + 1, :]).astype(BF))
            acc_ref[:n, :] += dot(pT_ref[base[b] : base[b] + n, :], jnp.concatenate(g2s, axis=0))

        @pl.when(step == HEADS // HB3 - 1)
        def _():
            split_rows(c, acc_ref, own_ref, oth_ref)

    @pl.when(step == 0)
    def _():
        acc_ref[...] = jnp.zeros_like(acc_ref)

    per_core(ids_ref, run)


def attend_back(ids, post, v, ghT, gh, pT, uT):
    return pl.pallas_call(
        attend_back_body,
        grid=(HEADS // HB3,),
        in_specs=[
            smem(), smem(), full((SEQ, INNER)), full((INNER, HALF)), full((HALF, INNER)),
            pl.BlockSpec((5 * BLK, HB3 * BLK), lambda h: (0, h)),
            pl.BlockSpec((HB3 * INNER, HALF), lambda h: (h, 0)),
        ],
        out_specs=[
            pl.BlockSpec((5 * BLK, HB3 * BLK), lambda h: (0, h)),
            full((SEQ, HI)), full((SEQ, HI)),
            pl.BlockSpec((HB3, HEADS, 128), lambda h: (h, 0, 0)),
        ],
        out_shape=[
            hbm((5 * BLK, HEADS * BLK)), sds((SEQ, HI)), sds((SEQ, HI)),
            hbm((HEADS, HEADS, 128), F32),
        ],
        scratch_shapes=[pltpu.VMEM((SEQ, INNER), F32), pltpu.VMEM((8, INNER), F32)],
        compiler_params=params(),
        cost_estimate=cost(12.1e9, 30e6),
        name="attend_back",
    )(ids, post, v, ghT, gh, far(pT), far(uT))


def scores_back_body(
    ids_ref, pre_ref, kT_ref, qT_ref, q_ref, gL_ref,
    gqa_ref, gqb_ref, own_ref, oth_ref, gpre_ref, accq_ref, acck_ref, rep_ref,
):
    step = pl.program_id(0)

    def run(c):
        nj = chunks(c)
        base = (0, nj[0] * BLK)
        scale = [
            [pre_ref[step * HB4 + hh, head(c, g)] * 0.125 for g in range(HEADS)] for hh in range(HB4)
        ]
        for hh in range(HB4):
            spread(rep_ref, hh, scale[hh])
        for b in range(2):
            n = nj[b] * BLK
            cs = slice(b * BLK, (b + 1) * BLK)
            ws, q2s = [], []
            for hh in range(HB4):
                ws.append(dot(kT_ref[:, :n], gL_ref[base[b] : base[b] + n, hh * BLK : (hh + 1) * BLK]))
                q2s.append((q_ref[cs, :].astype(F32) * rep_ref[hh : hh + 1, :]).astype(BF))
            for k in range(HEADS):
                rs = slice(k * HD, (k + 1) * HD)
                qk = qT_ref[rs, cs].astype(F32)
                t = None
                for hh in range(HB4):
                    w = ws[hh][rs, :]
                    g = jnp.sum(qk * w, axis=0, keepdims=True) * 0.125
                    keep_sum(gpre_ref, hh, head(c, k), b, g)
                    u = w * scale[hh][k]
                    t = u if t is None else t + u
                accq_ref[rs, cs] += t
            acck_ref[:n, :] += dot(gL_ref[base[b] : base[b] + n, :], jnp.concatenate(q2s, axis=0))

        @pl.when(step == HEADS // HB4 - 1)
        def _():
            split_rows(c, acck_ref, own_ref, oth_ref)

    @pl.when(step == 0)
    def _():
        accq_ref[...] = jnp.zeros_like(accq_ref)
        acck_ref[...] = jnp.zeros_like(acck_ref)

    per_core(ids_ref, run)

    @pl.when(step == HEADS // HB4 - 1)
    def _():
        gqa_ref[...] = accq_ref[:HI, :].T.astype(BF)
        gqb_ref[...] = accq_ref[HI:, :].T.astype(BF)


def scores_back(ids, pre, kT, qT, q, gL):
    return pl.pallas_call(
        scores_back_body,
        grid=(HEADS // HB4,),
        in_specs=[
            smem(), smem(), full((INNER, SEQ)), full((INNER, HALF)), full((HALF, INNER)),
            pl.BlockSpec((5 * BLK, HB4 * BLK), lambda h: (0, h)),
        ],
        out_specs=[
            full((HALF, HI)), full((HALF, HI)), full((SEQ, HI)), full((SEQ, HI)),
            pl.BlockSpec((HB4, HEADS, 128), lambda h: (h, 0, 0)),
        ],
        out_shape=[
            sds((HALF, HI)), sds((HALF, HI)), sds((SEQ, HI)), sds((SEQ, HI)),
            sds((HEADS, HEADS, 128), F32),
        ],
        scratch_shapes=[
            pltpu.VMEM((INNER, HALF), F32), pltpu.VMEM((SEQ, INNER), F32), pltpu.VMEM((8, INNER), F32),
        ],
        compiler_params=params(),
        cost_estimate=cost(12.1e9, 14e6),
        name="scores_back",
    )(ids, pre, kT, qT, q, far(gL))


def own_rows(loc, oth):
    return jnp.concatenate([loc[:BLK], oth[BLK:]], axis=0)


def project_qk_body(ids_ref, loc_ref, oth_ref, wa_ref, wb_ref, q_ref, qT_ref, k_ref, kT_ref):
    own = own_rows(loc_ref[...], oth_ref[...])
    for i, w in enumerate((wa_ref, wb_ref)):
        t = dot(own, w[:, :HI])
        cs = slice(i * HI, (i + 1) * HI)
        q_ref[:, cs] = t.astype(BF)
        qT_ref[cs, :] = t.T.astype(BF)
    project_rows(ids_ref, loc_ref, oth_ref, wa_ref, wb_ref, HI, k_ref, kT_ref)


def project_v_body(ids_ref, loc_ref, oth_ref, wa_ref, wb_ref, v_ref, vT_ref):
    project_rows(ids_ref, loc_ref, oth_ref, wa_ref, wb_ref, 0, v_ref, vT_ref)


def project_rows(ids_ref, loc_ref, oth_ref, wa_ref, wb_ref, col, k_ref, kT_ref):
    def run(c):
        for d, rows in enumerate((loc_ref, oth_ref)):
            rs = slice((c ^ d) * HALF, (c ^ d) * HALF + HALF)
            for i, w in enumerate((wa_ref, wb_ref)):
                t = dot(rows[...], w[:, col : col + HI])
                cs = slice(i * HI, (i + 1) * HI)
                k_ref[rs, cs] = t.astype(BF)
                kT_ref[cs, rs] = t.T.astype(BF)

    per_core(ids_ref, run)


def norm(v):
    inv = lax.rsqrt(jnp.mean(v * v, axis=-1, keepdims=True) + EPSILON)
    return v * inv, inv


def cast_body(q_ref, k_ref, v_ref, o_ref, in_ref, out_ref, qk_ref, vo_ref, ff_ref):
    qk_ref[:, :HI] = q_ref[...].astype(BF)
    qk_ref[:, HI:] = k_ref[...].astype(BF)
    vo_ref[:, :HI] = v_ref[...].astype(BF)
    vo_ref[:, HI:] = o_ref[...].T.astype(BF)
    ff = in_ref.shape[1]
    ff_ref[:, :ff] = in_ref[...].astype(BF)
    ff_ref[:, ff:] = out_ref[...].T.astype(BF)


def prepare_body(
    x_ref, xo_ref, c_ref, co_ref, gain_ref,
    loc_ref, oth_ref, actT_ref, own_ref, cown_ref, crest_ref, cT_ref,
):
    for src, dst, cs in ((x_ref, loc_ref, slice(0, HALF)), (xo_ref, oth_ref, slice(HALF, SEQ))):
        act = norm(src[...].astype(F32))[0] * gain_ref[...]
        dst[...] = act.astype(BF)
        actT_ref[:, cs] = act.T.astype(BF)
    own_ref[:BLK, :] = x_ref[:BLK, :]
    own_ref[BLK:, :] = xo_ref[BLK:, :]
    for dst, a, b, at in ((cown_ref, c_ref, co_ref, 0), (crest_ref, co_ref, c_ref, HALF)):
        dst[:BLK, :] = a[:BLK, :]
        dst[BLK:, :] = b[BLK:, :]
        cT_ref[:, at : at + BLK] = a[:BLK, :].astype(F32).T.astype(BF)
        cT_ref[:, at + BLK : at + HALF] = b[BLK:, :].astype(F32).T.astype(BF)


def middle_body(x_ref, h_ref, wa_ref, wb_ref, gain_ref, mid_ref, act_ref, actT_ref):
    mid = x_ref[...].astype(F32) + dot_nt(h_ref[:, :HI], wa_ref[:, HI:]) + dot_nt(h_ref[:, HI:], wb_ref[:, HI:])
    act = norm(mid)[0] * gain_ref[...]
    mid_ref[...] = mid
    act_ref[...] = act.astype(BF)
    actT_ref[...] = act.T.astype(BF)


def emit(me, scr_ref, cols, keep_ref, send_ref, outer_x):
    for e in range(16):
        x, y, z = e & 1, (e >> 1) & 1, e >> 2
        if me is None:
            ref, at, row = (keep_ref, send_ref)[e >> 3], e & 7, e * 48
        else:
            first, second = (x, y) if outer_x else (y, x)
            ref, at = (keep_ref, send_ref)[first], second * 4 + z
            row = pl.multiple_of(lax.bitwise_xor(me, e) * 48, 16)
        ref[at, :, cols] = scr_ref[pl.ds(row, 48), cols].astype(BF)


def ffn_body(
    xor, ids_ref, aown_ref, aoth_ref, aTown_ref, aToth_ref, cown_ref, coth_ref, cT_ref,
    win_ref, wout_ref, outa_ref, outb_ref, gaa_ref, gab_ref, ka_ref, sa_ref, kb_ref, sb_ref,
    acco_ref, accg_ref, scr_ref,
):
    step = pl.program_id(0)
    last = pl.num_programs(0) - 1
    me = ids_ref[1] if xor else None

    @pl.when(step == 0)
    def _():
        acco_ref[...] = jnp.zeros_like(acco_ref)
        accg_ref[...] = jnp.zeros_like(accg_ref)

    win, wout = win_ref[...], wout_ref[...]
    hid, gpre = [], []
    for a_ref, c_ref, rs in ((aown_ref, cown_ref, slice(0, HALF)), (aoth_ref, coth_ref, slice(HALF, SEQ))):
        v = dot(a_ref[...], win)
        sq = v * v
        t = jnp.tanh(0.7978845608028654 * v * (1.0 + 0.044715 * sq))
        hidden = (0.5 * v * (1.0 + t)).astype(BF)
        slope = 0.5 * (1.0 + t) + 0.5 * v * (1.0 - t * t) * (
            0.7978845608028654 * (1.0 + 0.134145 * sq)
        )
        gh = dot(c_ref[...], wout).astype(BF).astype(F32)
        gp = (gh * slope).astype(BF)
        acco_ref[rs, :] += dot_nt(hidden, wout)
        accg_ref[rs, :] += dot_nt(gp, win)
        hid.append(hidden)
        gpre.append(gp)
    scr_ref[...] = dot(cT_ref[:, :HALF], hid[0]) + dot(cT_ref[:, HALF:], hid[1])
    emit(me, scr_ref, slice(0, FT), ka_ref, sa_ref, True)
    scr_ref[...] = dot(aTown_ref[...], gpre[0]) + dot(aToth_ref[...], gpre[1])
    emit(me, scr_ref, slice(0, FT), kb_ref, sb_ref, False)

    @pl.when(step == last)
    def _():
        outa_ref[...] = acco_ref[:HALF, :]
        outb_ref[...] = acco_ref[HALF:, :].astype(BF)
        gaa_ref[...] = accg_ref[:HALF, :]
        gab_ref[...] = accg_ref[HALF:, :].astype(BF)


def ffn(xor, ids, aown, aoth, aTown, aToth, cown, coth, cT, w):
    width = w.shape[1] // 2
    steps = width // FT
    tile = pl.BlockSpec((INNER, FT), lambda t: (0, t))
    tile2 = pl.BlockSpec((INNER, FT), lambda t: (0, t + steps))
    grad = pl.BlockSpec((8, 48, FT), lambda t: (0, 0, t))
    half, halfT = full((HALF, INNER)), full((INNER, HALF))
    return pl.pallas_call(
        lambda *r: ffn_body(xor, *r),
        grid=(steps,),
        in_specs=[smem(), half, half, halfT, halfT, half, half, full((INNER, SEQ)), tile, tile2],
        out_specs=[half, half, half, half, grad, grad, grad, grad],
        out_shape=[
            sds((HALF, INNER), F32), sds((HALF, INNER)), sds((HALF, INNER), F32), sds((HALF, INNER)),
        ] + [sds((8, 48, width))] * 4,
        scratch_shapes=[
            pltpu.VMEM((SEQ, INNER), F32), pltpu.VMEM((SEQ, INNER), F32), pltpu.VMEM((INNER, FT), F32),
        ],
        compiler_params=params(48),
        cost_estimate=cost(14.5e9, 20e6, 1.6e6),
        name="ffn",
    )(ids, aown, aoth, aTown, aToth, cown, coth, cT, w, w)


def middle_back_body(
    ga_ref, gr_ref, mid_ref, cot_ref, gain_ref, h_ref, wa_ref, wb_ref,
    stay_ref, sent_ref, gh_ref, ghT_ref, gain_out, gwa_ref, gwb_ref,
):
    ga = ga_ref[...] + gr_ref[...].astype(F32)
    normed, inv = norm(mid_ref[...])
    scaled = ga * gain_ref[...]
    gm = cot_ref[...].astype(F32) + inv * (
        scaled - normed * jnp.mean(scaled * normed, axis=-1, keepdims=True)
    )
    gain_out[...] = jnp.sum(ga * normed, axis=0, keepdims=True)
    stay_ref[...] = gm[:BLK]
    sent_ref[...] = gm[BLK:]
    grad = gm.astype(BF)
    gT = gm.T.astype(BF)
    for i, (w, gw) in enumerate(((wa_ref, gwa_ref), (wb_ref, gwb_ref))):
        cs = slice(i * HI, (i + 1) * HI)
        t = dot(grad, w[:, HI:])
        gh_ref[:, cs] = t.astype(BF)
        ghT_ref[cs, :] = t.T.astype(BF)
        gw[...] = dot(gT, h_ref[:, cs]).astype(BF)


def joined(own, got):
    a, b = own.astype(F32), got.astype(F32)
    return jnp.concatenate([a[:HALF] + b[HALF:], a[HALF:] + b[:HALF]], axis=0).astype(BF)


def grad_vo_body(xor, ids_ref, aT_ref, gv_ref, rv_ref, go_ref, ro_ref, gv_out, ka, sa, kb, sb, scr):
    me = ids_ref[1] if xor else None
    gv = joined(gv_ref[...], rv_ref[...])
    gv_out[...] = gv
    scr[...] = dot(aT_ref[...], gv)
    emit(me, scr, slice(0, HI), ka, sa, True)
    scr[...] = go_ref[...].astype(F32) + ro_ref[...].astype(F32)
    emit(me, scr, slice(0, HI), kb, sb, False)


def grad_qk_body(xor, ids_ref, aT_ref, gq_ref, rq_ref, gk_ref, rk_ref, gq_out, gk_out, ka, sa, kb, sb, scr):
    me = ids_ref[1] if xor else None
    gq, rq = gq_ref[...], rq_ref[...]
    gq = jnp.concatenate([gq[:BLK], rq[BLK:], rq[:BLK], gq[BLK:]], axis=0)
    gq_out[...] = gq
    scr[...] = dot(aT_ref[...], gq)
    emit(me, scr, slice(0, HI), ka, sa, True)
    gk = joined(gk_ref[...], rk_ref[...])
    gk_out[...] = gk
    scr[...] = dot(aT_ref[...], gk)
    emit(me, scr, slice(0, HI), kb, sb, False)


def act_back_body(gq_ref, gk_ref, gv_ref, qk_ref, vo_ref, loc_ref, oth_ref):
    for rs, ref in ((slice(0, HALF), loc_ref), (slice(HALF, SEQ), oth_ref)):
        t = dot_nt(gq_ref[rs, :], qk_ref[:, :HI]) + dot_nt(gk_ref[rs, :], qk_ref[:, HI:])
        ref[...] = (t + dot_nt(gv_ref[rs, :], vo_ref[:, :HI])).astype(ref.dtype)


def output_body(mid_ref, own_ref, got_ref, stay_ref, sent_ref):
    out = (mid_ref[...] + own_ref[...] + got_ref[...].astype(F32)).astype(BF)
    stay_ref[...] = out[:BLK]
    sent_ref[...] = out[BLK:]


def tokens_back_body(
    ga_ref, gr_ref, x_ref, gain_ref, stay_ref, got_ref, gain2_ref, gpre_ref, gpost_ref,
    ostay_ref, ogot_ref, out_ref, small_ref, output_ref,
):
    output_ref[:BLK, :] = ostay_ref[...]
    output_ref[BLK:, :] = ogot_ref[...]
    ga = ga_ref[...] + gr_ref[...].astype(F32)
    normed, inv = norm(x_ref[...].astype(F32))
    scaled = ga * gain_ref[...]
    back = inv * (scaled - normed * jnp.mean(scaled * normed, axis=-1, keepdims=True))
    out_ref[:BLK, :] = (stay_ref[...] + back[:BLK]).astype(BF)
    out_ref[BLK:, :] = (got_ref[...] + back[BLK:]).astype(BF)
    gain1 = jnp.sum(ga * normed, axis=0, keepdims=True)
    small_ref[...] = jnp.zeros_like(small_ref)
    for i in range(6):
        cs = slice(i * 128, (i + 1) * 128)
        small_ref[i : i + 1, :] = gain1[:, cs]
        small_ref[8 + i : 9 + i, :] = gain2_ref[:, cs]
    small_ref[16 : 16 + HEADS, :HEADS] = jnp.sum(gpre_ref[...], axis=-1)
    small_ref[32 : 32 + HEADS, :HEADS] = jnp.sum(gpost_ref[...], axis=-1)


def swap(v):
    return lax.ppermute(v, "tensor", [(0, 1), (1, 0)])


def hop(v, mask):
    n = lax.axis_size("dp")
    return lax.ppermute(v, "dp", [(i, i ^ mask) for i in range(n)])


def after(v, *done):
    return lax.optimization_barrier((v, *done))[0]


def place_body(ids_ref, ax, ay, bx, by, out):
    me = ids_ref[1]
    w = ax.shape[3]
    for t, ref in enumerate((ax, ay, bx, by)):
        col = (t // 2) * w
        for i in range(2):
            for j in range(4):
                e = 4 * j + ((2 * i + t) if t < 2 else (i + 2 * (t - 2)))
                row = pl.multiple_of(lax.bitwise_xor(me, e) * 48, 16)
                out[pl.ds(row, 48), col : col + w] = ref[i, j]


def gather_z(shard):
    return [shard] + [hop(shard, 4 * e) for e in range(1, 4)]


def gather_one(pieces):
    z = jnp.stack(pieces, axis=0)
    w = z.shape[2] // 2
    a, b = z[:, :, :w], z[:, :, w:]
    return a, hop(a, 2), b, hop(b, 1)


def gather_two(a, ra, b, rb):
    a2, b2 = jnp.stack([a, ra], axis=0), jnp.stack([b, rb], axis=0)
    return a2, hop(a2, 1), b2, hop(b2, 2)


def gathered(ids, parts):
    return once(place_body, (sds((768, 2 * parts[0].shape[3])),), (ids, *parts), "place")[0]


def fold_one_body(ka, ra, kb, rb, oka, osa, okb, osb):
    for k, r, keep, send in ((ka, ra, oka, osa), (kb, rb, okb, osb)):
        t = (k[...].astype(F32) + r[...].astype(F32)).astype(BF)
        keep[...] = t[:4]
        send[...] = t[4:]


def fold_two_body(groups, *refs):
    ins, own, sends = refs[: 4 * groups], refs[4 * groups], refs[4 * groups + 1 :]
    at = 0
    for k, r in zip(ins[::2], ins[1::2]):
        w = k.shape[2]
        cs = slice(at, at + w)
        at += w
        t = k[...].astype(F32) + r[...].astype(F32)
        own[:, cs] = t[0]
        for e in range(3):
            sends[e][:, cs] = t[e + 1].astype(BF)


def fold_one(ka, ra, kb, rb):
    piece = sds((4,) + ka.shape[1:])
    return once(fold_one_body, (piece,) * 4, (ka, ra, kb, rb), "fold_one", scalars=0)


def fold_two(*parts):
    w = sum(p.shape[2] for p in parts[::2])
    body = lambda *r: fold_two_body(len(parts) // 4, *r)
    outs = (sds((48, w), F32),) + (sds((48, w)),) * 3
    return once(body, outs, parts, "fold_two", scalars=0)


def fold_ff_body(ka, ra, kb, rb, own, send):
    w = ka.shape[2]
    for k, r, cs in ((ka, ra, slice(0, w)), (kb, rb, slice(w, 2 * w))):
        t = (k[...].astype(F32) + r[...].astype(F32)).astype(BF)
        for z in range(2):
            own[z, :, cs] = t[2 * z]
            send[z, :, cs] = t[2 * z + 1]


def fold_ff_two_body(own, got, keep, send):
    t = own[...].astype(F32) + got[...].astype(F32)
    keep[...] = t[0]
    send[...] = t[1].astype(BF)


def scatter_plain(ka, sa, kb, sb):
    w = ka.shape[2]
    flat = jnp.concatenate(
        [jnp.concatenate([k, s], axis=0).reshape(768, w) for k, s in ((ka, sa), (kb, sb))], axis=1
    )
    return lax.psum_scatter(flat.astype(F32), "dp", scatter_dimension=0, tiled=True)


def sum_all(v):
    n = lax.axis_size("dp")
    v = v + swap(v)
    bit = 1
    while bit < n:
        v = v + hop(v, bit)
        bit *= 2
    return v


def on_device(
    tokens, cotangent, segment_ids, norm1_gain, w_query, w_key, w_value, pre_mix, post_mix,
    w_output, norm2_gain, w_in, w_out,
):
    ids = jnp.stack([lax.axis_index("tensor"), lax.axis_index("dp")]).astype(jnp.int32)
    xor = lax.axis_size("dp") == 16
    low = lambda v: v.astype(BF)
    D = norm1_gain.shape[0]
    tie = lax.optimization_barrier
    gain1, gain2 = norm1_gain.reshape(1, D), norm2_gain.reshape(1, D)
    seg = segment_ids.reshape(1, SEQ)

    every = lambda v: lax.all_gather(v, "dp", axis=0, tiled=True)
    r, ff = w_in.shape
    shard_qk, shard_vo, shard_ff = once(
        cast_body, (sds((r, INNER)), sds((r, INNER)), sds((r, 2 * ff))),
        tuple(far(w) for w in (w_query, w_key, w_value, w_output, w_in, w_out)), "cast", scalars=0,
    )
    if xor:
        z_qk = gather_z(shard_qk)
    w_ff = every(shard_ff)
    x_oth, cot_oth = swap(tokens), swap(cotangent)
    if xor:
        a, ra, b, rb = gather_one(z_qk)
        x_oth = after(x_oth, a)
    act_loc, act_oth, actT, x_own, cot_own, cot_rest, cotT = once(
        prepare_body,
        (sds((HALF, D)), sds((HALF, D)), hbm((D, SEQ)), hbm((HALF, D)), hbm((HALF, D)), hbm((HALF, D)), hbm((D, SEQ))),
        (tokens, x_oth, cotangent, cot_oth, gain1), "prepare", scalars=0,
    )
    if xor:
        z_vo = gather_z(after(shard_vo, *z_qk[1:]))
        ra, rb, act_loc = tie((ra, rb, act_loc))
        qk_parts = gather_two(a, ra, b, rb)
        *z_vo, ax, ay, bx, by = tie((*z_vo, *qk_parts))
        qk_parts = (ax, ay, bx, by)
        a, ra, b, rb = gather_one(z_vo)
        w_qk = gathered(ids, qk_parts)
        ra, rb = tie((ra, rb, w_qk))[:2]
        vo_parts = gather_two(a, ra, b, rb)
    else:
        w_qk, w_vo = every(shard_qk), every(shard_vo)
    q, qT, k, kT = once(
        project_qk_body,
        (hbm((HALF, INNER)), sds((INNER, HALF)), sds((SEQ, INNER)), hbm((INNER, SEQ))),
        (ids, act_loc, act_oth, w_qk, swap(w_qk)), "project_qk", flops=1.8e9,
    )
    pT = logits_softmax(ids, pre_mix, seg, k, qT)
    if xor:
        w_vo = gathered(ids, tie((*vo_parts, pT))[:4])
    vo_o = swap(w_vo)
    v, vT = once(
        project_v_body, (hbm((SEQ, INNER)), sds((INNER, SEQ))),
        (ids, act_loc, act_oth, w_vo, vo_o), "project_v", flops=1.2e9,
    )
    uT, heads = attend(ids, post_mix, vT, pT)
    mid, act2, act2T = once(
        middle_body, (hbm((HALF, D), F32), sds((HALF, D)), sds((D, HALF))),
        (x_own, heads, w_vo, vo_o, gain2), "middle", scalars=0, flops=6e8,
    )
    out_own, out_oth, ga_own, ga_oth, ka, sa, kb, sb = ffn(
        xor, ids, act2, swap(act2), act2T, swap(act2T), far(cot_own), far(cot_rest), far(cotT), far(w_ff)
    )
    if xor:
        ra, rb = hop(sa, 1), hop(sb, 2)
    stay, sent, gh, ghT, gain2_part, gwo, gwo_o = once(
        middle_back_body,
        (
            hbm((BLK, D), F32), hbm((BLK, D), F32), sds((HALF, INNER)), sds((INNER, HALF)),
            hbm((1, D), F32), sds((D, HI)), sds((D, HI)),
        ),
        (ga_own, swap(ga_oth), mid, cot_own, gain2, heads, w_vo, vo_o),
        "middle_back", scalars=0, flops=1.2e9,
    )
    gL, gv, gv_o, gpost = attend_back(ids, post_mix, v, ghT, gh, pT, uT)
    grads = (sds((8, 48, HI)),) * 4
    if xor:
        ra, rb, gv, gv_o = tie((ra, rb, gv, gv_o))
        ff_ka, ff_sa, ff_kb, ff_sb = fold_one(ka, ra, kb, rb)
        ff_ra, ff_rb = hop(ff_sa, 2), hop(ff_sb, 1)
        gv_o = after(gv_o, ff_sa)
    gv, *vo = once(
        lambda *r: grad_vo_body(xor, *r), (hbm((SEQ, HI)),) + grads,
        (ids, actT, gv, swap(gv_o), gwo, swap(gwo_o)), "grad_vo",
        scratch=[pltpu.VMEM((D, HI), F32)], flops=6e8,
    )
    if xor:
        vo_ka, vo_sa, vo_kb, vo_sb = vo
        vo_ra, vo_rb = hop(vo_sa, 1), hop(vo_sb, 2)
        gL = after(gL, ff_sa, vo_sa)
    gq, gq_o, gk, gk_o, gpre = scores_back(ids, pre_mix, kT, qT, q, gL)
    if xor:
        vo_ra, vo_rb, gq = tie((vo_ra, vo_rb, gq))
        vo_ka, vo_sa, vo_kb, vo_sb = fold_one(vo_ka, vo_ra, vo_kb, vo_rb)
        vo_ra, vo_rb = hop(vo_sa, 2), hop(vo_sb, 1)
        gq_o, gk_o, ff_ra, ff_rb, vo_sa = tie((gq_o, gk_o, ff_ra, ff_rb, vo_sa))
        wide = ff_ka.shape[2] * 2
        ff_own, ff_send = once(
            fold_ff_body, (sds((2, 48, wide)),) * 2, (ff_ka, ff_ra, ff_kb, ff_rb), "fold_ff", scalars=0
        )
        ff_got = hop(ff_send, 4)
        gq, gk = tie((gq, gk, ff_send))[:2]
    gq, gk, *qk = once(
        lambda *r: grad_qk_body(xor, *r), (sds((SEQ, HI)),) * 2 + grads,
        (ids, actT, gq, swap(gq_o), gk, swap(gk_o)), "grad_qk",
        scratch=[pltpu.VMEM((D, HI), F32)], flops=1.2e9,
    )
    out_stay, out_sent = once(
        output_body, (sds((BLK, D)),) * 2, (mid, out_own, after(swap(out_oth), gq)), "output", scalars=0
    )
    if xor:
        qk_ka, qk_sa, qk_kb, qk_sb = qk
        qk_ra, qk_rb = hop(qk_sa, 1), hop(qk_sb, 2)
        gq = tie((gq, qk_sa, out_sent))[0]
    ga_loc, ga_oth = once(
        act_back_body, (sds((HALF, D), F32), sds((HALF, D))), (gq, gk, gv, w_qk, w_vo),
        "act_back", scalars=0, flops=1.8e9,
    )
    grad_tokens, small, output = once(
        tokens_back_body, (sds((HALF, D)), sds((48, 128), F32), sds((HALF, D))),
        (
            ga_loc, swap(ga_oth), tokens, gain1, stay, swap(sent), gain2_part, gpre, gpost,
            out_stay, swap(out_sent),
        ),
        "tokens_back", scalars=0,
    )
    if xor:
        got = swap(small)
        ff_got, qk_ra, qk_rb, small, got = tie((ff_got, qk_ra, qk_rb, small, got))
        ff_own, ff_send = once(
            fold_ff_two_body, (sds((48, wide), F32), sds((48, wide))), (ff_own, ff_got), "fold_ff_two", scalars=0
        )
        ff_got = hop(ff_send, 8)
        qk_ka, qk_sa, qk_kb, qk_sb = fold_one(*tie((qk_ka, qk_ra, qk_kb, qk_rb, ff_send))[:4])
        qk_ra, qk_rb = hop(qk_sa, 2), hop(qk_sb, 1)
        small, got = tie((small, got, qk_sa))[:2]
        small = small + got
        got = hop(small, 1)
        qk_ra, qk_rb, got, small = tie((qk_ra, qk_rb, got, small))
        at, *sends = fold_two(qk_ka, qk_ra, qk_kb, qk_rb, vo_ka, vo_ra, vo_kb, vo_rb)
        gots = [hop(sends[e], 4 * (e + 1)) for e in range(3)]
        small, got = tie((small, got, at))[:2]
        small = small + got
        small = small + hop(small, 2)
        small = small + hop(small, 4)
        small = small + hop(small, 8)
        grad_ffn = ff_own + ff_got.astype(F32)
        for got in gots:
            at = at + got.astype(F32)
        grad_qk, grad_vo = at[:, :INNER], at[:, INNER:]
    else:
        grad_qk, grad_vo = scatter_plain(*qk), scatter_plain(*vo)
        grad_ffn = scatter_plain(ka, sa, kb, sb)
        small = sum_all(small)
    return (
        output, grad_tokens, small[:6].reshape(D), grad_qk[:, :HI], grad_qk[:, HI:], grad_vo[:, :HI],
        small[16 : 16 + HEADS, :HEADS], small[32 : 32 + HEADS, :HEADS].T,
        grad_vo[:, HI:].T, small[8:14].reshape(D), grad_ffn[:, ff:], grad_ffn[:, :ff].T,
    )


def solution(mesh):
    rows = P(("dp", "tensor"), None)
    w, wt = P("dp", "tensor"), P("tensor", "dp")
    return jax.shard_map(
        on_device,
        mesh=mesh,
        in_specs=(rows, rows, P("dp"), P(), w, w, w, P(), P(), wt, P(), w, wt),
        out_specs=(rows, rows, P(), w, w, w, P(), P(), wt, P(), w, wt),
        check_vma=False,
    )
```

```python
import math

import jax
import jax.numpy as jnp
from jax import lax
from jax.experimental import pallas as pl
from jax.experimental.pallas import tpu as pltpu
from jax.sharding import PartitionSpec as P

HEADS = 12
HD = 64
INNER = 768
HI = INNER // 2
SEQ = 1024
HALF = SEQ // 2
BLK = 256
EPSILON = 1e-06
LOG2E = 1.4426950408889634
BF = jnp.bfloat16
F32 = jnp.float32
HB1, HB2, HB3, HB4 = 3, 3, 2, 3
FT = 512


def dot(a, b):
    return jnp.dot(a, b, preferred_element_type=F32)


def dot_nt(a, b):
    return lax.dot_general(a, b, (((1,), (1,)), ((), ())), preferred_element_type=F32)


def smem():
    return pl.BlockSpec(memory_space=pltpu.SMEM)


def whole():
    return pl.BlockSpec(memory_space=pltpu.VMEM)


def full(s):
    return pl.BlockSpec(s, lambda *i: (0,) * len(s))


def params(mib=24):
    return pltpu.CompilerParams(vmem_limit_bytes=mib * 1024 * 1024)


def cost(flops, moved, exps=0):
    return pl.CostEstimate(flops=int(flops), bytes_accessed=int(moved), transcendentals=int(exps))


def sds(shape, dtype=BF):
    return jax.ShapeDtypeStruct(shape, dtype)


def once(body, outs, args, name, scalars=1, scratch=(), flops=0):
    moved = sum(math.prod(a.shape) * a.dtype.itemsize for a in (*args, *outs))
    return pl.pallas_call(
        body,
        in_specs=[smem()] * scalars + [whole()] * (len(args) - scalars),
        out_specs=[whole()] * len(outs),
        out_shape=list(outs),
        scratch_shapes=list(scratch),
        compiler_params=params(),
        cost_estimate=cost(flops, moved),
        name=name,
    )(*args)


def per_core(ids_ref, run):
    for c in range(2):
        pl.when(ids_ref[0] == c)(lambda c=c: run(c))


def head(c, i):
    return (i + c * (HEADS // 2)) % HEADS


def spread(rep_ref, row, values):
    for g, value in enumerate(values):
        rep_ref[row : row + 1, g * HD : (g + 1) * HD] = jnp.full((1, HD), value, F32)


def hbm(shape, dtype=BF):
    return pltpu.HBM(shape, dtype)


def far(v):
    return pltpu.with_memory_space_constraint(v, pltpu.HBM)


def chunks(c):
    return (1, 4) if c == 0 else (3, 2)


def blocks_of(c):
    return (0, 3) if c == 0 else (2, 1)


def logits_body(ids_ref, pre_ref, seg_ref, k_ref, qT_ref, pT_ref, mask_ref):
    step = pl.program_id(0)

    def run(c):
        nj, bl = chunks(c), blocks_of(c)
        base = (0, nj[0] * BLK)

        @pl.when(step == 0)
        def _():
            seg = seg_ref[...].astype(F32)
            down = jnp.broadcast_to(seg, (8, SEQ)).T[:, :1]
            for b in range(2):
                qpos = lax.broadcasted_iota(jnp.int32, (BLK, BLK), 1) + bl[b] * BLK
                qseg = seg[:, bl[b] * BLK : (bl[b] + 1) * BLK]
                for j in range(nj[b]):
                    kpos = lax.broadcasted_iota(jnp.int32, (BLK, BLK), 0) + j * BLK
                    ok = (kpos <= qpos) & (down[j * BLK : (j + 1) * BLK] == qseg)
                    at = base[b] + j * BLK
                    mask_ref[at : at + BLK, :] = jnp.where(ok, 0.0, -1e30)

        for hh in range(HB1):
            h = step * HB1 + hh
            scale = [pre_ref[h, head(c, g)] * (0.125 * LOG2E) for g in range(HEADS)]
            for b in range(2):
                n = nj[b] * BLK
                qs = jnp.concatenate(
                    [
                        (
                            qT_ref[g * HD : (g + 1) * HD, b * BLK : (b + 1) * BLK].astype(F32)
                            * scale[g]
                        ).astype(BF)
                        for g in range(HEADS)
                    ],
                    axis=0,
                )
                s = dot(k_ref[:n, :], qs) + mask_ref[base[b] : base[b] + n, :]
                m = jnp.max(s, axis=0, keepdims=True)
                e = jnp.exp2(s - m)
                inv = 1.0 / jnp.sum(e, axis=0, keepdims=True)
                pT_ref[base[b] : base[b] + n, hh * BLK : (hh + 1) * BLK] = (e * inv).astype(BF)

    per_core(ids_ref, run)


def logits_softmax(ids, pre, seg, k, qT):
    return pl.pallas_call(
        logits_body,
        grid=(HEADS // HB1,),
        in_specs=[smem(), smem(), full((1, SEQ)), full((SEQ, INNER)), full((INNER, HALF))],
        out_specs=pl.BlockSpec((5 * BLK, HB1 * BLK), lambda h: (0, h)),
        out_shape=hbm((5 * BLK, HEADS * BLK)),
        scratch_shapes=[pltpu.VMEM((5 * BLK, BLK), F32)],
        compiler_params=params(),
        cost_estimate=cost(6.04e9, 10e6, 4e6),
        name="logits_softmax",
    )(ids, pre, seg, k, qT)


def attend_body(ids_ref, post_ref, vT_ref, pT_ref, uT_ref, h_ref, acc_ref):
    step = pl.program_id(0)

    def run(c):
        nj = chunks(c)
        base = (0, nj[0] * BLK)
        for b in range(2):
            n = nj[b] * BLK
            cs = slice(b * BLK, (b + 1) * BLK)
            us = []
            for hh in range(HB2):
                u = dot(vT_ref[:, :n], pT_ref[base[b] : base[b] + n, hh * BLK : (hh + 1) * BLK])
                uT_ref[hh * INNER : (hh + 1) * INNER, cs] = u.astype(BF)
                us.append(u)
            for k in range(HEADS):
                rs = slice(k * HD, (k + 1) * HD)
                t = us[0][rs, :] * post_ref[head(c, k), step * HB2]
                for hh in range(1, HB2):
                    t = t + us[hh][rs, :] * post_ref[head(c, k), step * HB2 + hh]
                acc_ref[rs, cs] += t

    @pl.when(step == 0)
    def _():
        acc_ref[...] = jnp.zeros_like(acc_ref)

    per_core(ids_ref, run)

    @pl.when(step == HEADS // HB2 - 1)
    def _():
        h_ref[...] = acc_ref[...].T.astype(BF)


def attend(ids, post, vT, pT):
    return pl.pallas_call(
        attend_body,
        grid=(HEADS // HB2,),
        in_specs=[smem(), smem(), full((INNER, SEQ)), pl.BlockSpec((5 * BLK, HB2 * BLK), lambda h: (0, h))],
        out_specs=[pl.BlockSpec((HB2 * INNER, HALF), lambda h: (h, 0)), full((HALF, INNER))],
        out_shape=[hbm((HEADS * INNER, HALF)), sds((HALF, INNER))],
        scratch_shapes=[pltpu.VMEM((INNER, HALF), F32)],
        compiler_params=params(),
        cost_estimate=cost(6.04e9, 20e6),
        name="attend",
    )(ids, post, vT, far(pT))


def split_rows(c, acc_ref, own_ref, oth_ref):
    for d in range(2):
        src = slice((c ^ d) * HALF, (c ^ d) * HALF + HALF)
        dst = slice(d * HALF, (d + 1) * HALF)
        own_ref[dst, :] = acc_ref[src, :HI].astype(BF)
        oth_ref[dst, :] = acc_ref[src, HI:].astype(BF)


def keep_sum(ref, h, k, b, g):
    g = g[:, :128] + g[:, 128:]
    ref[h, k : k + 1, :] = g if b == 0 else ref[h, k : k + 1, :] + g


def attend_back_body(
    ids_ref, post_ref, v_ref, ghT_ref, gh_ref, pT_ref, uT_ref,
    gL_ref, own_ref, oth_ref, gpost_ref, acc_ref, rep_ref,
):
    step = pl.program_id(0)

    def run(c):
        nj = chunks(c)
        base = (0, nj[0] * BLK)
        for hh in range(HB3):
            spread(rep_ref, hh, [post_ref[head(c, k), step * HB3 + hh] for k in range(HEADS)])
        for b in range(2):
            n = nj[b] * BLK
            cs = slice(b * BLK, (b + 1) * BLK)
            g2s = []
            for hh in range(HB3):
                h = step * HB3 + hh
                hs = slice(hh * BLK, (hh + 1) * BLK)
                r = jnp.zeros((1, BLK), F32)
                parts = []
                for k in range(HEADS):
                    gk = ghT_ref[k * HD : (k + 1) * HD, cs].astype(F32)
                    u = uT_ref[hh * INNER + k * HD : hh * INNER + (k + 1) * HD, cs].astype(F32)
                    g = jnp.sum(gk * u, axis=0, keepdims=True)
                    w = post_ref[head(c, k), h]
                    keep_sum(gpost_ref, hh, head(c, k), b, g)
                    r = r + g * w
                    parts.append((gk * w).astype(BF))
                gP = dot(v_ref[:n, :], jnp.concatenate(parts, axis=0))
                p = pT_ref[base[b] : base[b] + n, hs]
                gL_ref[base[b] : base[b] + n, hs] = (p.astype(F32) * (gP - r)).astype(BF)
                g2s.append((gh_ref[cs, :].astype(F32) * rep_ref[hh : hh + 1, :]).astype(BF))
            acc_ref[:n, :] += dot(pT_ref[base[b] : base[b] + n, :], jnp.concatenate(g2s, axis=0))

        @pl.when(step == HEADS // HB3 - 1)
        def _():
            split_rows(c, acc_ref, own_ref, oth_ref)

    @pl.when(step == 0)
    def _():
        acc_ref[...] = jnp.zeros_like(acc_ref)

    per_core(ids_ref, run)


def attend_back(ids, post, v, ghT, gh, pT, uT):
    return pl.pallas_call(
        attend_back_body,
        grid=(HEADS // HB3,),
        in_specs=[
            smem(), smem(), full((SEQ, INNER)), full((INNER, HALF)), full((HALF, INNER)),
            pl.BlockSpec((5 * BLK, HB3 * BLK), lambda h: (0, h)),
            pl.BlockSpec((HB3 * INNER, HALF), lambda h: (h, 0)),
        ],
        out_specs=[
            pl.BlockSpec((5 * BLK, HB3 * BLK), lambda h: (0, h)),
            full((SEQ, HI)), full((SEQ, HI)),
            pl.BlockSpec((HB3, HEADS, 128), lambda h: (h, 0, 0)),
        ],
        out_shape=[
            hbm((5 * BLK, HEADS * BLK)), sds((SEQ, HI)), sds((SEQ, HI)),
            hbm((HEADS, HEADS, 128), F32),
        ],
        scratch_shapes=[pltpu.VMEM((SEQ, INNER), F32), pltpu.VMEM((8, INNER), F32)],
        compiler_params=params(),
        cost_estimate=cost(12.1e9, 30e6),
        name="attend_back",
    )(ids, post, v, ghT, gh, far(pT), far(uT))


def scores_back_body(
    ids_ref, pre_ref, kT_ref, qT_ref, q_ref, gL_ref,
    gqa_ref, gqb_ref, own_ref, oth_ref, gpre_ref, accq_ref, acck_ref, rep_ref,
):
    step = pl.program_id(0)

    def run(c):
        nj = chunks(c)
        base = (0, nj[0] * BLK)
        scale = [
            [pre_ref[step * HB4 + hh, head(c, g)] * 0.125 for g in range(HEADS)] for hh in range(HB4)
        ]
        for hh in range(HB4):
            spread(rep_ref, hh, scale[hh])
        for b in range(2):
            n = nj[b] * BLK
            cs = slice(b * BLK, (b + 1) * BLK)
            ws, q2s = [], []
            for hh in range(HB4):
                ws.append(dot(kT_ref[:, :n], gL_ref[base[b] : base[b] + n, hh * BLK : (hh + 1) * BLK]))
                q2s.append((q_ref[cs, :].astype(F32) * rep_ref[hh : hh + 1, :]).astype(BF))
            for k in range(HEADS):
                rs = slice(k * HD, (k + 1) * HD)
                qk = qT_ref[rs, cs].astype(F32)
                t = None
                for hh in range(HB4):
                    w = ws[hh][rs, :]
                    g = jnp.sum(qk * w, axis=0, keepdims=True) * 0.125
                    keep_sum(gpre_ref, hh, head(c, k), b, g)
                    u = w * scale[hh][k]
                    t = u if t is None else t + u
                accq_ref[rs, cs] += t
            acck_ref[:n, :] += dot(gL_ref[base[b] : base[b] + n, :], jnp.concatenate(q2s, axis=0))

        @pl.when(step == HEADS // HB4 - 1)
        def _():
            split_rows(c, acck_ref, own_ref, oth_ref)

    @pl.when(step == 0)
    def _():
        accq_ref[...] = jnp.zeros_like(accq_ref)
        acck_ref[...] = jnp.zeros_like(acck_ref)

    per_core(ids_ref, run)

    @pl.when(step == HEADS // HB4 - 1)
    def _():
        gqa_ref[...] = accq_ref[:HI, :].T.astype(BF)
        gqb_ref[...] = accq_ref[HI:, :].T.astype(BF)


def scores_back(ids, pre, kT, qT, q, gL):
    return pl.pallas_call(
        scores_back_body,
        grid=(HEADS // HB4,),
        in_specs=[
            smem(), smem(), full((INNER, SEQ)), full((INNER, HALF)), full((HALF, INNER)),
            pl.BlockSpec((5 * BLK, HB4 * BLK), lambda h: (0, h)),
        ],
        out_specs=[
            full((HALF, HI)), full((HALF, HI)), full((SEQ, HI)), full((SEQ, HI)),
            pl.BlockSpec((HB4, HEADS, 128), lambda h: (h, 0, 0)),
        ],
        out_shape=[
            sds((HALF, HI)), sds((HALF, HI)), sds((SEQ, HI)), sds((SEQ, HI)),
            sds((HEADS, HEADS, 128), F32),
        ],
        scratch_shapes=[
            pltpu.VMEM((INNER, HALF), F32), pltpu.VMEM((SEQ, INNER), F32), pltpu.VMEM((8, INNER), F32),
        ],
        compiler_params=params(),
        cost_estimate=cost(12.1e9, 14e6),
        name="scores_back",
    )(ids, pre, kT, qT, q, far(gL))


def own_rows(loc, oth):
    return jnp.concatenate([loc[:BLK], oth[BLK:]], axis=0)


def project_qk_body(ids_ref, loc_ref, oth_ref, wa_ref, wb_ref, q_ref, qT_ref, k_ref, kT_ref):
    own = own_rows(loc_ref[...], oth_ref[...])
    for i, w in enumerate((wa_ref, wb_ref)):
        t = dot(own, w[:, :HI])
        cs = slice(i * HI, (i + 1) * HI)
        q_ref[:, cs] = t.astype(BF)
        qT_ref[cs, :] = t.T.astype(BF)
    project_rows(ids_ref, loc_ref, oth_ref, wa_ref, wb_ref, HI, k_ref, kT_ref)


def project_v_body(ids_ref, loc_ref, oth_ref, wa_ref, wb_ref, v_ref, vT_ref):
    project_rows(ids_ref, loc_ref, oth_ref, wa_ref, wb_ref, 0, v_ref, vT_ref)


def project_rows(ids_ref, loc_ref, oth_ref, wa_ref, wb_ref, col, k_ref, kT_ref):
    def run(c):
        for d, rows in enumerate((loc_ref, oth_ref)):
            rs = slice((c ^ d) * HALF, (c ^ d) * HALF + HALF)
            for i, w in enumerate((wa_ref, wb_ref)):
                t = dot(rows[...], w[:, col : col + HI])
                cs = slice(i * HI, (i + 1) * HI)
                k_ref[rs, cs] = t.astype(BF)
                kT_ref[cs, rs] = t.T.astype(BF)

    per_core(ids_ref, run)


def norm(v):
    inv = lax.rsqrt(jnp.mean(v * v, axis=-1, keepdims=True) + EPSILON)
    return v * inv, inv


def cast_body(q_ref, k_ref, v_ref, o_ref, in_ref, out_ref, qk_ref, vo_ref, ff_ref):
    qk_ref[:, :HI] = q_ref[...].astype(BF)
    qk_ref[:, HI:] = k_ref[...].astype(BF)
    vo_ref[:, :HI] = v_ref[...].astype(BF)
    vo_ref[:, HI:] = o_ref[...].astype(BF)
    ff = in_ref.shape[1]
    ff_ref[:, :ff] = in_ref[...].astype(BF)
    ff_ref[:, ff:] = out_ref[...].astype(BF)


def prepare_body(
    x_ref, xo_ref, c_ref, co_ref, gain_ref,
    loc_ref, oth_ref, actT_ref, own_ref, cown_ref, crest_ref, cT_ref,
):
    for src, dst, cs in ((x_ref, loc_ref, slice(0, HALF)), (xo_ref, oth_ref, slice(HALF, SEQ))):
        act = norm(src[...].astype(F32))[0] * gain_ref[...]
        dst[...] = act.astype(BF)
        actT_ref[:, cs] = act.T.astype(BF)
    own_ref[:BLK, :] = x_ref[:BLK, :]
    own_ref[BLK:, :] = xo_ref[BLK:, :]
    for dst, a, b, at in ((cown_ref, c_ref, co_ref, 0), (crest_ref, co_ref, c_ref, HALF)):
        dst[:BLK, :] = a[:BLK, :]
        dst[BLK:, :] = b[BLK:, :]
        cT_ref[:, at : at + BLK] = a[:BLK, :].astype(F32).T.astype(BF)
        cT_ref[:, at + BLK : at + HALF] = b[BLK:, :].astype(F32).T.astype(BF)


def middle_body(x_ref, h_ref, wa_ref, wb_ref, gain_ref, mid_ref, act_ref, actT_ref):
    mid = x_ref[...].astype(F32) + dot_nt(h_ref[:, :HI], wa_ref[:, HI:]) + dot_nt(h_ref[:, HI:], wb_ref[:, HI:])
    act = norm(mid)[0] * gain_ref[...]
    mid_ref[...] = mid
    act_ref[...] = act.astype(BF)
    actT_ref[...] = act.T.astype(BF)


def emit(me, scr_ref, cols, keep_ref, send_ref, outer_x):
    for e in range(16):
        x, y, z = e & 1, (e >> 1) & 1, e >> 2
        if me is None:
            ref, at, row = (keep_ref, send_ref)[e >> 3], e & 7, e * 48
        else:
            first, second = (x, y) if outer_x else (y, x)
            ref, at = (keep_ref, send_ref)[first], second * 4 + z
            row = pl.multiple_of(lax.bitwise_xor(me, e) * 48, 16)
        ref[at, :, cols] = scr_ref[pl.ds(row, 48), cols].astype(BF)


def ffn_body(
    xor, ids_ref, aown_ref, aoth_ref, aTown_ref, aToth_ref, cown_ref, coth_ref, cT_ref,
    win_ref, wout_ref, outa_ref, outb_ref, gaa_ref, gab_ref, ka_ref, sa_ref, kb_ref, sb_ref,
    acco_ref, accg_ref, scr_ref,
):
    step = pl.program_id(0)
    last = pl.num_programs(0) - 1
    me = ids_ref[1] if xor else None

    @pl.when(step == 0)
    def _():
        acco_ref[...] = jnp.zeros_like(acco_ref)
        accg_ref[...] = jnp.zeros_like(accg_ref)

    win, wout = win_ref[...], wout_ref[...]
    hid, gpre = [], []
    for a_ref, c_ref, rs in ((aown_ref, cown_ref, slice(0, HALF)), (aoth_ref, coth_ref, slice(HALF, SEQ))):
        v = dot(a_ref[...], win)
        sq = v * v
        t = jnp.tanh(0.7978845608028654 * v * (1.0 + 0.044715 * sq))
        hidden = (0.5 * v * (1.0 + t)).astype(BF)
        slope = 0.5 * (1.0 + t) + 0.5 * v * (1.0 - t * t) * (
            0.7978845608028654 * (1.0 + 0.134145 * sq)
        )
        gh = dot(c_ref[...], wout).astype(BF).astype(F32)
        gp = (gh * slope).astype(BF)
        acco_ref[rs, :] += dot_nt(hidden, wout)
        accg_ref[rs, :] += dot_nt(gp, win)
        hid.append(hidden)
        gpre.append(gp)
    scr_ref[...] = dot(cT_ref[:, :HALF], hid[0]) + dot(cT_ref[:, HALF:], hid[1])
    emit(me, scr_ref, slice(0, FT), ka_ref, sa_ref, True)
    scr_ref[...] = dot(aTown_ref[...], gpre[0]) + dot(aToth_ref[...], gpre[1])
    emit(me, scr_ref, slice(0, FT), kb_ref, sb_ref, False)

    @pl.when(step == last)
    def _():
        outa_ref[...] = acco_ref[:HALF, :]
        outb_ref[...] = acco_ref[HALF:, :].astype(BF)
        gaa_ref[...] = accg_ref[:HALF, :]
        gab_ref[...] = accg_ref[HALF:, :].astype(BF)


def ffn(xor, ids, aown, aoth, aTown, aToth, cown, coth, cT, w):
    width = w.shape[1] // 2
    steps = width // FT
    tile = pl.BlockSpec((INNER, FT), lambda t: (0, t))
    tile2 = pl.BlockSpec((INNER, FT), lambda t: (0, t + steps))
    grad = pl.BlockSpec((8, 48, FT), lambda t: (0, 0, t))
    half, halfT = full((HALF, INNER)), full((INNER, HALF))
    return pl.pallas_call(
        lambda *r: ffn_body(xor, *r),
        grid=(steps,),
        in_specs=[smem(), half, half, halfT, halfT, half, half, full((INNER, SEQ)), tile, tile2],
        out_specs=[half, half, half, half, grad, grad, grad, grad],
        out_shape=[
            sds((HALF, INNER), F32), sds((HALF, INNER)), sds((HALF, INNER), F32), sds((HALF, INNER)),
        ] + [sds((8, 48, width))] * 4,
        scratch_shapes=[
            pltpu.VMEM((SEQ, INNER), F32), pltpu.VMEM((SEQ, INNER), F32), pltpu.VMEM((INNER, FT), F32),
        ],
        compiler_params=params(44),
        cost_estimate=cost(14.5e9, 20e6, 1.6e6),
        name="ffn",
    )(ids, aown, aoth, aTown, aToth, cown, coth, cT, w, w)


def middle_back_body(
    ga_ref, gr_ref, mid_ref, cot_ref, gain_ref, h_ref, wa_ref, wb_ref,
    stay_ref, sent_ref, gh_ref, ghT_ref, gain_out, gwa_ref, gwb_ref,
):
    ga = ga_ref[...] + gr_ref[...].astype(F32)
    normed, inv = norm(mid_ref[...])
    scaled = ga * gain_ref[...]
    gm = cot_ref[...].astype(F32) + inv * (
        scaled - normed * jnp.mean(scaled * normed, axis=-1, keepdims=True)
    )
    gain_out[...] = jnp.sum(ga * normed, axis=0, keepdims=True)
    stay_ref[...] = gm[:BLK]
    sent_ref[...] = gm[BLK:]
    grad = gm.astype(BF)
    gT = gm.T.astype(BF)
    for i, (w, gw) in enumerate(((wa_ref, gwa_ref), (wb_ref, gwb_ref))):
        cs = slice(i * HI, (i + 1) * HI)
        t = dot(grad, w[:, HI:])
        gh_ref[:, cs] = t.astype(BF)
        ghT_ref[cs, :] = t.T.astype(BF)
        gw[...] = dot(gT, h_ref[:, cs]).astype(BF)


def joined(own, got):
    a, b = own.astype(F32), got.astype(F32)
    return jnp.concatenate([a[:HALF] + b[HALF:], a[HALF:] + b[:HALF]], axis=0).astype(BF)


def grad_vo_body(xor, ids_ref, aT_ref, gv_ref, rv_ref, go_ref, ro_ref, gv_out, ka, sa, kb, sb, scr):
    me = ids_ref[1] if xor else None
    gv = joined(gv_ref[...], rv_ref[...])
    gv_out[...] = gv
    scr[...] = dot(aT_ref[...], gv)
    emit(me, scr, slice(0, HI), ka, sa, True)
    scr[...] = go_ref[...].astype(F32) + ro_ref[...].astype(F32)
    emit(me, scr, slice(0, HI), kb, sb, False)


def grad_qk_body(
    xor, ids_ref, aT_ref, gq_ref, rq_ref, gk_ref, rk_ref, gv_ref, qk_ref, vo_ref,
    loc_ref, oth_ref, ka, sa, kb, sb, scr,
):
    me = ids_ref[1] if xor else None
    gq, rq = gq_ref[...], rq_ref[...]
    gq = jnp.concatenate([gq[:BLK], rq[BLK:], rq[:BLK], gq[BLK:]], axis=0)
    scr[...] = dot(aT_ref[...], gq)
    emit(me, scr, slice(0, HI), ka, sa, True)
    gk = joined(gk_ref[...], rk_ref[...])
    scr[...] = dot(aT_ref[...], gk)
    emit(me, scr, slice(0, HI), kb, sb, False)
    for rs, ref in ((slice(0, HALF), loc_ref), (slice(HALF, SEQ), oth_ref)):
        t = dot_nt(gq[rs, :], qk_ref[:, :HI]) + dot_nt(gk[rs, :], qk_ref[:, HI:])
        ref[...] = (t + dot_nt(gv_ref[rs, :], vo_ref[:, :HI])).astype(ref.dtype)


def output_body(mid_ref, own_ref, got_ref, stay_ref, sent_ref):
    out = (mid_ref[...] + own_ref[...] + got_ref[...].astype(F32)).astype(BF)
    stay_ref[...] = out[:BLK]
    sent_ref[...] = out[BLK:]


def join_body(stay_ref, got_ref, out_ref):
    out_ref[:BLK, :] = stay_ref[...]
    out_ref[BLK:, :] = got_ref[...]


def tokens_back_body(
    ga_ref, gr_ref, x_ref, gain_ref, stay_ref, got_ref, gain2_ref, gpre_ref, gpost_ref,
    out_ref, small_ref,
):
    ga = ga_ref[...] + gr_ref[...].astype(F32)
    normed, inv = norm(x_ref[...].astype(F32))
    scaled = ga * gain_ref[...]
    back = inv * (scaled - normed * jnp.mean(scaled * normed, axis=-1, keepdims=True))
    out_ref[:BLK, :] = (stay_ref[...] + back[:BLK]).astype(BF)
    out_ref[BLK:, :] = (got_ref[...] + back[BLK:]).astype(BF)
    gain1 = jnp.sum(ga * normed, axis=0, keepdims=True)
    small_ref[...] = jnp.zeros_like(small_ref)
    for i in range(6):
        cs = slice(i * 128, (i + 1) * 128)
        small_ref[i : i + 1, :] = gain1[:, cs]
        small_ref[8 + i : 9 + i, :] = gain2_ref[:, cs]
    small_ref[16 : 16 + HEADS, :HEADS] = jnp.sum(gpre_ref[...], axis=-1)
    small_ref[32 : 32 + HEADS, :HEADS] = jnp.sum(gpost_ref[...], axis=-1)


def swap(v):
    return lax.ppermute(v, "tensor", [(0, 1), (1, 0)])


def hop(v, mask):
    n = lax.axis_size("dp")
    return lax.ppermute(v, "dp", [(i, i ^ mask) for i in range(n)])


def after(v, *done):
    return lax.optimization_barrier((v, *done))[0]


def place_body(ids_ref, ax, ay, bx, by, out):
    me = ids_ref[1]
    w = ax.shape[3]
    for t, ref in enumerate((ax, ay, bx, by)):
        col = (t // 2) * w
        for i in range(2):
            for j in range(4):
                e = 4 * j + ((2 * i + t) if t < 2 else (i + 2 * (t - 2)))
                row = pl.multiple_of(lax.bitwise_xor(me, e) * 48, 16)
                out[pl.ds(row, 48), col : col + w] = ref[i, j]


def gather_z(shard):
    return [shard] + [hop(shard, 4 * e) for e in range(1, 4)]


def gather_one(pieces):
    z = jnp.stack(pieces, axis=0)
    w = z.shape[2] // 2
    a, b = z[:, :, :w], z[:, :, w:]
    return a, hop(a, 2), b, hop(b, 1)


def gather_two(a, ra, b, rb):
    a2, b2 = jnp.stack([a, ra], axis=0), jnp.stack([b, rb], axis=0)
    return a2, hop(a2, 1), b2, hop(b2, 2)


def gathered(ids, parts):
    return once(place_body, (sds((768, 2 * parts[0].shape[3])),), (ids, *parts), "place")[0]


def fold_one_body(ka, ra, kb, rb, oka, osa, okb, osb):
    for k, r, keep, send in ((ka, ra, oka, osa), (kb, rb, okb, osb)):
        t = (k[...].astype(F32) + r[...].astype(F32)).astype(BF)
        keep[...] = t[:4]
        send[...] = t[4:]


def fold_two_body(ka, ra, kb, rb, own, *sends):
    w = ka.shape[2]
    for k, r, cs in ((ka, ra, slice(0, w)), (kb, rb, slice(w, 2 * w))):
        t = k[...].astype(F32) + r[...].astype(F32)
        own[:, cs] = t[0]
        for e in range(3):
            sends[e][:, cs] = t[e + 1].astype(BF)


def fold_one(ka, ra, kb, rb):
    piece = sds((4,) + ka.shape[1:])
    return once(fold_one_body, (piece,) * 4, (ka, ra, kb, rb), "fold_one", scalars=0)


def fold_two(*parts):
    w = 2 * parts[0].shape[2]
    outs = (sds((48, w), F32),) + (sds((48, w)),) * 3
    return once(fold_two_body, outs, parts, "fold_two", scalars=0)


def fold_ff_body(ka, ra, kb, rb, own, send):
    w = ka.shape[2]
    for k, r, cs in ((ka, ra, slice(0, w)), (kb, rb, slice(w, 2 * w))):
        t = (k[...].astype(F32) + r[...].astype(F32)).astype(BF)
        for z in range(2):
            own[z, :, cs] = t[2 * z]
            send[z, :, cs] = t[2 * z + 1]


def fold_at_body(*refs):
    ins, outs = refs[:8], refs[8:]
    for i in range(4):
        k, r = ins[2 * i], ins[2 * i + 1]
        kept, sent = outs[2 * (i // 2)], outs[2 * (i // 2) + 1]
        cs = slice((i % 2) * HI, (i % 2) * HI + HI)
        t = (k[...].astype(F32) + r[...].astype(F32)).astype(BF)
        kept[:, :, cs] = t[:4]
        sent[:, :, cs] = t[4:]


def fold_ff_two_body(own, got, keep, send):
    t = own[...].astype(F32) + got[...].astype(F32)
    keep[...] = t[0]
    send[...] = t[1].astype(BF)


def finish_ff_body(own, got, in_ref, out_ref):
    w = out_ref.shape[1]
    out_ref[...] = own[:, :w] + got[:, :w].astype(F32)
    in_ref[...] = own[:, w:] + got[:, w:].astype(F32)


def finish_body(own, a, b, c, *outs):
    for i, ref in enumerate(outs):
        cs = slice(i * HI, (i + 1) * HI)
        ref[...] = own[:, cs] + (a[:, cs].astype(F32) + b[:, cs].astype(F32) + c[:, cs].astype(F32))


def scatter_plain(ka, sa, kb, sb):
    w = ka.shape[2]
    flat = jnp.concatenate(
        [jnp.concatenate([k, s], axis=0).reshape(768, w) for k, s in ((ka, sa), (kb, sb))], axis=1
    )
    return lax.psum_scatter(flat.astype(F32), "dp", scatter_dimension=0, tiled=True)


def sum_all(v):
    n = lax.axis_size("dp")
    v = v + swap(v)
    bit = 1
    while bit < n:
        v = v + hop(v, bit)
        bit *= 2
    return v


def on_device(
    tokens, cotangent, segment_ids, norm1_gain, w_query, w_key, w_value, pre_mix, post_mix,
    w_output, norm2_gain, w_in, w_out,
):
    ids = jnp.stack([lax.axis_index("tensor"), lax.axis_index("dp")]).astype(jnp.int32)
    xor = lax.axis_size("dp") == 16
    low = lambda v: v.astype(BF)
    D = norm1_gain.shape[0]
    tie = lax.optimization_barrier
    gain1, gain2 = norm1_gain.reshape(1, D), norm2_gain.reshape(1, D)
    seg = segment_ids.reshape(1, SEQ)

    every = lambda v: lax.all_gather(v, "dp", axis=0, tiled=True)
    r, ff = w_in.shape
    shard_qk, shard_vo, shard_ff = once(
        cast_body, (sds((r, INNER)), sds((r, INNER)), sds((r, 2 * ff))),
        tuple(far(w) for w in (w_query, w_key, w_value, w_output.T, w_in, w_out.T)), "cast", scalars=0,
    )
    if xor:
        z_qk = gather_z(shard_qk)
    w_ff = every(shard_ff)
    x_oth, cot_oth = swap(tokens), swap(cotangent)
    act_loc, act_oth, actT, x_own, cot_own, cot_rest, cotT = once(
        prepare_body,
        (
            sds((HALF, D)), sds((HALF, D)), hbm((D, SEQ)), hbm((HALF, D)), hbm((HALF, D)),
            hbm((HALF, D)), hbm((D, SEQ)),
        ),
        (far(tokens), x_oth, far(cotangent), cot_oth, gain1), "prepare", scalars=0,
    )
    if xor:
        *z_qk, act_loc = tie((*z_qk, act_loc))
        a, ra, b, rb = gather_one(z_qk)
        z_vo = gather_z(after(shard_vo, *z_qk))
        qk_parts = gather_two(a, ra, b, rb)
        *z_vo, ax, ay, bx, by = tie((*z_vo, *qk_parts))
        a, ra, b, rb = gather_one(z_vo)
        w_qk = gathered(ids, (ax, ay, bx, by))
    else:
        w_qk, w_vo = every(shard_qk), every(shard_vo)
    q, qT, k, kT = once(
        project_qk_body,
        (hbm((HALF, INNER)), sds((INNER, HALF)), sds((SEQ, INNER)), hbm((INNER, SEQ))),
        (ids, act_loc, act_oth, w_qk, swap(w_qk)), "project_qk", flops=1.8e9,
    )
    if xor:
        ra, rb, k = tie((ra, rb, k))
        vo_parts = gather_two(a, ra, b, rb)
        k = after(k, vo_parts[0], vo_parts[2])
    pT = logits_softmax(ids, pre_mix, seg, k, qT)
    if xor:
        w_vo = gathered(ids, tie((*vo_parts, pT))[:4])
    vo_o = swap(w_vo)
    v, vT = once(
        project_v_body, (hbm((SEQ, INNER)), sds((INNER, SEQ))),
        (ids, act_loc, act_oth, w_vo, vo_o), "project_v", flops=1.2e9,
    )
    uT, heads = attend(ids, post_mix, vT, pT)
    mid, act2, act2T = once(
        middle_body, (hbm((HALF, D), F32), hbm((HALF, D)), hbm((D, HALF))),
        (x_own, heads, w_vo, vo_o, gain2), "middle", scalars=0, flops=6e8,
    )
    out_own, out_oth, ga_own, ga_oth, ka, sa, kb, sb = ffn(
        xor, ids, far(act2), far(swap(act2)), far(act2T), far(swap(act2T)), far(cot_own), far(cot_rest), far(cotT), far(w_ff)
    )
    if xor:
        ra, rb = hop(sa, 1), hop(sb, 2)
    stay, sent, gh, ghT, gain2_part, gwo, gwo_o = once(
        middle_back_body,
        (
            hbm((BLK, D), F32), hbm((BLK, D), F32), sds((HALF, INNER)), sds((INNER, HALF)),
            hbm((1, D), F32), sds((D, HI)), sds((D, HI)),
        ),
        (ga_own, swap(ga_oth), mid, cot_own, gain2, heads, w_vo, vo_o),
        "middle_back", scalars=0, flops=1.2e9,
    )
    got_sent, got_out = swap(sent), swap(out_oth)
    gL, gv, gv_o, gpost = attend_back(ids, post_mix, v, ghT, gh, pT, uT)
    grads = (sds((8, 48, HI)),) * 4
    if xor:
        gv, gv_o, got_sent, got_out = tie((gv, gv_o, got_sent, got_out))
    gv, *vo = once(
        lambda *r: grad_vo_body(xor, *r), (hbm((SEQ, HI)),) + grads,
        (ids, actT, gv, swap(gv_o), gwo, swap(gwo_o)), "grad_vo",
        scratch=[pltpu.VMEM((D, HI), F32)], flops=6e8,
    )
    if xor:
        vo_ka, vo_sa, vo_kb, vo_sb = vo
        ra, rb = tie((ra, rb, vo_sa))[:2]
        ff_ka, ff_sa, ff_kb, ff_sb = fold_one(ka, ra, kb, rb)
        ff_ra, ff_rb = hop(ff_sa, 2), hop(ff_sb, 1)
        vo_ra, vo_rb = hop(vo_sa, 1), hop(vo_sb, 2)
        gL = after(gL, ff_sa, vo_sa)
    gq, gq_o, gk, gk_o, gpre = scores_back(ids, pre_mix, kT, qT, q, gL)
    if xor:
        ff_ra, ff_rb, vo_ra, vo_rb, gq, gq_o, gk_o = tie((ff_ra, ff_rb, vo_ra, vo_rb, gq, gq_o, gk_o))
        wide = ff_ka.shape[2] * 2
        ff_own, ff_send = once(
            fold_ff_body, (sds((2, 48, wide)),) * 2, (ff_ka, ff_ra, ff_kb, ff_rb), "fold_ff", scalars=0
        )
        ff_got = hop(ff_send, 4)
        gq, gk = tie((gq, gk, ff_send))[:2]
    ga_loc, ga_oth, *qk = once(
        lambda *r: grad_qk_body(xor, *r), (sds((HALF, D), F32), sds((HALF, D))) + grads,
        (ids, actT, gq, swap(gq_o), gk, swap(gk_o), gv, w_qk, w_vo), "grad_qk",
        scratch=[pltpu.VMEM((D, HI), F32)], flops=3e9,
    )
    ga_got = swap(ga_oth)
    if xor:
        qk_ka, qk_sa, qk_kb, qk_sb = qk
        qk_ra, qk_rb = hop(qk_sa, 1), hop(qk_sb, 2)
        ff_own, ff_got = tie((ff_own, ff_got, qk_sa))[:2]
        ff_own, ff_send = once(
            fold_ff_two_body, (sds((48, wide), F32), sds((48, wide))), (ff_own, ff_got), "fold_ff_two", scalars=0,
            flops=3e9,
        )
        ff_got = hop(ff_send, 8)
        qk_ra, qk_rb, ff_two = tie((qk_ra, qk_rb, ff_send))
        at_ka, at_sa, at_kb, at_sb = once(
            fold_at_body, (sds((4, 48, INNER)),) * 4,
            (qk_ka, qk_ra, vo_ka, vo_ra, qk_kb, qk_rb, vo_kb, vo_rb), "fold_at", scalars=0,
        )
        at_ra, at_rb = hop(at_sa, 2), hop(at_sb, 1)
        ga_loc, ga_got = tie((ga_loc, ga_got, at_sa))[:2]
    grad_tokens, small = once(
        tokens_back_body, (sds((HALF, D)), sds((48, 128), F32)),
        (ga_loc, ga_got, tokens, gain1, stay, got_sent, gain2_part, gpre, gpost),
        "tokens_back", scalars=0,
    )
    r = w_in.shape[0]
    part = sds((r, HI), F32)
    if xor:
        got = swap(small)
        mid, small = tie((mid, small))
        out_stay, out_sent = once(
            output_body, (sds((BLK, D)), sds((BLK, D))), (mid, out_own, got_out), "output", scalars=0
        )
        out_got = swap(out_sent)
        small, got = tie((small, got, out_sent))[:2]
        small = small + got
        small = small + hop(small, 1)
        got = hop(small, 2)
        at_ra, at_rb, got, small, ff_got = tie((at_ra, at_rb, got, small, ff_got))
        at, *sends = fold_two(at_ka, at_ra, at_kb, at_rb)
        gots = [hop(sends[e], 4 * (e + 1)) for e in range(3)]
        small, got, out_got = tie((small, got, out_got, at))[:3]
        (output,) = once(join_body, (sds((HALF, D)),), (out_stay, out_got), "join", scalars=0)
        small = small + got
        small = small + hop(small, 4)
        small = small + hop(small, 8)
        grad_in, grad_out = once(
            finish_ff_body, (sds((r, ff), F32),) * 2, (ff_own, ff_got), "finish_ff", scalars=0
        )
        grad_q, grad_v, grad_k, grad_o = once(
            finish_body, (part,) * 4, (at, *gots), "finish", scalars=0
        )
    else:
        grad_qk, grad_vo = scatter_plain(*qk), scatter_plain(*vo)
        grad_ffn = scatter_plain(ka, sa, kb, sb)
        grad_q, grad_k, grad_v, grad_o = grad_qk[:, :HI], grad_qk[:, HI:], grad_vo[:, :HI], grad_vo[:, HI:]
        grad_in, grad_out = grad_ffn[:, ff:], grad_ffn[:, :ff]
        small = sum_all(small)
        out_stay, out_sent = once(
            output_body, (sds((BLK, D)), sds((BLK, D))), (mid, out_own, got_out), "output", scalars=0
        )
        output = jnp.concatenate([out_stay, swap(out_sent)], axis=0)
    return (
        output, grad_tokens, small[:6].reshape(D), grad_q, grad_k, grad_v,
        small[16 : 16 + HEADS, :HEADS], small[32 : 32 + HEADS, :HEADS].T,
        grad_o.T, small[8:14].reshape(D), grad_in, grad_out.T,
    )


def solution(mesh):
    rows = P(("dp", "tensor"), None)
    w, wt = P("dp", "tensor"), P("tensor", "dp")
    return jax.shard_map(
        on_device,
        mesh=mesh,
        in_specs=(rows, rows, P("dp"), P(), w, w, w, P(), P(), wt, P(), w, wt),
        out_specs=(rows, rows, P(), w, w, w, P(), P(), wt, P(), w, wt),
        check_vma=False,
    )
```

```python
import math

import jax
import jax.numpy as jnp
from jax import lax
from jax.experimental import pallas as pl
from jax.experimental.pallas import tpu as pltpu
from jax.sharding import PartitionSpec as P

HEADS = 12
HD = 64
INNER = 768
HI = INNER // 2
SEQ = 1024
HALF = SEQ // 2
BLK = 256
EPSILON = 1e-06
LOG2E = 1.4426950408889634
BF = jnp.bfloat16
F32 = jnp.float32
HB1, HB2, HB3, HB4 = 3, 3, 3, 3
FT = 512


def dot(a, b):
    return jnp.dot(a, b, preferred_element_type=F32)


def dot_nt(a, b):
    return lax.dot_general(a, b, (((1,), (1,)), ((), ())), preferred_element_type=F32)


def smem():
    return pl.BlockSpec(memory_space=pltpu.SMEM)


def whole():
    return pl.BlockSpec(memory_space=pltpu.VMEM)


def full(s):
    return pl.BlockSpec(s, lambda *i: (0,) * len(s))


def params(mib=24):
    return pltpu.CompilerParams(vmem_limit_bytes=mib * 1024 * 1024)


def cost(flops, moved, exps=0):
    return pl.CostEstimate(flops=int(flops), bytes_accessed=int(moved), transcendentals=int(exps))


def sds(shape, dtype=BF):
    return jax.ShapeDtypeStruct(shape, dtype)


def once(body, outs, args, name, scalars=1, scratch=(), flops=0, moved=None):
    if moved is None:
        moved = sum(math.prod(a.shape) * a.dtype.itemsize for a in (*args, *outs))
    return pl.pallas_call(
        body,
        in_specs=[smem()] * scalars + [whole()] * (len(args) - scalars),
        out_specs=[whole()] * len(outs),
        out_shape=list(outs),
        scratch_shapes=list(scratch),
        compiler_params=params(),
        cost_estimate=cost(flops, moved),
        name=name,
    )(*args)


def per_core(ids_ref, run):
    for c in range(2):
        pl.when(ids_ref[0] == c)(lambda c=c: run(c))


def head(c, i):
    return (i + c * (HEADS // 2)) % HEADS


def spread(rep_ref, row, values):
    for g, value in enumerate(values):
        rep_ref[row : row + 1, g * HD : (g + 1) * HD] = jnp.full((1, HD), value, F32)


def hbm(shape, dtype=BF):
    return pltpu.HBM(shape, dtype)


def far(v):
    return pltpu.with_memory_space_constraint(v, pltpu.HBM)


def chunks(c):
    return (1, 4) if c == 0 else (3, 2)


def blocks_of(c):
    return (0, 3) if c == 0 else (2, 1)


def logits_body(ids_ref, pre_ref, seg_ref, k_ref, qT_ref, pT_ref, mask_ref):
    step = pl.program_id(0)

    def run(c):
        nj, bl = chunks(c), blocks_of(c)
        base = (0, nj[0] * BLK)

        @pl.when(step == 0)
        def _():
            seg = seg_ref[...].astype(F32)
            down = jnp.broadcast_to(seg, (8, SEQ)).T[:, :1]
            for b in range(2):
                qpos = lax.broadcasted_iota(jnp.int32, (BLK, BLK), 1) + bl[b] * BLK
                qseg = seg[:, bl[b] * BLK : (bl[b] + 1) * BLK]
                for j in range(nj[b]):
                    kpos = lax.broadcasted_iota(jnp.int32, (BLK, BLK), 0) + j * BLK
                    ok = (kpos <= qpos) & (down[j * BLK : (j + 1) * BLK] == qseg)
                    at = base[b] + j * BLK
                    mask_ref[at : at + BLK, :] = jnp.where(ok, 0.0, -1e30)

        for hh in range(HB1):
            h = step * HB1 + hh
            scale = [pre_ref[h, head(c, g)] * (0.125 * LOG2E) for g in range(HEADS)]
            for b in range(2):
                n = nj[b] * BLK
                qs = jnp.concatenate(
                    [
                        (
                            qT_ref[g * HD : (g + 1) * HD, b * BLK : (b + 1) * BLK].astype(F32)
                            * scale[g]
                        ).astype(BF)
                        for g in range(HEADS)
                    ],
                    axis=0,
                )
                s = dot(k_ref[:n, :], qs) + mask_ref[base[b] : base[b] + n, :]
                m = jnp.max(s, axis=0, keepdims=True)
                e = jnp.exp2(s - m)
                inv = 1.0 / jnp.sum(e, axis=0, keepdims=True)
                pT_ref[base[b] : base[b] + n, hh * BLK : (hh + 1) * BLK] = (e * inv).astype(BF)

    per_core(ids_ref, run)


def logits_softmax(ids, pre, seg, k, qT):
    return pl.pallas_call(
        logits_body,
        grid=(HEADS // HB1,),
        in_specs=[smem(), smem(), full((1, SEQ)), full((SEQ, INNER)), full((INNER, HALF))],
        out_specs=pl.BlockSpec((5 * BLK, HB1 * BLK), lambda h: (0, h)),
        out_shape=hbm((5 * BLK, HEADS * BLK)),
        scratch_shapes=[pltpu.VMEM((5 * BLK, BLK), F32)],
        compiler_params=params(),
        cost_estimate=cost(6.04e9, 10e6, 4e6),
        name="logits_softmax",
    )(ids, pre, seg, k, qT)


def attend_body(ids_ref, post_ref, vT_ref, pT_ref, uT_ref, h_ref, acc_ref):
    step = pl.program_id(0)

    def run(c):
        nj = chunks(c)
        base = (0, nj[0] * BLK)
        for b in range(2):
            n = nj[b] * BLK
            cs = slice(b * BLK, (b + 1) * BLK)
            us = []
            for hh in range(HB2):
                u = dot(vT_ref[:, :n], pT_ref[base[b] : base[b] + n, hh * BLK : (hh + 1) * BLK])
                uT_ref[hh * INNER : (hh + 1) * INNER, cs] = u.astype(BF)
                us.append(u)
            for k in range(HEADS):
                rs = slice(k * HD, (k + 1) * HD)
                t = us[0][rs, :] * post_ref[head(c, k), step * HB2]
                for hh in range(1, HB2):
                    t = t + us[hh][rs, :] * post_ref[head(c, k), step * HB2 + hh]
                acc_ref[rs, cs] += t

    @pl.when(step == 0)
    def _():
        acc_ref[...] = jnp.zeros_like(acc_ref)

    per_core(ids_ref, run)

    @pl.when(step == HEADS // HB2 - 1)
    def _():
        h_ref[...] = acc_ref[...].T.astype(BF)


def attend(ids, post, vT, pT):
    return pl.pallas_call(
        attend_body,
        grid=(HEADS // HB2,),
        in_specs=[smem(), smem(), full((INNER, SEQ)), pl.BlockSpec((5 * BLK, HB2 * BLK), lambda h: (0, h))],
        out_specs=[pl.BlockSpec((HB2 * INNER, HALF), lambda h: (h, 0)), full((HALF, INNER))],
        out_shape=[hbm((HEADS * INNER, HALF)), sds((HALF, INNER))],
        scratch_shapes=[pltpu.VMEM((INNER, HALF), F32)],
        compiler_params=params(),
        cost_estimate=cost(6.04e9, 20e6),
        name="attend",
    )(ids, post, vT, far(pT))


def split_rows(c, acc_ref, own_ref, oth_ref):
    for d in range(2):
        src = slice((c ^ d) * HALF, (c ^ d) * HALF + HALF)
        dst = slice(d * HALF, (d + 1) * HALF)
        own_ref[dst, :] = acc_ref[src, :HI].astype(BF)
        oth_ref[dst, :] = acc_ref[src, HI:].astype(BF)


def keep_sum(ref, h, k, b, g):
    g = g[:, :128] + g[:, 128:]
    ref[h, k : k + 1, :] = g if b == 0 else ref[h, k : k + 1, :] + g


def attend_back_body(
    ids_ref, post_ref, v_ref, ghT_ref, gh_ref, pT_ref, uT_ref,
    gL_ref, own_ref, oth_ref, gpost_ref, acc_ref, rep_ref,
):
    step = pl.program_id(0)

    def run(c):
        nj = chunks(c)
        base = (0, nj[0] * BLK)
        for hh in range(HB3):
            spread(rep_ref, hh, [post_ref[head(c, k), step * HB3 + hh] for k in range(HEADS)])
        for b in range(2):
            n = nj[b] * BLK
            cs = slice(b * BLK, (b + 1) * BLK)
            g2s = []
            for hh in range(HB3):
                h = step * HB3 + hh
                hs = slice(hh * BLK, (hh + 1) * BLK)
                r = jnp.zeros((1, BLK), F32)
                parts = []
                for k in range(HEADS):
                    gk = ghT_ref[k * HD : (k + 1) * HD, cs].astype(F32)
                    u = uT_ref[hh * INNER + k * HD : hh * INNER + (k + 1) * HD, cs].astype(F32)
                    g = jnp.sum(gk * u, axis=0, keepdims=True)
                    w = post_ref[head(c, k), h]
                    keep_sum(gpost_ref, hh, head(c, k), b, g)
                    r = r + g * w
                    parts.append((gk * w).astype(BF))
                gP = dot(v_ref[:n, :], jnp.concatenate(parts, axis=0))
                p = pT_ref[base[b] : base[b] + n, hs]
                gL_ref[base[b] : base[b] + n, hs] = (p.astype(F32) * (gP - r)).astype(BF)
                g2s.append((gh_ref[cs, :].astype(F32) * rep_ref[hh : hh + 1, :]).astype(BF))
            acc_ref[:n, :] += dot(pT_ref[base[b] : base[b] + n, :], jnp.concatenate(g2s, axis=0))

        @pl.when(step == HEADS // HB3 - 1)
        def _():
            split_rows(c, acc_ref, own_ref, oth_ref)

    @pl.when(step == 0)
    def _():
        acc_ref[...] = jnp.zeros_like(acc_ref)

    per_core(ids_ref, run)


def attend_back(ids, post, v, ghT, gh, pT, uT):
    return pl.pallas_call(
        attend_back_body,
        grid=(HEADS // HB3,),
        in_specs=[
            smem(), smem(), full((SEQ, INNER)), full((INNER, HALF)), full((HALF, INNER)),
            pl.BlockSpec((5 * BLK, HB3 * BLK), lambda h: (0, h)),
            pl.BlockSpec((HB3 * INNER, HALF), lambda h: (h, 0)),
        ],
        out_specs=[
            pl.BlockSpec((5 * BLK, HB3 * BLK), lambda h: (0, h)),
            full((SEQ, HI)), full((SEQ, HI)),
            pl.BlockSpec((HB3, HEADS, 128), lambda h: (h, 0, 0)),
        ],
        out_shape=[
            hbm((5 * BLK, HEADS * BLK)), sds((SEQ, HI)), sds((SEQ, HI)),
            hbm((HEADS, HEADS, 128), F32),
        ],
        scratch_shapes=[pltpu.VMEM((SEQ, INNER), F32), pltpu.VMEM((8, INNER), F32)],
        compiler_params=params(),
        cost_estimate=cost(12.1e9, 30e6),
        name="attend_back",
    )(ids, post, v, ghT, gh, far(pT), far(uT))


def scores_back_body(
    ids_ref, pre_ref, kT_ref, qT_ref, q_ref, gL_ref,
    gqa_ref, gqb_ref, own_ref, oth_ref, gpre_ref, accq_ref, acck_ref, rep_ref,
):
    step = pl.program_id(0)

    def run(c):
        nj = chunks(c)
        base = (0, nj[0] * BLK)
        scale = [
            [pre_ref[step * HB4 + hh, head(c, g)] * 0.125 for g in range(HEADS)] for hh in range(HB4)
        ]
        for hh in range(HB4):
            spread(rep_ref, hh, scale[hh])
        for b in range(2):
            n = nj[b] * BLK
            cs = slice(b * BLK, (b + 1) * BLK)
            ws, q2s = [], []
            for hh in range(HB4):
                ws.append(dot(kT_ref[:, :n], gL_ref[base[b] : base[b] + n, hh * BLK : (hh + 1) * BLK]))
                q2s.append((q_ref[cs, :].astype(F32) * rep_ref[hh : hh + 1, :]).astype(BF))
            for k in range(HEADS):
                rs = slice(k * HD, (k + 1) * HD)
                qk = qT_ref[rs, cs].astype(F32)
                t = None
                for hh in range(HB4):
                    w = ws[hh][rs, :]
                    g = jnp.sum(qk * w, axis=0, keepdims=True) * 0.125
                    keep_sum(gpre_ref, hh, head(c, k), b, g)
                    u = w * scale[hh][k]
                    t = u if t is None else t + u
                accq_ref[rs, cs] += t
            acck_ref[:n, :] += dot(gL_ref[base[b] : base[b] + n, :], jnp.concatenate(q2s, axis=0))

        @pl.when(step == HEADS // HB4 - 1)
        def _():
            split_rows(c, acck_ref, own_ref, oth_ref)

    @pl.when(step == 0)
    def _():
        accq_ref[...] = jnp.zeros_like(accq_ref)
        acck_ref[...] = jnp.zeros_like(acck_ref)

    per_core(ids_ref, run)

    @pl.when(step == HEADS // HB4 - 1)
    def _():
        gqa_ref[...] = accq_ref[:HI, :].T.astype(BF)
        gqb_ref[...] = accq_ref[HI:, :].T.astype(BF)


def scores_back(ids, pre, kT, qT, q, gL):
    return pl.pallas_call(
        scores_back_body,
        grid=(HEADS // HB4,),
        in_specs=[
            smem(), smem(), full((INNER, SEQ)), full((INNER, HALF)), full((HALF, INNER)),
            pl.BlockSpec((5 * BLK, HB4 * BLK), lambda h: (0, h)),
        ],
        out_specs=[
            full((HALF, HI)), full((HALF, HI)), full((SEQ, HI)), full((SEQ, HI)),
            pl.BlockSpec((HB4, HEADS, 128), lambda h: (h, 0, 0)),
        ],
        out_shape=[
            sds((HALF, HI)), sds((HALF, HI)), sds((SEQ, HI)), sds((SEQ, HI)),
            sds((HEADS, HEADS, 128), F32),
        ],
        scratch_shapes=[
            pltpu.VMEM((INNER, HALF), F32), pltpu.VMEM((SEQ, INNER), F32), pltpu.VMEM((8, INNER), F32),
        ],
        compiler_params=params(),
        cost_estimate=cost(12.1e9, 14e6),
        name="scores_back",
    )(ids, pre, kT, qT, q, far(gL))


def own_rows(loc, oth):
    return jnp.concatenate([loc[:BLK], oth[BLK:]], axis=0)


def project_qk_body(ids_ref, loc_ref, oth_ref, wa_ref, wb_ref, q_ref, qT_ref, k_ref, kT_ref):
    own = own_rows(loc_ref[...], oth_ref[...])
    for i, w in enumerate((wa_ref, wb_ref)):
        t = dot(own, w[:, :HI])
        cs = slice(i * HI, (i + 1) * HI)
        q_ref[:, cs] = t.astype(BF)
        qT_ref[cs, :] = t.T.astype(BF)
    project_rows(ids_ref, loc_ref, oth_ref, wa_ref, wb_ref, HI, k_ref, kT_ref)


def project_v_body(ids_ref, loc_ref, oth_ref, wa_ref, wb_ref, v_ref, vT_ref):
    project_rows(ids_ref, loc_ref, oth_ref, wa_ref, wb_ref, 0, v_ref, vT_ref)


def project_rows(ids_ref, loc_ref, oth_ref, wa_ref, wb_ref, col, k_ref, kT_ref):
    def run(c):
        for d, rows in enumerate((loc_ref, oth_ref)):
            rs = slice((c ^ d) * HALF, (c ^ d) * HALF + HALF)
            for i, w in enumerate((wa_ref, wb_ref)):
                t = dot(rows[...], w[:, col : col + HI])
                cs = slice(i * HI, (i + 1) * HI)
                k_ref[rs, cs] = t.astype(BF)
                kT_ref[cs, rs] = t.T.astype(BF)

    per_core(ids_ref, run)


def norm(v):
    inv = lax.rsqrt(jnp.mean(v * v, axis=-1, keepdims=True) + EPSILON)
    return v * inv, inv


def cast_body(q_ref, k_ref, v_ref, o_ref, in_ref, out_ref, qk_ref, vo_ref, ff_ref):
    qk_ref[:, :HI] = q_ref[...].astype(BF)
    qk_ref[:, HI:] = k_ref[...].astype(BF)
    vo_ref[:, :HI] = v_ref[...].astype(BF)
    vo_ref[:, HI:] = o_ref[...].astype(BF)
    ff = in_ref.shape[1]
    ff_ref[:, :ff] = in_ref[...].astype(BF)
    ff_ref[:, ff:] = out_ref[...].astype(BF)


def prepare_body(
    x_ref, xo_ref, c_ref, co_ref, gain_ref,
    loc_ref, oth_ref, actT_ref, own_ref, cown_ref, crest_ref, cT_ref,
):
    for src, dst, cs in ((x_ref, loc_ref, slice(0, HALF)), (xo_ref, oth_ref, slice(HALF, SEQ))):
        act = norm(src[...].astype(F32))[0] * gain_ref[...]
        dst[...] = act.astype(BF)
        actT_ref[:, cs] = act.T.astype(BF)
    own_ref[:BLK, :] = x_ref[:BLK, :]
    own_ref[BLK:, :] = xo_ref[BLK:, :]
    for dst, a, b, at in ((cown_ref, c_ref, co_ref, 0), (crest_ref, co_ref, c_ref, HALF)):
        dst[:BLK, :] = a[:BLK, :]
        dst[BLK:, :] = b[BLK:, :]
        cT_ref[:, at : at + BLK] = a[:BLK, :].astype(F32).T.astype(BF)
        cT_ref[:, at + BLK : at + HALF] = b[BLK:, :].astype(F32).T.astype(BF)


def middle_body(x_ref, h_ref, wa_ref, wb_ref, gain_ref, mid_ref, act_ref, actT_ref):
    mid = x_ref[...].astype(F32) + dot_nt(h_ref[:, :HI], wa_ref[:, HI:]) + dot_nt(h_ref[:, HI:], wb_ref[:, HI:])
    act = norm(mid)[0] * gain_ref[...]
    mid_ref[...] = mid
    act_ref[...] = act.astype(BF)
    actT_ref[...] = act.T.astype(BF)


def emit(me, scr_ref, cols, keep_ref, send_ref, outer_x):
    for e in range(16):
        x, y, z = e & 1, (e >> 1) & 1, e >> 2
        if me is None:
            ref, at, row = (keep_ref, send_ref)[e >> 3], e & 7, e * 48
        else:
            first, second = (x, y) if outer_x else (y, x)
            ref, at = (keep_ref, send_ref)[first], second * 4 + z
            row = pl.multiple_of(lax.bitwise_xor(me, e) * 48, 16)
        ref[at, :, cols] = scr_ref[pl.ds(row, 48), cols].astype(BF)


def gates(v):
    sq = v * v
    s = 0.5 * jnp.tanh(v * (0.7978845608028654 + 0.035677408136300125 * sq)) + 0.5
    slope = s + v * (1.5957691216057308 + 0.21406444881780075 * sq) * (s - s * s)
    return (v * s).astype(BF), slope


def ffn_body(
    xor, ids_ref, aown_ref, aoth_ref, aTown_ref, aToth_ref, cown_ref, coth_ref, cT_ref,
    win_ref, wout_ref, outa_ref, outb_ref, gaa_ref, gab_ref, ka_ref, sa_ref, kb_ref, sb_ref,
    acco_ref, accg_ref, scr_ref,
):
    step = pl.program_id(0)
    last = pl.num_programs(0) - 1
    me = ids_ref[1] if xor else None

    @pl.when(step == 0)
    def _():
        acco_ref[...] = jnp.zeros_like(acco_ref)
        accg_ref[...] = jnp.zeros_like(accg_ref)

    win, wout = win_ref[...], wout_ref[...]
    v0, v1 = dot(aown_ref[...], win), dot(aoth_ref[...], win)
    h0, s0 = gates(v0)
    g0 = dot(cown_ref[...], wout)
    h1, s1 = gates(v1)
    g1 = dot(coth_ref[...], wout)
    acco_ref[:HALF, :] += dot_nt(h0, wout)
    p0 = (g0.astype(BF).astype(F32) * s0).astype(BF)
    acco_ref[HALF:, :] += dot_nt(h1, wout)
    p1 = (g1.astype(BF).astype(F32) * s1).astype(BF)
    accg_ref[:HALF, :] += dot_nt(p0, win)
    accg_ref[HALF:, :] += dot_nt(p1, win)
    hid, gpre = (h0, h1), (p0, p1)
    scr_ref[...] = dot(cT_ref[:, :HALF], hid[0]) + dot(cT_ref[:, HALF:], hid[1])
    emit(me, scr_ref, slice(0, FT), ka_ref, sa_ref, True)
    scr_ref[...] = dot(aTown_ref[...], gpre[0]) + dot(aToth_ref[...], gpre[1])
    emit(me, scr_ref, slice(0, FT), kb_ref, sb_ref, False)

    @pl.when(step == last)
    def _():
        outa_ref[...] = acco_ref[:HALF, :]
        outb_ref[...] = acco_ref[HALF:, :].astype(BF)
        gaa_ref[...] = accg_ref[:HALF, :]
        gab_ref[...] = accg_ref[HALF:, :].astype(BF)


def ffn(xor, ids, aown, aoth, aTown, aToth, cown, coth, cT, w):
    width = w.shape[1] // 2
    steps = width // FT
    tile = pl.BlockSpec((INNER, FT), lambda t: (0, t))
    tile2 = pl.BlockSpec((INNER, FT), lambda t: (0, t + steps))
    grad = pl.BlockSpec((8, 48, FT), lambda t: (0, 0, t))
    half, halfT = full((HALF, INNER)), full((INNER, HALF))
    return pl.pallas_call(
        lambda *r: ffn_body(xor, *r),
        grid=(steps,),
        in_specs=[smem(), half, half, halfT, halfT, half, half, full((INNER, SEQ)), tile, tile2],
        out_specs=[half, half, half, half, grad, grad, grad, grad],
        out_shape=[
            sds((HALF, INNER), F32), sds((HALF, INNER)), sds((HALF, INNER), F32), sds((HALF, INNER)),
        ] + [sds((8, 48, width))] * 4,
        scratch_shapes=[
            pltpu.VMEM((SEQ, INNER), F32), pltpu.VMEM((SEQ, INNER), F32), pltpu.VMEM((INNER, FT), F32),
        ],
        compiler_params=params(44),
        cost_estimate=cost(14.5e9, 20e6, 1.6e6),
        name="ffn",
    )(ids, aown, aoth, aTown, aToth, cown, coth, cT, w, w)


def middle_back_body(
    ga_ref, gr_ref, mid_ref, cot_ref, gain_ref, h_ref, wa_ref, wb_ref,
    stay_ref, sent_ref, gh_ref, ghT_ref, gain_out, gwa_ref, gwb_ref,
):
    ga = ga_ref[...] + gr_ref[...].astype(F32)
    normed, inv = norm(mid_ref[...])
    scaled = ga * gain_ref[...]
    gm = cot_ref[...].astype(F32) + inv * (
        scaled - normed * jnp.mean(scaled * normed, axis=-1, keepdims=True)
    )
    gain_out[...] = jnp.sum(ga * normed, axis=0, keepdims=True)
    stay_ref[...] = gm[:BLK]
    sent_ref[...] = gm[BLK:]
    grad = gm.astype(BF)
    gT = gm.T.astype(BF)
    for i, (w, gw) in enumerate(((wa_ref, gwa_ref), (wb_ref, gwb_ref))):
        cs = slice(i * HI, (i + 1) * HI)
        t = dot(grad, w[:, HI:])
        gh_ref[:, cs] = t.astype(BF)
        ghT_ref[cs, :] = t.T.astype(BF)
        gw[...] = dot(gT, h_ref[:, cs]).astype(BF)


def joined(own, got):
    a, b = own.astype(F32), got.astype(F32)
    return jnp.concatenate([a[:HALF] + b[HALF:], a[HALF:] + b[:HALF]], axis=0).astype(BF)


def grad_vo_body(xor, ids_ref, aT_ref, gv_ref, rv_ref, go_ref, ro_ref, gv_out, ka, sa, kb, sb, scr):
    me = ids_ref[1] if xor else None
    gv = joined(gv_ref[...], rv_ref[...])
    gv_out[...] = gv
    scr[...] = dot(aT_ref[...], gv)
    emit(me, scr, slice(0, HI), ka, sa, True)
    scr[...] = go_ref[...].astype(F32) + ro_ref[...].astype(F32)
    emit(me, scr, slice(0, HI), kb, sb, False)


def grad_qk_body(xor, ids_ref, aT_ref, gq_ref, rq_ref, gk_ref, rk_ref, gq_out, gk_out, ka, sa, kb, sb, scr):
    me = ids_ref[1] if xor else None
    gq, rq = gq_ref[...], rq_ref[...]
    gq = jnp.concatenate([gq[:BLK], rq[BLK:], rq[:BLK], gq[BLK:]], axis=0)
    gq_out[...] = gq
    scr[...] = dot(aT_ref[...], gq)
    emit(me, scr, slice(0, HI), ka, sa, True)
    gk = joined(gk_ref[...], rk_ref[...])
    gk_out[...] = gk
    scr[...] = dot(aT_ref[...], gk)
    emit(me, scr, slice(0, HI), kb, sb, False)


def act_back_body(gq_ref, gk_ref, gv_ref, qk_ref, vo_ref, loc_ref, oth_ref):
    for rs, ref in ((slice(0, HALF), loc_ref), (slice(HALF, SEQ), oth_ref)):
        t = dot_nt(gq_ref[rs, :], qk_ref[:, :HI]) + dot_nt(gk_ref[rs, :], qk_ref[:, HI:])
        ref[...] = (t + dot_nt(gv_ref[rs, :], vo_ref[:, :HI])).astype(ref.dtype)


def output_body(mid_ref, own_ref, got_ref, stay_ref, sent_ref):
    out = (mid_ref[...] + own_ref[...] + got_ref[...].astype(F32)).astype(BF)
    stay_ref[...] = out[:BLK]
    sent_ref[...] = out[BLK:]


def join_body(stay_ref, got_ref, out_ref):
    out_ref[:BLK, :] = stay_ref[...]
    out_ref[BLK:, :] = got_ref[...]


def tokens_back_body(
    ga_ref, gr_ref, x_ref, gain_ref, stay_ref, got_ref, gain2_ref, gpre_ref, gpost_ref,
    out_ref, small_ref,
):
    ga = ga_ref[...] + gr_ref[...].astype(F32)
    normed, inv = norm(x_ref[...].astype(F32))
    scaled = ga * gain_ref[...]
    back = inv * (scaled - normed * jnp.mean(scaled * normed, axis=-1, keepdims=True))
    out_ref[:BLK, :] = (stay_ref[...] + back[:BLK]).astype(BF)
    out_ref[BLK:, :] = (got_ref[...] + back[BLK:]).astype(BF)
    gain1 = jnp.sum(ga * normed, axis=0, keepdims=True)
    small_ref[...] = jnp.zeros_like(small_ref)
    for i in range(6):
        cs = slice(i * 128, (i + 1) * 128)
        small_ref[i : i + 1, :] = gain1[:, cs]
        small_ref[8 + i : 9 + i, :] = gain2_ref[:, cs]
    small_ref[16 : 16 + HEADS, :HEADS] = jnp.sum(gpre_ref[...], axis=-1)
    small_ref[32 : 32 + HEADS, :HEADS] = jnp.sum(gpost_ref[...], axis=-1)


def swap(v):
    return lax.ppermute(v, "tensor", [(0, 1), (1, 0)])


def hop(v, mask):
    n = lax.axis_size("dp")
    return lax.ppermute(v, "dp", [(i, i ^ mask) for i in range(n)])


def after(v, *done):
    return lax.optimization_barrier((v, *done))[0]


def place_body(ids_ref, ax, ay, bx, by, out):
    me = ids_ref[1]
    w = ax.shape[3]
    for t, ref in enumerate((ax, ay, bx, by)):
        col = (t // 2) * w
        for i in range(2):
            for j in range(4):
                e = 4 * j + ((2 * i + t) if t < 2 else (i + 2 * (t - 2)))
                row = pl.multiple_of(lax.bitwise_xor(me, e) * 48, 16)
                out[pl.ds(row, 48), col : col + w] = ref[i, j]


def gather_z(shard):
    return [shard] + [hop(shard, 4 * e) for e in range(1, 4)]


def gather_one(pieces):
    z = jnp.stack(pieces, axis=0)
    w = z.shape[2] // 2
    a, b = z[:, :, :w], z[:, :, w:]
    return a, hop(a, 2), b, hop(b, 1)


def gather_two(a, ra, b, rb):
    a2, b2 = jnp.stack([a, ra], axis=0), jnp.stack([b, rb], axis=0)
    return a2, hop(a2, 1), b2, hop(b2, 2)


def gathered(ids, parts):
    return once(place_body, (sds((768, 2 * parts[0].shape[3])),), (ids, *parts), "place")[0]


def fold_one_body(ka, ra, kb, rb, oka, osa, okb, osb):
    for k, r, keep, send in ((ka, ra, oka, osa), (kb, rb, okb, osb)):
        t = (k[...].astype(F32) + r[...].astype(F32)).astype(BF)
        keep[...] = t[:4]
        send[...] = t[4:]


def fold_two_body(ka, ra, kb, rb, small, got, own, total, *sends):
    w = ka.shape[2]
    for k, r, cs in ((ka, ra, slice(0, w)), (kb, rb, slice(w, 2 * w))):
        t = k[...].astype(F32) + r[...].astype(F32)
        own[:, cs] = t[0]
        for e in range(3):
            sends[e][:, cs] = t[e + 1].astype(BF)
    v = small[...] + got[...]
    total[...] = v
    high = v.astype(BF)
    low = (v - high.astype(F32)).astype(BF)
    for send in sends:
        send[:, 2 * w : 2 * w + 128] = high
        send[:, 2 * w + 128 :] = low


def fold_one(ka, ra, kb, rb):
    piece = sds((4,) + ka.shape[1:])
    return once(fold_one_body, (piece,) * 4, (ka, ra, kb, rb), "fold_one", scalars=0)


def fold_two(*parts):
    w = 2 * parts[0].shape[2]
    outs = (sds((48, w), F32), sds((48, 128), F32)) + (sds((48, w + 256)),) * 3
    return once(fold_two_body, outs, parts, "fold_two", scalars=0)


def fold_ff_body(ka, ra, kb, rb, own, send):
    w = ka.shape[2]
    for k, r, cs in ((ka, ra, slice(0, w)), (kb, rb, slice(w, 2 * w))):
        t = (k[...].astype(F32) + r[...].astype(F32)).astype(BF)
        for z in range(2):
            own[z, :, cs] = t[2 * z]
            send[z, :, cs] = t[2 * z + 1]


def fold_at_body(*refs):
    ins, outs = refs[:8], refs[8:]
    for i in range(4):
        k, r = ins[2 * i], ins[2 * i + 1]
        kept, sent = outs[2 * (i // 2)], outs[2 * (i // 2) + 1]
        cs = slice((i % 2) * HI, (i % 2) * HI + HI)
        t = (k[...].astype(F32) + r[...].astype(F32)).astype(BF)
        kept[:, :, cs] = t[:4]
        sent[:, :, cs] = t[4:]


def fold_ff_two_body(own, got, keep, send):
    t = own[...].astype(F32) + got[...].astype(F32)
    keep[...] = t[0]
    send[...] = t[1].astype(BF)


def finish_ff_body(own, got, in_ref, out_ref):
    w = out_ref.shape[1]
    out_ref[...] = own[:, :w] + got[:, :w].astype(F32)
    in_ref[...] = own[:, w:] + got[:, w:].astype(F32)


def finish_body(own, total, a, b, c, *outs):
    def got(cs):
        return a[:, cs].astype(F32) + b[:, cs].astype(F32) + c[:, cs].astype(F32)

    for i, ref in enumerate(outs[:4]):
        cs = slice(i * HI, (i + 1) * HI)
        ref[...] = own[:, cs] + got(cs)
    at = 4 * HI
    split_small(total[...] + (got(slice(at, at + 128)) + got(slice(at + 128, at + 256))), *outs[4:])


def split_small(v, gain1, gain2, gpre, gpost):
    for i in range(6):
        gain1[i * 128 : (i + 1) * 128] = v[i]
        gain2[i * 128 : (i + 1) * 128] = v[8 + i]
    gpre[...] = v[16 : 16 + HEADS, :HEADS]
    gpost[...] = v[32:48].T[:HEADS, :HEADS]


def split_small_body(v, *outs):
    split_small(v[...], *outs)


def scatter_plain(ka, sa, kb, sb):
    w = ka.shape[2]
    flat = jnp.concatenate(
        [jnp.concatenate([k, s], axis=0).reshape(768, w) for k, s in ((ka, sa), (kb, sb))], axis=1
    )
    return lax.psum_scatter(flat.astype(F32), "dp", scatter_dimension=0, tiled=True)


def sum_all(v):
    n = lax.axis_size("dp")
    v = v + swap(v)
    bit = 1
    while bit < n:
        v = v + hop(v, bit)
        bit *= 2
    return v


def on_device(
    tokens, cotangent, segment_ids, norm1_gain, w_query, w_key, w_value, pre_mix, post_mix,
    w_output, norm2_gain, w_in, w_out,
):
    ids = jnp.stack([lax.axis_index("tensor"), lax.axis_index("dp")]).astype(jnp.int32)
    xor = lax.axis_size("dp") == 16
    low = lambda v: v.astype(BF)
    D = norm1_gain.shape[0]
    tie = lax.optimization_barrier
    gain1, gain2 = norm1_gain.reshape(1, D), norm2_gain.reshape(1, D)
    seg = segment_ids.reshape(1, SEQ)

    every = lambda v: lax.all_gather(v, "dp", axis=0, tiled=True)
    r, ff = w_in.shape
    shard_qk, shard_vo, shard_ff = once(
        cast_body, (sds((r, INNER)), sds((r, INNER)), sds((r, 2 * ff))),
        tuple(far(w) for w in (w_query, w_key, w_value, w_output.T, w_in, w_out.T)), "cast", scalars=0,
    )
    if xor:
        z_qk = gather_z(shard_qk)
    w_ff = every(shard_ff)
    x_oth, cot_oth = swap(tokens), swap(cotangent)
    act_loc, act_oth, actT, x_own, cot_own, cot_rest, cotT = once(
        prepare_body,
        (
            sds((HALF, D)), sds((HALF, D)), hbm((D, SEQ)), hbm((HALF, D)), hbm((HALF, D)),
            hbm((HALF, D)), hbm((D, SEQ)),
        ),
        (far(tokens), x_oth, far(cotangent), cot_oth, gain1), "prepare", scalars=0,
    )
    if xor:
        *z_qk, act_loc = tie((*z_qk, act_loc))
        a, ra, b, rb = gather_one(z_qk)
        z_vo = gather_z(after(shard_vo, *z_qk))
        qk_parts = gather_two(a, ra, b, rb)
        *z_vo, ax, ay, bx, by = tie((*z_vo, *qk_parts))
        a, ra, b, rb = gather_one(z_vo)
        w_qk = gathered(ids, (ax, ay, bx, by))
    else:
        w_qk, w_vo = every(shard_qk), every(shard_vo)
    q, qT, k, kT = once(
        project_qk_body,
        (hbm((HALF, INNER)), sds((INNER, HALF)), sds((SEQ, INNER)), hbm((INNER, SEQ))),
        (ids, act_loc, act_oth, w_qk, swap(w_qk)), "project_qk", flops=1.8e9,
    )
    if xor:
        ra, rb, k = tie((ra, rb, k))
        vo_parts = gather_two(a, ra, b, rb)
        k = after(k, vo_parts[0], vo_parts[2])
    pT = logits_softmax(ids, pre_mix, seg, k, qT)
    if xor:
        w_vo = gathered(ids, tie((*vo_parts, pT))[:4])
    vo_o = swap(w_vo)
    v, vT = once(
        project_v_body, (hbm((SEQ, INNER)), sds((INNER, SEQ))),
        (ids, act_loc, act_oth, w_vo, vo_o), "project_v", flops=1.2e9,
    )
    uT, heads = attend(ids, post_mix, vT, pT)
    mid, act2, act2T = once(
        middle_body, (hbm((HALF, D), F32), hbm((HALF, D)), hbm((D, HALF))),
        (x_own, heads, w_vo, vo_o, gain2), "middle", scalars=0, flops=6e8,
    )
    out_own, out_oth, ga_own, ga_oth, ka, sa, kb, sb = ffn(
        xor, ids, far(act2), far(swap(act2)), far(act2T), far(swap(act2T)), far(cot_own), far(cot_rest), far(cotT), far(w_ff)
    )
    if xor:
        ra, rb = hop(sa, 1), hop(sb, 2)
    stay, sent, gh, ghT, gain2_part, gwo, gwo_o = once(
        middle_back_body,
        (
            hbm((BLK, D), F32), hbm((BLK, D), F32), sds((HALF, INNER)), sds((INNER, HALF)),
            hbm((1, D), F32), sds((D, HI)), sds((D, HI)),
        ),
        (ga_own, swap(ga_oth), mid, cot_own, gain2, heads, w_vo, vo_o),
        "middle_back", scalars=0, flops=1.2e9,
    )
    got_sent, got_out = swap(sent), swap(out_oth)
    gL, gv, gv_o, gpost = attend_back(ids, post_mix, v, ghT, gh, pT, uT)
    grads = (sds((8, 48, HI)),) * 4
    if xor:
        gv, gv_o, got_sent, got_out = tie((gv, gv_o, got_sent, got_out))
    gv, *vo = once(
        lambda *r: grad_vo_body(xor, *r), (hbm((SEQ, HI)),) + grads,
        (ids, actT, gv, swap(gv_o), gwo, swap(gwo_o)), "grad_vo",
        scratch=[pltpu.VMEM((D, HI), F32)], flops=6e8,
    )
    if xor:
        vo_ka, vo_sa, vo_kb, vo_sb = vo
        ra, rb = tie((ra, rb, vo_sa))[:2]
        ff_ka, ff_sa, ff_kb, ff_sb = fold_one(ka, ra, kb, rb)
        ff_ra, ff_rb = hop(ff_sa, 2), hop(ff_sb, 1)
        gL = after(gL, ff_sa, vo_sa)
    gq, gq_o, gk, gk_o, gpre = scores_back(ids, pre_mix, kT, qT, q, gL)
    if xor:
        ff_ra, ff_rb, gq, gq_o, gk_o = tie((ff_ra, ff_rb, gq, gq_o, gk_o))
        wide = ff_ka.shape[2] * 2
        ff_own, ff_send = once(
            fold_ff_body, (sds((2, 48, wide)),) * 2, (ff_ka, ff_ra, ff_kb, ff_rb), "fold_ff", scalars=0
        )
        ff_got = hop(ff_send, 4)
        vo_sa, vo_sb = tie((vo_sa, vo_sb, ff_send))[:2]
        vo_ra, vo_rb = hop(vo_sa, 1), hop(vo_sb, 2)
        gq, gk = tie((gq, gk, ff_send))[:2]
    gq, gk, *qk = once(
        lambda *r: grad_qk_body(xor, *r), (sds((SEQ, HI)),) * 2 + grads,
        (ids, actT, gq, swap(gq_o), gk, swap(gk_o)), "grad_qk",
        scratch=[pltpu.VMEM((D, HI), F32)], flops=1.2e9,
    )
    if xor:
        qk_ka, qk_sa, qk_kb, qk_sb = qk
        qk_ra, qk_rb = hop(qk_sa, 1), hop(qk_sb, 2)
        gq, vo_ra, vo_rb = tie((gq, vo_ra, vo_rb))
    ga_loc, ga_oth = once(
        act_back_body, (sds((HALF, D), F32), sds((HALF, D))), (gq, gk, gv, w_qk, w_vo),
        "act_back", scalars=0, flops=0.3e9, moved=1,
    )
    ga_got = swap(ga_oth)
    if xor:
        ff_own, ff_got = tie((ff_own, ff_got, ga_oth))[:2]
        ff_own, ff_send = once(
            fold_ff_two_body, (sds((48, wide), F32), sds((48, wide))), (ff_own, ff_got), "fold_ff_two", scalars=0,
            flops=2e9, moved=1,
        )
        ff_got = hop(ff_send, 8)
        qk_ra, qk_rb, ff_two = tie((qk_ra, qk_rb, ff_send))
        at_ka, at_sa, at_kb, at_sb = once(
            fold_at_body, (sds((4, 48, INNER)),) * 4,
            (qk_ka, qk_ra, vo_ka, vo_ra, qk_kb, qk_rb, vo_kb, vo_rb), "fold_at", scalars=0, flops=5e9,
        )
        at_ra, at_rb = hop(at_sa, 2), hop(at_sb, 1)
        ga_loc, ga_got = tie((ga_loc, ga_got, at_sa))[:2]
    grad_tokens, small = once(
        tokens_back_body, (sds((HALF, D)), sds((48, 128), F32)),
        (ga_loc, ga_got, tokens, gain1, stay, got_sent, gain2_part, gpre, gpost),
        "tokens_back", scalars=0,
    )
    r = w_in.shape[0]
    part = sds((r, HI), F32)
    small_outs = (sds((D,), F32),) * 2 + (sds((HEADS, HEADS), F32),) * 2
    if xor:
        got = swap(small)
        mid, small = tie((mid, small))
        out_stay, out_sent = once(
            output_body, (sds((BLK, D)), sds((BLK, D))), (mid, out_own, got_out), "output", scalars=0
        )
        out_got = swap(out_sent)
        small, got = tie((small, got, out_sent))[:2]
        small = small + got
        small = small + hop(small, 1)
        got = hop(small, 2)
        at_ra, at_rb, got, small, ff_got = tie((at_ra, at_rb, got, small, ff_got))
        at, total, *sends = fold_two(at_ka, at_ra, at_kb, at_rb, small, got)
        gots = [hop(sends[e], 4 * (e + 1)) for e in range(3)]
        out_got = tie((out_got, at))[0]
        (output,) = once(join_body, (sds((HALF, D)),), (out_stay, out_got), "join", scalars=0)
        grad_in, grad_out = once(
            finish_ff_body, (sds((r, ff), F32),) * 2, (ff_own, ff_got), "finish_ff", scalars=0
        )
        gots = tie((*gots, output, grad_in))[:3]
        grad_q, grad_v, grad_k, grad_o, *sums = once(
            finish_body, (part,) * 4 + small_outs, (at, total, *gots), "finish", scalars=0
        )
    else:
        grad_qk, grad_vo = scatter_plain(*qk), scatter_plain(*vo)
        grad_ffn = scatter_plain(ka, sa, kb, sb)
        grad_q, grad_k, grad_v, grad_o = grad_qk[:, :HI], grad_qk[:, HI:], grad_vo[:, :HI], grad_vo[:, HI:]
        grad_in, grad_out = grad_ffn[:, ff:], grad_ffn[:, :ff]
        sums = once(split_small_body, small_outs, (sum_all(small),), "split_small", scalars=0)
        out_stay, out_sent = once(
            output_body, (sds((BLK, D)), sds((BLK, D))), (mid, out_own, got_out), "output", scalars=0
        )
        output = jnp.concatenate([out_stay, swap(out_sent)], axis=0)
    return (
        output, grad_tokens, sums[0], grad_q, grad_k, grad_v, sums[2], sums[3],
        grad_o.T, sums[1], grad_in, grad_out.T,
    )


def solution(mesh):
    rows = P(("dp", "tensor"), None)
    w, wt = P("dp", "tensor"), P("tensor", "dp")
    return jax.shard_map(
        on_device,
        mesh=mesh,
        in_specs=(rows, rows, P("dp"), P(), w, w, w, P(), P(), wt, P(), w, wt),
        out_specs=(rows, rows, P(), w, w, w, P(), P(), wt, P(), w, wt),
        check_vma=False,
    )
```

```python
import math

import jax
import jax.numpy as jnp
from jax import lax
from jax.experimental import pallas as pl
from jax.experimental.pallas import tpu as pltpu
from jax.sharding import PartitionSpec as P

HEADS = 12
HD = 64
INNER = 768
HI = INNER // 2
SEQ = 1024
HALF = SEQ // 2
BLK = 256
EPSILON = 1e-06
LOG2E = 1.4426950408889634
BF = jnp.bfloat16
F32 = jnp.float32
HB1, HB2, HB3, HB4 = 3, 3, 3, 3
FT = 512
PART = 256


def dot(a, b):
    return jnp.dot(a, b, preferred_element_type=F32)


def dot_nt(a, b):
    return lax.dot_general(a, b, (((1,), (1,)), ((), ())), preferred_element_type=F32)


def smem():
    return pl.BlockSpec(memory_space=pltpu.SMEM)


def whole():
    return pl.BlockSpec(memory_space=pltpu.VMEM)


def full(s):
    return pl.BlockSpec(s, lambda *i: (0,) * len(s))


def params(mib=24):
    return pltpu.CompilerParams(vmem_limit_bytes=mib * 1024 * 1024)


def cost(flops, moved, exps=0):
    return pl.CostEstimate(flops=int(flops), bytes_accessed=int(moved), transcendentals=int(exps))


def sds(shape, dtype=BF):
    return jax.ShapeDtypeStruct(shape, dtype)


def once(body, outs, args, name, scalars=1, scratch=(), flops=0, moved=None):
    if moved is None:
        moved = sum(math.prod(a.shape) * a.dtype.itemsize for a in (*args, *outs))
    return pl.pallas_call(
        body,
        in_specs=[smem()] * scalars + [whole()] * (len(args) - scalars),
        out_specs=[whole()] * len(outs),
        out_shape=list(outs),
        scratch_shapes=list(scratch),
        compiler_params=params(),
        cost_estimate=cost(flops, moved),
        name=name,
    )(*args)


def per_core(ids_ref, run):
    for c in range(2):
        pl.when(ids_ref[0] == c)(lambda c=c: run(c))


def head(c, i):
    return (i + c * (HEADS // 2)) % HEADS


def spread(rep_ref, row, values):
    for g, value in enumerate(values):
        rep_ref[row : row + 1, g * HD : (g + 1) * HD] = jnp.full((1, HD), value, F32)


def hbm(shape, dtype=BF):
    return pltpu.HBM(shape, dtype)


def far(v):
    return pltpu.with_memory_space_constraint(v, pltpu.HBM)


def chunks(c):
    return (1, 4) if c == 0 else (3, 2)


def blocks_of(c):
    return (0, 3) if c == 0 else (2, 1)


def logits_body(ids_ref, pre_ref, seg_ref, k_ref, qT_ref, pT_ref, mask_ref):
    step = pl.program_id(0)

    def run(c):
        nj, bl = chunks(c), blocks_of(c)
        base = (0, nj[0] * BLK)

        @pl.when(step == 0)
        def _():
            seg = seg_ref[...].astype(F32)
            down = jnp.broadcast_to(seg, (8, SEQ)).T[:, :1]
            for b in range(2):
                qpos = lax.broadcasted_iota(jnp.int32, (BLK, BLK), 1) + bl[b] * BLK
                qseg = seg[:, bl[b] * BLK : (bl[b] + 1) * BLK]
                for j in range(nj[b]):
                    kpos = lax.broadcasted_iota(jnp.int32, (BLK, BLK), 0) + j * BLK
                    ok = (kpos <= qpos) & (down[j * BLK : (j + 1) * BLK] == qseg)
                    at = base[b] + j * BLK
                    mask_ref[at : at + BLK, :] = jnp.where(ok, 0.0, -1e30)

        for hh in range(HB1):
            h = step * HB1 + hh
            scale = [pre_ref[h, head(c, g)] * (0.125 * LOG2E) for g in range(HEADS)]
            for b in range(2):
                n = nj[b] * BLK
                qs = jnp.concatenate(
                    [
                        (
                            qT_ref[g * HD : (g + 1) * HD, b * BLK : (b + 1) * BLK].astype(F32)
                            * scale[g]
                        ).astype(BF)
                        for g in range(HEADS)
                    ],
                    axis=0,
                )
                s = dot(k_ref[:n, :], qs) + mask_ref[base[b] : base[b] + n, :]
                m = jnp.max(s, axis=0, keepdims=True)
                e = jnp.exp2(s - m)
                inv = 1.0 / jnp.sum(e, axis=0, keepdims=True)
                pT_ref[base[b] : base[b] + n, hh * BLK : (hh + 1) * BLK] = (e * inv).astype(BF)

    per_core(ids_ref, run)


def logits_softmax(ids, pre, seg, k, qT):
    return pl.pallas_call(
        logits_body,
        grid=(HEADS // HB1,),
        in_specs=[smem(), smem(), full((1, SEQ)), full((SEQ, INNER)), full((INNER, HALF))],
        out_specs=pl.BlockSpec((5 * BLK, HB1 * BLK), lambda h: (0, h)),
        out_shape=hbm((5 * BLK, HEADS * BLK)),
        scratch_shapes=[pltpu.VMEM((5 * BLK, BLK), F32)],
        compiler_params=params(),
        cost_estimate=cost(6.04e9, 10e6, 4e6),
        name="logits_softmax",
    )(ids, pre, seg, k, qT)


def attend_body(ids_ref, post_ref, vT_ref, pT_ref, uT_ref, h_ref, acc_ref):
    step = pl.program_id(0)

    def run(c):
        nj = chunks(c)
        base = (0, nj[0] * BLK)
        for b in range(2):
            n = nj[b] * BLK
            cs = slice(b * BLK, (b + 1) * BLK)
            us = []
            for hh in range(HB2):
                u = dot(vT_ref[:, :n], pT_ref[base[b] : base[b] + n, hh * BLK : (hh + 1) * BLK])
                uT_ref[hh * INNER : (hh + 1) * INNER, cs] = u.astype(BF)
                us.append(u)
            for k in range(HEADS):
                rs = slice(k * HD, (k + 1) * HD)
                t = us[0][rs, :] * post_ref[head(c, k), step * HB2]
                for hh in range(1, HB2):
                    t = t + us[hh][rs, :] * post_ref[head(c, k), step * HB2 + hh]
                acc_ref[rs, cs] += t

    @pl.when(step == 0)
    def _():
        acc_ref[...] = jnp.zeros_like(acc_ref)

    per_core(ids_ref, run)

    @pl.when(step == HEADS // HB2 - 1)
    def _():
        h_ref[...] = acc_ref[...].T.astype(BF)


def attend(ids, post, vT, pT):
    return pl.pallas_call(
        attend_body,
        grid=(HEADS // HB2,),
        in_specs=[smem(), smem(), full((INNER, SEQ)), pl.BlockSpec((5 * BLK, HB2 * BLK), lambda h: (0, h))],
        out_specs=[pl.BlockSpec((HB2 * INNER, HALF), lambda h: (h, 0)), full((HALF, INNER))],
        out_shape=[hbm((HEADS * INNER, HALF)), sds((HALF, INNER))],
        scratch_shapes=[pltpu.VMEM((INNER, HALF), F32)],
        compiler_params=params(),
        cost_estimate=cost(6.04e9, 20e6),
        name="attend",
    )(ids, post, vT, far(pT))


def split_rows(c, acc_ref, own_ref, oth_ref):
    for d in range(2):
        src = slice((c ^ d) * HALF, (c ^ d) * HALF + HALF)
        dst = slice(d * HALF, (d + 1) * HALF)
        own_ref[dst, :] = acc_ref[src, :HI].astype(BF)
        oth_ref[dst, :] = acc_ref[src, HI:].astype(BF)


def keep_sum(ref, h, k, b, g):
    g = g[:, :128] + g[:, 128:]
    ref[h, k : k + 1, :] = g if b == 0 else ref[h, k : k + 1, :] + g


def attend_back_body(
    ids_ref, post_ref, v_ref, ghT_ref, gh_ref, pT_ref, uT_ref,
    gL_ref, own_ref, oth_ref, gpost_ref, acc_ref, rep_ref,
):
    step = pl.program_id(0)

    def run(c):
        nj = chunks(c)
        base = (0, nj[0] * BLK)
        for hh in range(HB3):
            spread(rep_ref, hh, [post_ref[head(c, k), step * HB3 + hh] for k in range(HEADS)])
        for b in range(2):
            n = nj[b] * BLK
            cs = slice(b * BLK, (b + 1) * BLK)
            g2s = []
            for hh in range(HB3):
                h = step * HB3 + hh
                hs = slice(hh * BLK, (hh + 1) * BLK)
                r = jnp.zeros((1, BLK), F32)
                parts = []
                for k in range(HEADS):
                    gk = ghT_ref[k * HD : (k + 1) * HD, cs].astype(F32)
                    u = uT_ref[hh * INNER + k * HD : hh * INNER + (k + 1) * HD, cs].astype(F32)
                    g = jnp.sum(gk * u, axis=0, keepdims=True)
                    w = post_ref[head(c, k), h]
                    keep_sum(gpost_ref, hh, head(c, k), b, g)
                    r = r + g * w
                    parts.append((gk * w).astype(BF))
                gP = dot(v_ref[:n, :], jnp.concatenate(parts, axis=0))
                p = pT_ref[base[b] : base[b] + n, hs]
                gL_ref[base[b] : base[b] + n, hs] = (p.astype(F32) * (gP - r)).astype(BF)
                g2s.append((gh_ref[cs, :].astype(F32) * rep_ref[hh : hh + 1, :]).astype(BF))
            acc_ref[:n, :] += dot(pT_ref[base[b] : base[b] + n, :], jnp.concatenate(g2s, axis=0))

        @pl.when(step == HEADS // HB3 - 1)
        def _():
            split_rows(c, acc_ref, own_ref, oth_ref)

    @pl.when(step == 0)
    def _():
        acc_ref[...] = jnp.zeros_like(acc_ref)

    per_core(ids_ref, run)


def attend_back(ids, post, v, ghT, gh, pT, uT):
    return pl.pallas_call(
        attend_back_body,
        grid=(HEADS // HB3,),
        in_specs=[
            smem(), smem(), full((SEQ, INNER)), full((INNER, HALF)), full((HALF, INNER)),
            pl.BlockSpec((5 * BLK, HB3 * BLK), lambda h: (0, h)),
            pl.BlockSpec((HB3 * INNER, HALF), lambda h: (h, 0)),
        ],
        out_specs=[
            pl.BlockSpec((5 * BLK, HB3 * BLK), lambda h: (0, h)),
            full((SEQ, HI)), full((SEQ, HI)),
            pl.BlockSpec((HB3, HEADS, 128), lambda h: (h, 0, 0)),
        ],
        out_shape=[
            hbm((5 * BLK, HEADS * BLK)), sds((SEQ, HI)), sds((SEQ, HI)),
            hbm((HEADS, HEADS, 128), F32),
        ],
        scratch_shapes=[pltpu.VMEM((SEQ, INNER), F32), pltpu.VMEM((8, INNER), F32)],
        compiler_params=params(),
        cost_estimate=cost(12.1e9, 30e6),
        name="attend_back",
    )(ids, post, v, ghT, gh, far(pT), far(uT))


def scores_back_body(
    ids_ref, pre_ref, kT_ref, qT_ref, q_ref, gL_ref,
    gqa_ref, gqb_ref, own_ref, oth_ref, gpre_ref, accq_ref, acck_ref, rep_ref,
):
    step = pl.program_id(0)

    def run(c):
        nj = chunks(c)
        base = (0, nj[0] * BLK)
        scale = [
            [pre_ref[step * HB4 + hh, head(c, g)] * 0.125 for g in range(HEADS)] for hh in range(HB4)
        ]
        for hh in range(HB4):
            spread(rep_ref, hh, scale[hh])
        for b in range(2):
            n = nj[b] * BLK
            cs = slice(b * BLK, (b + 1) * BLK)
            ws, q2s = [], []
            for hh in range(HB4):
                ws.append(dot(kT_ref[:, :n], gL_ref[base[b] : base[b] + n, hh * BLK : (hh + 1) * BLK]))
                q2s.append((q_ref[cs, :].astype(F32) * rep_ref[hh : hh + 1, :]).astype(BF))
            for k in range(HEADS):
                rs = slice(k * HD, (k + 1) * HD)
                qk = qT_ref[rs, cs].astype(F32)
                t = None
                for hh in range(HB4):
                    w = ws[hh][rs, :]
                    g = jnp.sum(qk * w, axis=0, keepdims=True) * 0.125
                    keep_sum(gpre_ref, hh, head(c, k), b, g)
                    u = w * scale[hh][k]
                    t = u if t is None else t + u
                accq_ref[rs, cs] += t
            acck_ref[:n, :] += dot(gL_ref[base[b] : base[b] + n, :], jnp.concatenate(q2s, axis=0))

        @pl.when(step == HEADS // HB4 - 1)
        def _():
            split_rows(c, acck_ref, own_ref, oth_ref)

    @pl.when(step == 0)
    def _():
        accq_ref[...] = jnp.zeros_like(accq_ref)
        acck_ref[...] = jnp.zeros_like(acck_ref)

    per_core(ids_ref, run)

    @pl.when(step == HEADS // HB4 - 1)
    def _():
        gqa_ref[...] = accq_ref[:HI, :].T.astype(BF)
        gqb_ref[...] = accq_ref[HI:, :].T.astype(BF)


def scores_back(ids, pre, kT, qT, q, gL):
    return pl.pallas_call(
        scores_back_body,
        grid=(HEADS // HB4,),
        in_specs=[
            smem(), smem(), full((INNER, SEQ)), full((INNER, HALF)), full((HALF, INNER)),
            pl.BlockSpec((5 * BLK, HB4 * BLK), lambda h: (0, h)),
        ],
        out_specs=[
            full((HALF, HI)), full((HALF, HI)), full((SEQ, HI)), full((SEQ, HI)),
            pl.BlockSpec((HB4, HEADS, 128), lambda h: (h, 0, 0)),
        ],
        out_shape=[
            sds((HALF, HI)), sds((HALF, HI)), sds((SEQ, HI)), sds((SEQ, HI)),
            sds((HEADS, HEADS, 128), F32),
        ],
        scratch_shapes=[
            pltpu.VMEM((INNER, HALF), F32), pltpu.VMEM((SEQ, INNER), F32), pltpu.VMEM((8, INNER), F32),
        ],
        compiler_params=params(),
        cost_estimate=cost(12.1e9, 14e6),
        name="scores_back",
    )(ids, pre, kT, qT, q, far(gL))


def own_rows(loc, oth):
    return jnp.concatenate([loc[:BLK], oth[BLK:]], axis=0)


def project_qk_body(ids_ref, loc_ref, oth_ref, wa_ref, wb_ref, q_ref, qT_ref, k_ref, kT_ref):
    own = own_rows(loc_ref[...], oth_ref[...])
    for i, w in enumerate((wa_ref, wb_ref)):
        t = dot(own, w[:, :HI])
        cs = slice(i * HI, (i + 1) * HI)
        q_ref[:, cs] = t.astype(BF)
        qT_ref[cs, :] = t.T.astype(BF)
    project_rows(ids_ref, loc_ref, oth_ref, wa_ref, wb_ref, HI, k_ref, kT_ref)


def project_v_body(ids_ref, loc_ref, oth_ref, wa_ref, wb_ref, v_ref, vT_ref):
    project_rows(ids_ref, loc_ref, oth_ref, wa_ref, wb_ref, 0, v_ref, vT_ref)


def project_rows(ids_ref, loc_ref, oth_ref, wa_ref, wb_ref, col, k_ref, kT_ref):
    def run(c):
        for d, rows in enumerate((loc_ref, oth_ref)):
            rs = slice((c ^ d) * HALF, (c ^ d) * HALF + HALF)
            for i, w in enumerate((wa_ref, wb_ref)):
                t = dot(rows[...], w[:, col : col + HI])
                cs = slice(i * HI, (i + 1) * HI)
                k_ref[rs, cs] = t.astype(BF)
                kT_ref[cs, rs] = t.T.astype(BF)

    per_core(ids_ref, run)


def norm(v):
    inv = lax.rsqrt(jnp.mean(v * v, axis=-1, keepdims=True) + EPSILON)
    return v * inv, inv


def cast_body(q_ref, k_ref, v_ref, o_ref, in_ref, out_ref, qk_ref, vo_ref, ff_ref):
    qk_ref[:, :HI] = q_ref[...].astype(BF)
    qk_ref[:, HI:] = k_ref[...].astype(BF)
    vo_ref[:, :HI] = v_ref[...].astype(BF)
    vo_ref[:, HI:INNER] = o_ref[...].astype(BF)
    ff = in_ref.shape[1]
    ff_ref[:, :ff] = in_ref[...].astype(BF)
    ff_ref[:, ff:] = out_ref[:, : ff - PART].astype(BF)
    vo_ref[:, INNER:] = out_ref[:, ff - PART :].astype(BF)


def prepare_body(
    x_ref, xo_ref, c_ref, co_ref, gain_ref,
    loc_ref, oth_ref, actT_ref, own_ref, cown_ref, crest_ref, cT_ref,
):
    for src, dst, cs in ((x_ref, loc_ref, slice(0, HALF)), (xo_ref, oth_ref, slice(HALF, SEQ))):
        act = norm(src[...].astype(F32))[0] * gain_ref[...]
        dst[...] = act.astype(BF)
        actT_ref[:, cs] = act.T.astype(BF)
    own_ref[:BLK, :] = x_ref[:BLK, :]
    own_ref[BLK:, :] = xo_ref[BLK:, :]
    for dst, a, b, at in ((cown_ref, c_ref, co_ref, 0), (crest_ref, co_ref, c_ref, HALF)):
        dst[:BLK, :] = a[:BLK, :]
        dst[BLK:, :] = b[BLK:, :]
        cT_ref[:, at : at + BLK] = a[:BLK, :].astype(F32).T.astype(BF)
        cT_ref[:, at + BLK : at + HALF] = b[BLK:, :].astype(F32).T.astype(BF)


def middle_body(x_ref, h_ref, wa_ref, wb_ref, gain_ref, mid_ref, act_ref, actT_ref):
    mid = x_ref[...].astype(F32) + dot_nt(h_ref[:, :HI], wa_ref[:, HI:]) + dot_nt(h_ref[:, HI:], wb_ref[:, HI:])
    act = norm(mid)[0] * gain_ref[...]
    mid_ref[...] = mid
    act_ref[...] = act.astype(BF)
    actT_ref[...] = act.T.astype(BF)


def emit(me, scr_ref, cols, keep_ref, send_ref, outer_x):
    for e in range(16):
        x, y, z = e & 1, (e >> 1) & 1, e >> 2
        if me is None:
            ref, at, row = (keep_ref, send_ref)[e >> 3], e & 7, e * 48
        else:
            first, second = (x, y) if outer_x else (y, x)
            ref, at = (keep_ref, send_ref)[first], second * 4 + z
            row = pl.multiple_of(lax.bitwise_xor(me, e) * 48, 16)
        ref[at, :, cols] = scr_ref[pl.ds(row, 48), cols].astype(BF)


def gates(v):
    sq = v * v
    s = 0.5 * jnp.tanh(v * (0.7978845608028654 + 0.035677408136300125 * sq)) + 0.5
    slope = s + v * (1.5957691216057308 + 0.21406444881780075 * sq) * (s - s * s)
    return (v * s).astype(BF), slope


def ffn_body(
    xor, ids_ref, aown_ref, aoth_ref, aTown_ref, aToth_ref, cown_ref, coth_ref, cT_ref,
    win_ref, wouta_ref, woutb_ref, part_ref, outa_ref, outb_ref, gaa_ref, gab_ref, ka_ref, sa_ref, kb_ref, sb_ref,
    acco_ref, accg_ref, scr_ref,
):
    step = pl.program_id(0)
    last = pl.num_programs(0) - 1
    me = ids_ref[1] if xor else None

    @pl.when(step == 0)
    def _():
        acco_ref[...] = jnp.zeros_like(acco_ref)
        accg_ref[...] = jnp.zeros_like(accg_ref)

    win = win_ref[...]
    wout = jnp.concatenate(
        [wouta_ref[...], jnp.where(step == last, part_ref[...], woutb_ref[...])], axis=1
    )
    v0, v1 = dot(aown_ref[...], win), dot(aoth_ref[...], win)
    h0, s0 = gates(v0)
    g0 = dot(cown_ref[...], wout)
    h1, s1 = gates(v1)
    g1 = dot(coth_ref[...], wout)
    acco_ref[:HALF, :] += dot_nt(h0, wout)
    p0 = (g0.astype(BF).astype(F32) * s0).astype(BF)
    acco_ref[HALF:, :] += dot_nt(h1, wout)
    p1 = (g1.astype(BF).astype(F32) * s1).astype(BF)
    accg_ref[:HALF, :] += dot_nt(p0, win)
    accg_ref[HALF:, :] += dot_nt(p1, win)
    hid, gpre = (h0, h1), (p0, p1)
    scr_ref[...] = dot(cT_ref[:, :HALF], hid[0]) + dot(cT_ref[:, HALF:], hid[1])
    emit(me, scr_ref, slice(0, FT), ka_ref, sa_ref, True)
    scr_ref[...] = dot(aTown_ref[...], gpre[0]) + dot(aToth_ref[...], gpre[1])
    emit(me, scr_ref, slice(0, FT), kb_ref, sb_ref, False)

    @pl.when(step == last)
    def _():
        outa_ref[...] = acco_ref[:HALF, :]
        outb_ref[...] = acco_ref[HALF:, :].astype(BF)
        gaa_ref[...] = accg_ref[:HALF, :]
        gab_ref[...] = accg_ref[HALF:, :].astype(BF)


def ffn(xor, ids, aown, aoth, aTown, aToth, cown, coth, cT, w, part):
    width = (w.shape[1] + PART) // 2
    steps = width // FT
    tile = pl.BlockSpec((INNER, FT), lambda t: (0, t))
    end = w.shape[1] // PART - 1
    tile2 = pl.BlockSpec((INNER, PART), lambda t: (0, 2 * (steps + t)))
    tile3 = pl.BlockSpec((INNER, PART), lambda t: (0, jnp.minimum(2 * (steps + t) + 1, end)))
    grad = pl.BlockSpec((8, 48, FT), lambda t: (0, 0, t))
    half, halfT = full((HALF, INNER)), full((INNER, HALF))
    return pl.pallas_call(
        lambda *r: ffn_body(xor, *r),
        grid=(steps,),
        in_specs=[smem(), half, half, halfT, halfT, half, half, full((INNER, SEQ)), tile, tile2, tile3, full((INNER, PART))],
        out_specs=[half, half, half, half, grad, grad, grad, grad],
        out_shape=[
            sds((HALF, INNER), F32), sds((HALF, INNER)), sds((HALF, INNER), F32), sds((HALF, INNER)),
        ] + [sds((8, 48, width))] * 4,
        scratch_shapes=[
            pltpu.VMEM((SEQ, INNER), F32), pltpu.VMEM((SEQ, INNER), F32), pltpu.VMEM((INNER, FT), F32),
        ],
        compiler_params=params(44),
        cost_estimate=cost(14.5e9, 20e6, 1.6e6),
        name="ffn",
    )(ids, aown, aoth, aTown, aToth, cown, coth, cT, w, w, w, part)


def middle_back_body(
    ga_ref, gr_ref, mid_ref, cot_ref, gain_ref, h_ref, wa_ref, wb_ref,
    stay_ref, sent_ref, gh_ref, ghT_ref, gain_out, gwa_ref, gwb_ref,
):
    ga = ga_ref[...] + gr_ref[...].astype(F32)
    normed, inv = norm(mid_ref[...])
    scaled = ga * gain_ref[...]
    gm = cot_ref[...].astype(F32) + inv * (
        scaled - normed * jnp.mean(scaled * normed, axis=-1, keepdims=True)
    )
    gain_out[...] = jnp.sum(ga * normed, axis=0, keepdims=True)
    stay_ref[...] = gm[:BLK]
    sent_ref[...] = gm[BLK:]
    grad = gm.astype(BF)
    gT = gm.T.astype(BF)
    for i, (w, gw) in enumerate(((wa_ref, gwa_ref), (wb_ref, gwb_ref))):
        cs = slice(i * HI, (i + 1) * HI)
        t = dot(grad, w[:, HI:])
        gh_ref[:, cs] = t.astype(BF)
        ghT_ref[cs, :] = t.T.astype(BF)
        gw[...] = dot(gT, h_ref[:, cs]).astype(BF)


def joined(own, got):
    a, b = own.astype(F32), got.astype(F32)
    return jnp.concatenate([a[:HALF] + b[HALF:], a[HALF:] + b[:HALF]], axis=0).astype(BF)


def grad_vo_body(xor, ids_ref, aT_ref, gv_ref, rv_ref, go_ref, ro_ref, gv_out, ka, sa, kb, sb, scr):
    me = ids_ref[1] if xor else None
    gv = joined(gv_ref[...], rv_ref[...])
    gv_out[...] = gv
    scr[...] = dot(aT_ref[...], gv)
    emit(me, scr, slice(0, HI), ka, sa, True)
    scr[...] = go_ref[...].astype(F32) + ro_ref[...].astype(F32)
    emit(me, scr, slice(0, HI), kb, sb, False)


def grad_qk_body(xor, ids_ref, aT_ref, gq_ref, rq_ref, gk_ref, rk_ref, gq_out, gk_out, ka, sa, kb, sb, scr):
    me = ids_ref[1] if xor else None
    gq, rq = gq_ref[...], rq_ref[...]
    gq = jnp.concatenate([gq[:BLK], rq[BLK:], rq[:BLK], gq[BLK:]], axis=0)
    gq_out[...] = gq
    scr[...] = dot(aT_ref[...], gq)
    emit(me, scr, slice(0, HI), ka, sa, True)
    gk = joined(gk_ref[...], rk_ref[...])
    gk_out[...] = gk
    scr[...] = dot(aT_ref[...], gk)
    emit(me, scr, slice(0, HI), kb, sb, False)


def act_back_body(gq_ref, gk_ref, gv_ref, qk_ref, vo_ref, loc_ref, oth_ref):
    for rs, ref in ((slice(0, HALF), loc_ref), (slice(HALF, SEQ), oth_ref)):
        t = dot_nt(gq_ref[rs, :], qk_ref[:, :HI]) + dot_nt(gk_ref[rs, :], qk_ref[:, HI:])
        ref[...] = (t + dot_nt(gv_ref[rs, :], vo_ref[:, :HI])).astype(ref.dtype)


def output_body(mid_ref, own_ref, got_ref, stay_ref, sent_ref):
    out = (mid_ref[...] + own_ref[...] + got_ref[...].astype(F32)).astype(BF)
    stay_ref[...] = out[:BLK]
    sent_ref[...] = out[BLK:]


def join_body(stay_ref, got_ref, out_ref):
    out_ref[:BLK, :] = stay_ref[...]
    out_ref[BLK:, :] = got_ref[...]


def tokens_back_body(
    ga_ref, gr_ref, x_ref, gain_ref, stay_ref, got_ref, gain2_ref, gpre_ref, gpost_ref,
    out_ref, small_ref,
):
    ga = ga_ref[...] + gr_ref[...].astype(F32)
    normed, inv = norm(x_ref[...].astype(F32))
    scaled = ga * gain_ref[...]
    back = inv * (scaled - normed * jnp.mean(scaled * normed, axis=-1, keepdims=True))
    out_ref[:BLK, :] = (stay_ref[...] + back[:BLK]).astype(BF)
    out_ref[BLK:, :] = (got_ref[...] + back[BLK:]).astype(BF)
    gain1 = jnp.sum(ga * normed, axis=0, keepdims=True)
    small_ref[...] = jnp.zeros_like(small_ref)
    for i in range(6):
        cs = slice(i * 128, (i + 1) * 128)
        small_ref[i : i + 1, :] = gain1[:, cs]
        small_ref[8 + i : 9 + i, :] = gain2_ref[:, cs]
    small_ref[16 : 16 + HEADS, :HEADS] = jnp.sum(gpre_ref[...], axis=-1)
    small_ref[32 : 32 + HEADS, :HEADS] = jnp.sum(gpost_ref[...], axis=-1)


def swap(v):
    return lax.ppermute(v, "tensor", [(0, 1), (1, 0)])


def hop(v, mask):
    n = lax.axis_size("dp")
    return lax.ppermute(v, "dp", [(i, i ^ mask) for i in range(n)])


def after(v, *done):
    return lax.optimization_barrier((v, *done))[0]


def place_body(ids_ref, ax, ay, bx, by, *outs):
    me = ids_ref[1]
    w = ax.shape[3]
    for t, ref in enumerate((ax, ay, bx, by)):
        col = (t // 2) * w
        for i in range(2):
            for j in range(4):
                e = 4 * j + ((2 * i + t) if t < 2 else (i + 2 * (t - 2)))
                row = pl.multiple_of(lax.bitwise_xor(me, e) * 48, 16)
                start = 0
                for out in outs:
                    end = start + out.shape[1]
                    lo, hi = max(col, start), min(col + w, end)
                    if lo < hi:
                        out[pl.ds(row, 48), lo - start : hi - start] = ref[i, j, :, lo - col : hi - col]
                    start = end


def gather_z(shard):
    return [shard] + [hop(shard, 4 * e) for e in range(1, 4)]


def gather_one(pieces):
    z = jnp.stack(pieces, axis=0)
    w = z.shape[2] // 2
    a, b = z[:, :, :w], z[:, :, w:]
    return a, hop(a, 2), b, hop(b, 1)


def gather_two(a, ra, b, rb):
    a2, b2 = jnp.stack([a, ra], axis=0), jnp.stack([b, rb], axis=0)
    return a2, hop(a2, 1), b2, hop(b2, 2)


def gathered(ids, parts, *outs):
    return once(place_body, outs, (ids, *parts), "place")


def fold_one_body(ka, ra, kb, rb, oka, osa, okb, osb):
    for k, r, keep, send in ((ka, ra, oka, osa), (kb, rb, okb, osb)):
        t = (k[...].astype(F32) + r[...].astype(F32)).astype(BF)
        keep[...] = t[:4]
        send[...] = t[4:]


def fold_two_body(ka, ra, kb, rb, small, got, own, total, *sends):
    w = ka.shape[2]
    for k, r, cs in ((ka, ra, slice(0, w)), (kb, rb, slice(w, 2 * w))):
        t = k[...].astype(F32) + r[...].astype(F32)
        own[:, cs] = t[0]
        for e in range(3):
            sends[e][:, cs] = t[e + 1].astype(BF)
    v = small[...] + got[...]
    total[...] = v
    for send in sends:
        send[:, 2 * w :] = v.astype(BF)


def fold_one(ka, ra, kb, rb):
    piece = sds((4,) + ka.shape[1:])
    return once(fold_one_body, (piece,) * 4, (ka, ra, kb, rb), "fold_one", scalars=0)


def fold_two(*parts):
    w = 2 * parts[0].shape[2]
    outs = (sds((48, w), F32), sds((48, 128), F32)) + (sds((48, w + 128)),) * 3
    return once(fold_two_body, outs, parts, "fold_two", scalars=0)


def fold_ff_body(ka, ra, kb, rb, own, send):
    w = ka.shape[2]
    for k, r, cs in ((ka, ra, slice(0, w)), (kb, rb, slice(w, 2 * w))):
        t = (k[...].astype(F32) + r[...].astype(F32)).astype(BF)
        for z in range(2):
            own[z, :, cs] = t[2 * z]
            send[z, :, cs] = t[2 * z + 1]


def fold_at_body(*refs):
    ins, outs = refs[:8], refs[8:]
    for i in range(4):
        k, r = ins[2 * i], ins[2 * i + 1]
        kept, sent = outs[2 * (i // 2)], outs[2 * (i // 2) + 1]
        cs = slice((i % 2) * HI, (i % 2) * HI + HI)
        t = (k[...].astype(F32) + r[...].astype(F32)).astype(BF)
        kept[:, :, cs] = t[:4]
        sent[:, :, cs] = t[4:]


def fold_ff_two_body(own, got, keep, send):
    t = own[...].astype(F32) + got[...].astype(F32)
    keep[...] = t[0]
    send[...] = t[1].astype(BF)


def finish_ff_body(own, got, in_ref, out_ref):
    w = out_ref.shape[1]
    out_ref[...] = own[:, :w] + got[:, :w].astype(F32)
    in_ref[...] = own[:, w:] + got[:, w:].astype(F32)


def finish_body(own, total, a, b, c, *outs):
    def got(cs):
        return a[:, cs].astype(F32) + b[:, cs].astype(F32) + c[:, cs].astype(F32)

    for i, ref in enumerate(outs[:4]):
        cs = slice(i * HI, (i + 1) * HI)
        ref[...] = own[:, cs] + got(cs)
    at = 4 * HI
    split_small(total[...] + got(slice(at, at + 128)), *outs[4:])


def split_small(v, gain1, gain2, gpre, gpost):
    for i in range(6):
        gain1[i * 128 : (i + 1) * 128] = v[i]
        gain2[i * 128 : (i + 1) * 128] = v[8 + i]
    gpre[...] = v[16 : 16 + HEADS, :HEADS]
    gpost[...] = v[32:48].T[:HEADS, :HEADS]


def split_small_body(v, *outs):
    split_small(v[...], *outs)


def scatter_plain(ka, sa, kb, sb):
    w = ka.shape[2]
    flat = jnp.concatenate(
        [jnp.concatenate([k, s], axis=0).reshape(768, w) for k, s in ((ka, sa), (kb, sb))], axis=1
    )
    return lax.psum_scatter(flat.astype(F32), "dp", scatter_dimension=0, tiled=True)


def sum_all(v):
    n = lax.axis_size("dp")
    v = v + swap(v)
    bit = 1
    while bit < n:
        v = v + hop(v, bit)
        bit *= 2
    return v


def on_device(
    tokens, cotangent, segment_ids, norm1_gain, w_query, w_key, w_value, pre_mix, post_mix,
    w_output, norm2_gain, w_in, w_out,
):
    ids = jnp.stack([lax.axis_index("tensor"), lax.axis_index("dp")]).astype(jnp.int32)
    xor = lax.axis_size("dp") == 16
    low = lambda v: v.astype(BF)
    D = norm1_gain.shape[0]
    tie = lax.optimization_barrier
    gain1, gain2 = norm1_gain.reshape(1, D), norm2_gain.reshape(1, D)
    seg = segment_ids.reshape(1, SEQ)

    every = lambda v: lax.all_gather(v, "dp", axis=0, tiled=True)
    r, ff = w_in.shape
    shard_qk, shard_vo, shard_ff = once(
        cast_body, (sds((r, INNER)), sds((r, INNER + PART)), sds((r, 2 * ff - PART))),
        tuple(far(w) for w in (w_query, w_key, w_value, w_output.T, w_in, w_out.T)), "cast", scalars=0,
    )
    if xor:
        z_qk = gather_z(shard_qk)
    w_ff = every(shard_ff)
    x_oth, cot_oth = swap(tokens), swap(cotangent)
    act_loc, act_oth, actT, x_own, cot_own, cot_rest, cotT = once(
        prepare_body,
        (
            sds((HALF, D)), sds((HALF, D)), hbm((D, SEQ)), hbm((HALF, D)), hbm((HALF, D)),
            hbm((HALF, D)), hbm((D, SEQ)),
        ),
        (far(tokens), x_oth, far(cotangent), cot_oth, gain1), "prepare", scalars=0,
    )
    if xor:
        *z_qk, act_loc = tie((*z_qk, act_loc))
        a, ra, b, rb = gather_one(z_qk)
        z_vo = gather_z(after(shard_vo, *z_qk))
        qk_parts = gather_two(a, ra, b, rb)
        *z_vo, ax, ay, bx, by = tie((*z_vo, *qk_parts))
        a, ra, b, rb = gather_one(z_vo)
        (w_qk,) = gathered(ids, (ax, ay, bx, by), sds((D, INNER)))
    else:
        w_qk, w_vo = every(shard_qk), every(shard_vo)
        w_vo, w_part = w_vo[:, :INNER], w_vo[:, INNER:]
    q, qT, k, kT = once(
        project_qk_body,
        (hbm((HALF, INNER)), sds((INNER, HALF)), sds((SEQ, INNER)), hbm((INNER, SEQ))),
        (ids, act_loc, act_oth, w_qk, swap(w_qk)), "project_qk", flops=1.8e9,
    )
    if xor:
        ra, rb, k = tie((ra, rb, k))
        vo_parts = gather_two(a, ra, b, rb)
        k = after(k, vo_parts[0], vo_parts[2])
    pT = logits_softmax(ids, pre_mix, seg, k, qT)
    if xor:
        w_vo, w_part = gathered(ids, tie((*vo_parts, pT))[:4], sds((D, INNER)), hbm((D, PART)))
    vo_o = swap(w_vo)
    v, vT = once(
        project_v_body, (hbm((SEQ, INNER)), sds((INNER, SEQ))),
        (ids, act_loc, act_oth, w_vo, vo_o), "project_v", flops=1.2e9,
    )
    uT, heads = attend(ids, post_mix, vT, pT)
    mid, act2, act2T = once(
        middle_body, (hbm((HALF, D), F32), hbm((HALF, D)), hbm((D, HALF))),
        (x_own, heads, w_vo, vo_o, gain2), "middle", scalars=0, flops=6e8,
    )
    out_own, out_oth, ga_own, ga_oth, ka, sa, kb, sb = ffn(
        xor, ids, far(act2), far(swap(act2)), far(act2T), far(swap(act2T)), far(cot_own), far(cot_rest), far(cotT), far(w_ff), far(w_part)
    )
    if xor:
        ra, rb = hop(sa, 1), hop(sb, 2)
    stay, sent, gh, ghT, gain2_part, gwo, gwo_o = once(
        middle_back_body,
        (
            hbm((BLK, D), F32), hbm((BLK, D), F32), sds((HALF, INNER)), sds((INNER, HALF)),
            hbm((1, D), F32), sds((D, HI)), sds((D, HI)),
        ),
        (ga_own, swap(ga_oth), mid, cot_own, gain2, heads, w_vo, vo_o),
        "middle_back", scalars=0, flops=1.2e9,
    )
    got_sent, got_out, gwo_r = swap(sent), swap(out_oth), swap(gwo_o)
    gL, gv, gv_o, gpost = attend_back(ids, post_mix, v, ghT, gh, pT, uT)
    grads = (sds((8, 48, HI)),) * 4
    if xor:
        gv, gv_o, got_sent, got_out, gwo_r = tie((gv, gv_o, got_sent, got_out, gwo_r))
    gv, *vo = once(
        lambda *r: grad_vo_body(xor, *r), (hbm((SEQ, HI)),) + grads,
        (ids, actT, gv, swap(gv_o), gwo, gwo_r), "grad_vo",
        scratch=[pltpu.VMEM((D, HI), F32)], flops=6e8,
    )
    if xor:
        vo_ka, vo_sa, vo_kb, vo_sb = vo
        ra, rb = tie((ra, rb, vo_sa))[:2]
        ff_ka, ff_sa, ff_kb, ff_sb = fold_one(ka, ra, kb, rb)
        ff_ra, ff_rb = hop(ff_sa, 2), hop(ff_sb, 1)
        gL = after(gL, ff_sa, vo_sa)
    gq, gq_o, gk, gk_o, gpre = scores_back(ids, pre_mix, kT, qT, q, gL)
    if xor:
        ff_ra, ff_rb, gq, gq_o, gk_o = tie((ff_ra, ff_rb, gq, gq_o, gk_o))
        wide = ff_ka.shape[2] * 2
        ff_own, ff_send = once(
            fold_ff_body, (sds((2, 48, wide)),) * 2, (ff_ka, ff_ra, ff_kb, ff_rb), "fold_ff", scalars=0
        )
        ff_got = hop(ff_send, 4)
        vo_sa, vo_sb = tie((vo_sa, vo_sb, ff_send))[:2]
        vo_ra, vo_rb = hop(vo_sa, 1), hop(vo_sb, 2)
        gq, gk = tie((gq, gk, ff_send))[:2]
    gq, gk, *qk = once(
        lambda *r: grad_qk_body(xor, *r), (sds((SEQ, HI)),) * 2 + grads,
        (ids, actT, gq, swap(gq_o), gk, swap(gk_o)), "grad_qk",
        scratch=[pltpu.VMEM((D, HI), F32)], flops=1.2e9,
    )
    if xor:
        qk_ka, qk_sa, qk_kb, qk_sb = qk
        qk_ra, qk_rb = hop(qk_sa, 1), hop(qk_sb, 2)
        gq, vo_ra, vo_rb = tie((gq, vo_ra, vo_rb))
    ga_loc, ga_oth = once(
        act_back_body, (sds((HALF, D), F32), sds((HALF, D))), (gq, gk, gv, w_qk, w_vo),
        "act_back", scalars=0, flops=0.3e9, moved=1,
    )
    ga_got = swap(ga_oth)
    if xor:
        ff_own, ff_got = tie((ff_own, ff_got, ga_oth))[:2]
        ff_own, ff_send = once(
            fold_ff_two_body, (sds((48, wide), F32), sds((48, wide))), (ff_own, ff_got), "fold_ff_two", scalars=0,
            flops=2e9, moved=1,
        )
        ff_got = hop(ff_send, 8)
        qk_ra, qk_rb, ff_two = tie((qk_ra, qk_rb, ff_send))
        at_ka, at_sa, at_kb, at_sb = once(
            fold_at_body, (sds((4, 48, INNER)),) * 4,
            (qk_ka, qk_ra, vo_ka, vo_ra, qk_kb, qk_rb, vo_kb, vo_rb), "fold_at", scalars=0, flops=5e9,
        )
        at_ra, at_rb = hop(at_sa, 2), hop(at_sb, 1)
        ga_loc, ga_got = tie((ga_loc, ga_got, at_sa))[:2]
    grad_tokens, small = once(
        tokens_back_body, (sds((HALF, D)), sds((48, 128), F32)),
        (ga_loc, ga_got, tokens, gain1, stay, got_sent, gain2_part, gpre, gpost),
        "tokens_back", scalars=0,
    )
    r = w_in.shape[0]
    part = sds((r, HI), F32)
    small_outs = (sds((D,), F32),) * 2 + (sds((HEADS, HEADS), F32),) * 2
    if xor:
        got = swap(small)
        mid, small = tie((mid, small))
        out_stay, out_sent = once(
            output_body, (sds((BLK, D)), sds((BLK, D))), (mid, out_own, got_out), "output", scalars=0
        )
        out_got = swap(out_sent)
        small, got = tie((small, got, out_sent))[:2]
        small = small + got
        small = small + hop(small, 1)
        got = hop(small, 2)
        at_ra, at_rb, got, small, ff_got = tie((at_ra, at_rb, got, small, ff_got))
        at, total, *sends = fold_two(at_ka, at_ra, at_kb, at_rb, small, got)
        gots = [hop(sends[e], 4 * (e + 1)) for e in range(3)]
        out_got = tie((out_got, at))[0]
        (output,) = once(join_body, (sds((HALF, D)),), (out_stay, out_got), "join", scalars=0)
        grad_in, grad_out = once(
            finish_ff_body, (sds((r, ff), F32),) * 2, (ff_own, ff_got), "finish_ff", scalars=0
        )
        gots = tie((*gots, output, grad_in))[:3]
        grad_q, grad_v, grad_k, grad_o, *sums = once(
            finish_body, (part,) * 4 + small_outs, (at, total, *gots), "finish", scalars=0
        )
    else:
        grad_qk, grad_vo = scatter_plain(*qk), scatter_plain(*vo)
        grad_ffn = scatter_plain(ka, sa, kb, sb)
        grad_q, grad_k, grad_v, grad_o = grad_qk[:, :HI], grad_qk[:, HI:], grad_vo[:, :HI], grad_vo[:, HI:]
        grad_in, grad_out = grad_ffn[:, ff:], grad_ffn[:, :ff]
        sums = once(split_small_body, small_outs, (sum_all(small),), "split_small", scalars=0)
        out_stay, out_sent = once(
            output_body, (sds((BLK, D)), sds((BLK, D))), (mid, out_own, got_out), "output", scalars=0
        )
        output = jnp.concatenate([out_stay, swap(out_sent)], axis=0)
    return (
        output, grad_tokens, sums[0], grad_q, grad_k, grad_v, sums[2], sums[3],
        grad_o.T, sums[1], grad_in, grad_out.T,
    )


def solution(mesh):
    rows = P(("dp", "tensor"), None)
    w, wt = P("dp", "tensor"), P("tensor", "dp")
    return jax.shard_map(
        on_device,
        mesh=mesh,
        in_specs=(rows, rows, P("dp"), P(), w, w, w, P(), P(), wt, P(), w, wt),
        out_specs=(rows, rows, P(), w, w, w, P(), P(), wt, P(), w, wt),
        check_vma=False,
    )
```

```python
import math

import jax
import jax.numpy as jnp
from jax import lax
from jax.experimental import pallas as pl
from jax.experimental.pallas import tpu as pltpu
from jax.sharding import PartitionSpec as P

HEADS = 12
HD = 64
INNER = 768
HI = INNER // 2
SEQ = 1024
HALF = SEQ // 2
BLK = 256
EPSILON = 1e-06
LOG2E = 1.4426950408889634
BF = jnp.bfloat16
F32 = jnp.float32
HB1, HB2, HB3, HB4 = 3, 3, 3, 3
FT = 512
PART = 256


def dot(a, b):
    return jnp.dot(a, b, preferred_element_type=F32)


def dot_nt(a, b):
    return lax.dot_general(a, b, (((1,), (1,)), ((), ())), preferred_element_type=F32)


def smem():
    return pl.BlockSpec(memory_space=pltpu.SMEM)


def whole():
    return pl.BlockSpec(memory_space=pltpu.VMEM)


def full(s):
    return pl.BlockSpec(s, lambda *i: (0,) * len(s))


def params(mib=24):
    return pltpu.CompilerParams(vmem_limit_bytes=mib * 1024 * 1024)


def cost(flops, moved, exps=0):
    return pl.CostEstimate(flops=int(flops), bytes_accessed=int(moved), transcendentals=int(exps))


def sds(shape, dtype=BF):
    return jax.ShapeDtypeStruct(shape, dtype)


def once(body, outs, args, name, scalars=1, scratch=(), flops=0, moved=None):
    if moved is None:
        moved = sum(math.prod(a.shape) * a.dtype.itemsize for a in (*args, *outs))
    return pl.pallas_call(
        body,
        in_specs=[smem()] * scalars + [whole()] * (len(args) - scalars),
        out_specs=[whole()] * len(outs),
        out_shape=list(outs),
        scratch_shapes=list(scratch),
        compiler_params=params(),
        cost_estimate=cost(flops, moved),
        name=name,
    )(*args)


def per_core(ids_ref, run):
    for c in range(2):
        pl.when(ids_ref[0] == c)(lambda c=c: run(c))


def head(c, i):
    return (i + c * (HEADS // 2)) % HEADS


def spread(rep_ref, row, values):
    for g, value in enumerate(values):
        rep_ref[row : row + 1, g * HD : (g + 1) * HD] = jnp.full((1, HD), value, F32)


def hbm(shape, dtype=BF):
    return pltpu.HBM(shape, dtype)


def far(v):
    return pltpu.with_memory_space_constraint(v, pltpu.HBM)


def chunks(c):
    return (1, 4) if c == 0 else (3, 2)


def blocks_of(c):
    return (0, 3) if c == 0 else (2, 1)


def logits_body(ids_ref, pre_ref, seg_ref, k_ref, qT_ref, pT_ref, mask_ref):
    step = pl.program_id(0)

    def run(c):
        nj, bl = chunks(c), blocks_of(c)
        base = (0, nj[0] * BLK)

        @pl.when(step == 0)
        def _():
            seg = seg_ref[...].astype(F32)
            down = jnp.broadcast_to(seg, (8, SEQ)).T[:, :1]
            for b in range(2):
                qpos = lax.broadcasted_iota(jnp.int32, (BLK, BLK), 1) + bl[b] * BLK
                qseg = seg[:, bl[b] * BLK : (bl[b] + 1) * BLK]
                for j in range(nj[b]):
                    kpos = lax.broadcasted_iota(jnp.int32, (BLK, BLK), 0) + j * BLK
                    ok = (kpos <= qpos) & (down[j * BLK : (j + 1) * BLK] == qseg)
                    at = base[b] + j * BLK
                    mask_ref[at : at + BLK, :] = jnp.where(ok, 0.0, -1e30)

        for hh in range(HB1):
            h = step * HB1 + hh
            scale = [pre_ref[h, head(c, g)] * (0.125 * LOG2E) for g in range(HEADS)]
            for b in range(2):
                n = nj[b] * BLK
                qs = jnp.concatenate(
                    [
                        (
                            qT_ref[g * HD : (g + 1) * HD, b * BLK : (b + 1) * BLK].astype(F32)
                            * scale[g]
                        ).astype(BF)
                        for g in range(HEADS)
                    ],
                    axis=0,
                )
                s = dot(k_ref[:n, :], qs) + mask_ref[base[b] : base[b] + n, :]
                m = jnp.max(s, axis=0, keepdims=True)
                e = jnp.exp2(s - m)
                inv = 1.0 / jnp.sum(e, axis=0, keepdims=True)
                pT_ref[base[b] : base[b] + n, hh * BLK : (hh + 1) * BLK] = (e * inv).astype(BF)

    per_core(ids_ref, run)


def logits_softmax(ids, pre, seg, k, qT):
    return pl.pallas_call(
        logits_body,
        grid=(HEADS // HB1,),
        in_specs=[smem(), smem(), full((1, SEQ)), full((SEQ, INNER)), full((INNER, HALF))],
        out_specs=pl.BlockSpec((5 * BLK, HB1 * BLK), lambda h: (0, h)),
        out_shape=hbm((5 * BLK, HEADS * BLK)),
        scratch_shapes=[pltpu.VMEM((5 * BLK, BLK), F32)],
        compiler_params=params(),
        cost_estimate=cost(6.04e9, 10e6, 4e6),
        name="logits_softmax",
    )(ids, pre, seg, k, qT)


def attend_body(ids_ref, post_ref, vT_ref, pT_ref, uT_ref, h_ref, acc_ref):
    step = pl.program_id(0)

    def run(c):
        nj = chunks(c)
        base = (0, nj[0] * BLK)
        for b in range(2):
            n = nj[b] * BLK
            cs = slice(b * BLK, (b + 1) * BLK)
            us = []
            for hh in range(HB2):
                u = dot(vT_ref[:, :n], pT_ref[base[b] : base[b] + n, hh * BLK : (hh + 1) * BLK])
                uT_ref[hh * INNER : (hh + 1) * INNER, cs] = u.astype(BF)
                us.append(u)
            for k in range(HEADS):
                rs = slice(k * HD, (k + 1) * HD)
                t = us[0][rs, :] * post_ref[head(c, k), step * HB2]
                for hh in range(1, HB2):
                    t = t + us[hh][rs, :] * post_ref[head(c, k), step * HB2 + hh]
                acc_ref[rs, cs] += t

    @pl.when(step == 0)
    def _():
        acc_ref[...] = jnp.zeros_like(acc_ref)

    per_core(ids_ref, run)

    @pl.when(step == HEADS // HB2 - 1)
    def _():
        h_ref[...] = acc_ref[...].T.astype(BF)


def attend(ids, post, vT, pT):
    return pl.pallas_call(
        attend_body,
        grid=(HEADS // HB2,),
        in_specs=[smem(), smem(), full((INNER, SEQ)), pl.BlockSpec((5 * BLK, HB2 * BLK), lambda h: (0, h))],
        out_specs=[pl.BlockSpec((HB2 * INNER, HALF), lambda h: (h, 0)), full((HALF, INNER))],
        out_shape=[hbm((HEADS * INNER, HALF)), sds((HALF, INNER))],
        scratch_shapes=[pltpu.VMEM((INNER, HALF), F32)],
        compiler_params=params(),
        cost_estimate=cost(6.04e9, 20e6),
        name="attend",
    )(ids, post, vT, far(pT))


def split_rows(c, acc_ref, own_ref, oth_ref):
    for d in range(2):
        src = slice((c ^ d) * HALF, (c ^ d) * HALF + HALF)
        dst = slice(d * HALF, (d + 1) * HALF)
        own_ref[dst, :] = acc_ref[src, :HI].astype(BF)
        oth_ref[dst, :] = acc_ref[src, HI:].astype(BF)


def keep_sum(ref, h, k, b, g):
    g = g[:, :128] + g[:, 128:]
    ref[h, k : k + 1, :] = g if b == 0 else ref[h, k : k + 1, :] + g


def attend_back_body(
    ids_ref, post_ref, v_ref, ghT_ref, gh_ref, pT_ref, uT_ref,
    gL_ref, own_ref, oth_ref, gpost_ref, acc_ref, rep_ref,
):
    step = pl.program_id(0)

    def run(c):
        nj = chunks(c)
        base = (0, nj[0] * BLK)
        for hh in range(HB3):
            spread(rep_ref, hh, [post_ref[head(c, k), step * HB3 + hh] for k in range(HEADS)])
        for b in range(2):
            n = nj[b] * BLK
            cs = slice(b * BLK, (b + 1) * BLK)
            g2s = []
            for hh in range(HB3):
                h = step * HB3 + hh
                hs = slice(hh * BLK, (hh + 1) * BLK)
                r = jnp.zeros((1, BLK), F32)
                parts = []
                for k in range(HEADS):
                    gk = ghT_ref[k * HD : (k + 1) * HD, cs].astype(F32)
                    u = uT_ref[hh * INNER + k * HD : hh * INNER + (k + 1) * HD, cs].astype(F32)
                    g = jnp.sum(gk * u, axis=0, keepdims=True)
                    w = post_ref[head(c, k), h]
                    keep_sum(gpost_ref, hh, head(c, k), b, g)
                    r = r + g * w
                    parts.append((gk * w).astype(BF))
                gP = dot(v_ref[:n, :], jnp.concatenate(parts, axis=0))
                p = pT_ref[base[b] : base[b] + n, hs]
                gL_ref[base[b] : base[b] + n, hs] = (p.astype(F32) * (gP - r)).astype(BF)
                g2s.append((gh_ref[cs, :].astype(F32) * rep_ref[hh : hh + 1, :]).astype(BF))
            acc_ref[:n, :] += dot(pT_ref[base[b] : base[b] + n, :], jnp.concatenate(g2s, axis=0))

        @pl.when(step == HEADS // HB3 - 1)
        def _():
            split_rows(c, acc_ref, own_ref, oth_ref)

    @pl.when(step == 0)
    def _():
        acc_ref[...] = jnp.zeros_like(acc_ref)

    per_core(ids_ref, run)


def attend_back(ids, post, v, ghT, gh, pT, uT):
    return pl.pallas_call(
        attend_back_body,
        grid=(HEADS // HB3,),
        in_specs=[
            smem(), smem(), full((SEQ, INNER)), full((INNER, HALF)), full((HALF, INNER)),
            pl.BlockSpec((5 * BLK, HB3 * BLK), lambda h: (0, h)),
            pl.BlockSpec((HB3 * INNER, HALF), lambda h: (h, 0)),
        ],
        out_specs=[
            pl.BlockSpec((5 * BLK, HB3 * BLK), lambda h: (0, h)),
            full((SEQ, HI)), full((SEQ, HI)),
            pl.BlockSpec((HB3, HEADS, 128), lambda h: (h, 0, 0)),
        ],
        out_shape=[
            hbm((5 * BLK, HEADS * BLK)), sds((SEQ, HI)), sds((SEQ, HI)),
            hbm((HEADS, HEADS, 128), F32),
        ],
        scratch_shapes=[pltpu.VMEM((SEQ, INNER), F32), pltpu.VMEM((8, INNER), F32)],
        compiler_params=params(),
        cost_estimate=cost(12.1e9, 30e6),
        name="attend_back",
    )(ids, post, v, ghT, gh, far(pT), far(uT))


def scores_back_body(
    ids_ref, pre_ref, kT_ref, qT_ref, q_ref, gL_ref,
    gqa_ref, gqb_ref, own_ref, oth_ref, gpre_ref, accq_ref, acck_ref, rep_ref,
):
    step = pl.program_id(0)

    def run(c):
        nj = chunks(c)
        base = (0, nj[0] * BLK)
        scale = [
            [pre_ref[step * HB4 + hh, head(c, g)] * 0.125 for g in range(HEADS)] for hh in range(HB4)
        ]
        for hh in range(HB4):
            spread(rep_ref, hh, scale[hh])
        for b in range(2):
            n = nj[b] * BLK
            cs = slice(b * BLK, (b + 1) * BLK)
            ws, q2s = [], []
            for hh in range(HB4):
                ws.append(dot(kT_ref[:, :n], gL_ref[base[b] : base[b] + n, hh * BLK : (hh + 1) * BLK]))
                q2s.append((q_ref[cs, :].astype(F32) * rep_ref[hh : hh + 1, :]).astype(BF))
            for k in range(HEADS):
                rs = slice(k * HD, (k + 1) * HD)
                qk = qT_ref[rs, cs].astype(F32)
                t = None
                for hh in range(HB4):
                    w = ws[hh][rs, :]
                    g = jnp.sum(qk * w, axis=0, keepdims=True) * 0.125
                    keep_sum(gpre_ref, hh, head(c, k), b, g)
                    u = w * scale[hh][k]
                    t = u if t is None else t + u
                accq_ref[rs, cs] += t
            acck_ref[:n, :] += dot(gL_ref[base[b] : base[b] + n, :], jnp.concatenate(q2s, axis=0))

        @pl.when(step == HEADS // HB4 - 1)
        def _():
            split_rows(c, acck_ref, own_ref, oth_ref)

    @pl.when(step == 0)
    def _():
        accq_ref[...] = jnp.zeros_like(accq_ref)
        acck_ref[...] = jnp.zeros_like(acck_ref)

    per_core(ids_ref, run)

    @pl.when(step == HEADS // HB4 - 1)
    def _():
        gqa_ref[...] = accq_ref[:HI, :].T.astype(BF)
        gqb_ref[...] = accq_ref[HI:, :].T.astype(BF)


def scores_back(ids, pre, kT, qT, q, gL):
    return pl.pallas_call(
        scores_back_body,
        grid=(HEADS // HB4,),
        in_specs=[
            smem(), smem(), full((INNER, SEQ)), full((INNER, HALF)), full((HALF, INNER)),
            pl.BlockSpec((5 * BLK, HB4 * BLK), lambda h: (0, h)),
        ],
        out_specs=[
            full((HALF, HI)), full((HALF, HI)), full((SEQ, HI)), full((SEQ, HI)),
            pl.BlockSpec((HB4, HEADS, 128), lambda h: (h, 0, 0)),
        ],
        out_shape=[
            sds((HALF, HI)), sds((HALF, HI)), sds((SEQ, HI)), sds((SEQ, HI)),
            sds((HEADS, HEADS, 128), F32),
        ],
        scratch_shapes=[
            pltpu.VMEM((INNER, HALF), F32), pltpu.VMEM((SEQ, INNER), F32), pltpu.VMEM((8, INNER), F32),
        ],
        compiler_params=params(),
        cost_estimate=cost(12.1e9, 14e6),
        name="scores_back",
    )(ids, pre, kT, qT, q, far(gL))


def own_rows(loc, oth):
    return jnp.concatenate([loc[:BLK], oth[BLK:]], axis=0)


def project_qk_body(ids_ref, loc_ref, oth_ref, wa_ref, wb_ref, q_ref, qT_ref, k_ref, kT_ref):
    own = own_rows(loc_ref[...], oth_ref[...])
    for i, w in enumerate((wa_ref, wb_ref)):
        t = dot(own, w[:, :HI])
        cs = slice(i * HI, (i + 1) * HI)
        q_ref[:, cs] = t.astype(BF)
        qT_ref[cs, :] = t.T.astype(BF)
    project_rows(ids_ref, loc_ref, oth_ref, wa_ref, wb_ref, HI, k_ref, kT_ref)


def project_v_body(ids_ref, loc_ref, oth_ref, wa_ref, wb_ref, v_ref, vT_ref):
    project_rows(ids_ref, loc_ref, oth_ref, wa_ref, wb_ref, 0, v_ref, vT_ref)


def project_rows(ids_ref, loc_ref, oth_ref, wa_ref, wb_ref, col, k_ref, kT_ref):
    for d, rows in enumerate((loc_ref, oth_ref)):
        at = pl.multiple_of(lax.bitwise_xor(ids_ref[0], d) * HALF, HALF)
        for i, w in enumerate((wa_ref, wb_ref)):
            t = dot(rows[...], w[:, col : col + HI])
            cs = slice(i * HI, (i + 1) * HI)
            k_ref[pl.ds(at, HALF), cs] = t.astype(BF)
            kT_ref[cs, pl.ds(at, HALF)] = t.T.astype(BF)


def norm(v):
    inv = lax.rsqrt(jnp.mean(v * v, axis=-1, keepdims=True) + EPSILON)
    return v * inv, inv


def cast_body(q_ref, k_ref, v_ref, o_ref, in_ref, out_ref, qk_ref, vo_ref, ff_ref):
    qk_ref[:, :HI] = q_ref[...].astype(BF)
    qk_ref[:, HI:] = k_ref[...].astype(BF)
    vo_ref[:, :HI] = v_ref[...].astype(BF)
    vo_ref[:, HI:INNER] = o_ref[...].astype(BF)
    ff = in_ref.shape[1]
    ff_ref[:, :ff] = in_ref[...].astype(BF)
    ff_ref[:, ff:] = out_ref[:, : ff - PART].astype(BF)
    vo_ref[:, INNER:] = out_ref[:, ff - PART :].astype(BF)


def prepare_body(
    x_ref, xo_ref, c_ref, co_ref, gain_ref,
    loc_ref, oth_ref, actT_ref, own_ref, cown_ref, crest_ref, cT_ref,
):
    for src, dst, cs in ((x_ref, loc_ref, slice(0, HALF)), (xo_ref, oth_ref, slice(HALF, SEQ))):
        act = norm(src[...].astype(F32))[0] * gain_ref[...]
        dst[...] = act.astype(BF)
        actT_ref[:, cs] = act.T.astype(BF)
    own_ref[:BLK, :] = x_ref[:BLK, :]
    own_ref[BLK:, :] = xo_ref[BLK:, :]
    for dst, a, b, at in ((cown_ref, c_ref, co_ref, 0), (crest_ref, co_ref, c_ref, HALF)):
        dst[:BLK, :] = a[:BLK, :]
        dst[BLK:, :] = b[BLK:, :]
        cT_ref[:, at : at + BLK] = a[:BLK, :].astype(F32).T.astype(BF)
        cT_ref[:, at + BLK : at + HALF] = b[BLK:, :].astype(F32).T.astype(BF)


def middle_body(x_ref, h_ref, wa_ref, wb_ref, gain_ref, mid_ref, act_ref, actT_ref):
    mid = x_ref[...].astype(F32) + dot_nt(h_ref[:, :HI], wa_ref[:, HI:]) + dot_nt(h_ref[:, HI:], wb_ref[:, HI:])
    act = norm(mid)[0] * gain_ref[...]
    mid_ref[...] = mid
    act_ref[...] = act.astype(BF)
    actT_ref[...] = act.T.astype(BF)


def emit(me, scr_ref, cols, keep_ref, send_ref, outer_x):
    for e in range(16):
        x, y, z = e & 1, (e >> 1) & 1, e >> 2
        if me is None:
            ref, at, row = (keep_ref, send_ref)[e >> 3], e & 7, e * 48
        else:
            first, second = (x, y) if outer_x else (y, x)
            ref, at = (keep_ref, send_ref)[first], second * 4 + z
            row = pl.multiple_of(lax.bitwise_xor(me, e) * 48, 16)
        ref[at, :, cols] = scr_ref[pl.ds(row, 48), cols].astype(BF)


def gates(v):
    sq = v * v
    s = 0.5 * jnp.tanh(v * (0.7978845608028654 + 0.035677408136300125 * sq)) + 0.5
    slope = s + v * (1.5957691216057308 + 0.21406444881780075 * sq) * (s - s * s)
    return (v * s).astype(BF), slope


def ffn_body(
    xor, ids_ref, aown_ref, aoth_ref, aTown_ref, aToth_ref, cown_ref, coth_ref, cT_ref,
    win_ref, wouta_ref, woutb_ref, part_ref, outa_ref, outb_ref, gaa_ref, gab_ref, ka_ref, sa_ref, kb_ref, sb_ref,
    acco_ref, accg_ref, scr_ref,
):
    step = pl.program_id(0)
    last = pl.num_programs(0) - 1
    me = ids_ref[1] if xor else None

    @pl.when(step == 0)
    def _():
        acco_ref[...] = jnp.zeros_like(acco_ref)
        accg_ref[...] = jnp.zeros_like(accg_ref)

    win = win_ref[...]
    wout = jnp.concatenate(
        [wouta_ref[...], jnp.where(step == last, part_ref[...], woutb_ref[...])], axis=1
    )
    v0, v1 = dot(aown_ref[...], win), dot(aoth_ref[...], win)
    h0, s0 = gates(v0)
    g0 = dot(cown_ref[...], wout)
    h1, s1 = gates(v1)
    g1 = dot(coth_ref[...], wout)
    acco_ref[:HALF, :] += dot_nt(h0, wout)
    p0 = (g0.astype(BF).astype(F32) * s0).astype(BF)
    acco_ref[HALF:, :] += dot_nt(h1, wout)
    p1 = (g1.astype(BF).astype(F32) * s1).astype(BF)
    accg_ref[:HALF, :] += dot_nt(p0, win)
    accg_ref[HALF:, :] += dot_nt(p1, win)
    hid, gpre = (h0, h1), (p0, p1)
    scr_ref[...] = dot(cT_ref[:, :HALF], hid[0]) + dot(cT_ref[:, HALF:], hid[1])
    emit(me, scr_ref, slice(0, FT), ka_ref, sa_ref, True)
    scr_ref[...] = dot(aTown_ref[...], gpre[0]) + dot(aToth_ref[...], gpre[1])
    emit(me, scr_ref, slice(0, FT), kb_ref, sb_ref, False)

    @pl.when(step == last)
    def _():
        outa_ref[...] = acco_ref[:HALF, :]
        outb_ref[...] = acco_ref[HALF:, :].astype(BF)
        gaa_ref[...] = accg_ref[:HALF, :]
        gab_ref[...] = accg_ref[HALF:, :].astype(BF)


def ffn(xor, ids, aown, aoth, aTown, aToth, cown, coth, cT, w, part):
    width = (w.shape[1] + PART) // 2
    steps = width // FT
    tile = pl.BlockSpec((INNER, FT), lambda t: (0, t))
    end = w.shape[1] // PART - 1
    tile2 = pl.BlockSpec((INNER, PART), lambda t: (0, 2 * (steps + t)))
    tile3 = pl.BlockSpec((INNER, PART), lambda t: (0, jnp.minimum(2 * (steps + t) + 1, end)))
    grad = pl.BlockSpec((8, 48, FT), lambda t: (0, 0, t))
    half, halfT = full((HALF, INNER)), full((INNER, HALF))
    return pl.pallas_call(
        lambda *r: ffn_body(xor, *r),
        grid=(steps,),
        in_specs=[smem(), half, half, halfT, halfT, half, half, full((INNER, SEQ)), tile, tile2, tile3, full((INNER, PART))],
        out_specs=[half, half, half, half, grad, grad, grad, grad],
        out_shape=[
            sds((HALF, INNER), F32), sds((HALF, INNER)), sds((HALF, INNER), F32), sds((HALF, INNER)),
        ] + [sds((8, 48, width))] * 4,
        scratch_shapes=[
            pltpu.VMEM((SEQ, INNER), F32), pltpu.VMEM((SEQ, INNER), F32), pltpu.VMEM((INNER, FT), F32),
        ],
        compiler_params=params(44),
        cost_estimate=cost(14.5e9, 20e6, 1.6e6),
        name="ffn",
    )(ids, aown, aoth, aTown, aToth, cown, coth, cT, w, w, w, part)


def middle_back_body(
    ga_ref, gr_ref, mid_ref, cot_ref, gain_ref, h_ref, wa_ref, wb_ref,
    stay_ref, sent_ref, gh_ref, ghT_ref, gain_out, gwa_ref, gwb_ref,
):
    ga = ga_ref[...] + gr_ref[...].astype(F32)
    normed, inv = norm(mid_ref[...])
    scaled = ga * gain_ref[...]
    gm = cot_ref[...].astype(F32) + inv * (
        scaled - normed * jnp.mean(scaled * normed, axis=-1, keepdims=True)
    )
    gain_out[...] = jnp.sum(ga * normed, axis=0, keepdims=True)
    stay_ref[...] = gm[:BLK]
    sent_ref[...] = gm[BLK:]
    grad = gm.astype(BF)
    gT = gm.T.astype(BF)
    for i, (w, gw) in enumerate(((wa_ref, gwa_ref), (wb_ref, gwb_ref))):
        cs = slice(i * HI, (i + 1) * HI)
        t = dot(grad, w[:, HI:])
        gh_ref[:, cs] = t.astype(BF)
        ghT_ref[cs, :] = t.T.astype(BF)
        gw[...] = dot(gT, h_ref[:, cs]).astype(BF)


def joined(own, got):
    a, b = own.astype(F32), got.astype(F32)
    return jnp.concatenate([a[:HALF] + b[HALF:], a[HALF:] + b[:HALF]], axis=0).astype(BF)


def grad_vo_body(xor, ids_ref, aT_ref, gv_ref, rv_ref, go_ref, ro_ref, gv_out, ka, sa, kb, sb, scr):
    me = ids_ref[1] if xor else None
    gv = joined(gv_ref[...], rv_ref[...])
    gv_out[...] = gv
    scr[...] = dot(aT_ref[...], gv)
    emit(me, scr, slice(0, HI), ka, sa, True)
    scr[...] = go_ref[...].astype(F32) + ro_ref[...].astype(F32)
    emit(me, scr, slice(0, HI), kb, sb, False)


def grad_qk_body(xor, ids_ref, aT_ref, gq_ref, rq_ref, gk_ref, rk_ref, gq_out, gk_out, ka, sa, kb, sb, scr):
    me = ids_ref[1] if xor else None
    gq, rq = gq_ref[...], rq_ref[...]
    gq = jnp.concatenate([gq[:BLK], rq[BLK:], rq[:BLK], gq[BLK:]], axis=0)
    gq_out[...] = gq
    scr[...] = dot(aT_ref[...], gq)
    emit(me, scr, slice(0, HI), ka, sa, True)
    gk = joined(gk_ref[...], rk_ref[...])
    gk_out[...] = gk
    scr[...] = dot(aT_ref[...], gk)
    emit(me, scr, slice(0, HI), kb, sb, False)


def act_back_body(gq_ref, gk_ref, gv_ref, qk_ref, vo_ref, loc_ref, oth_ref):
    for rs, ref in ((slice(0, HALF), loc_ref), (slice(HALF, SEQ), oth_ref)):
        t = dot_nt(gq_ref[rs, :], qk_ref[:, :HI]) + dot_nt(gk_ref[rs, :], qk_ref[:, HI:])
        ref[...] = (t + dot_nt(gv_ref[rs, :], vo_ref[:, :HI])).astype(ref.dtype)


def output_body(mid_ref, own_ref, got_ref, stay_ref, sent_ref):
    out = (mid_ref[...] + own_ref[...] + got_ref[...].astype(F32)).astype(BF)
    stay_ref[...] = out[:BLK]
    sent_ref[...] = out[BLK:]


def join_body(stay_ref, got_ref, out_ref):
    out_ref[:BLK, :] = stay_ref[...]
    out_ref[BLK:, :] = got_ref[...]


def tokens_back_body(
    ga_ref, gr_ref, x_ref, gain_ref, stay_ref, got_ref, gain2_ref, gpre_ref, gpost_ref,
    out_ref, small_ref,
):
    ga = ga_ref[...] + gr_ref[...].astype(F32)
    normed, inv = norm(x_ref[...].astype(F32))
    scaled = ga * gain_ref[...]
    back = inv * (scaled - normed * jnp.mean(scaled * normed, axis=-1, keepdims=True))
    out_ref[:BLK, :] = (stay_ref[...] + back[:BLK]).astype(BF)
    out_ref[BLK:, :] = (got_ref[...] + back[BLK:]).astype(BF)
    gain1 = jnp.sum(ga * normed, axis=0, keepdims=True)
    small_ref[...] = jnp.zeros_like(small_ref)
    for i in range(6):
        cs = slice(i * 128, (i + 1) * 128)
        small_ref[i : i + 1, :] = gain1[:, cs]
        small_ref[8 + i : 9 + i, :] = gain2_ref[:, cs]
    small_ref[16 : 16 + HEADS, :HEADS] = jnp.sum(gpre_ref[...], axis=-1)
    small_ref[32 : 32 + HEADS, :HEADS] = jnp.sum(gpost_ref[...], axis=-1)


def swap(v):
    return lax.ppermute(v, "tensor", [(0, 1), (1, 0)])


def hop(v, mask):
    n = lax.axis_size("dp")
    return lax.ppermute(v, "dp", [(i, i ^ mask) for i in range(n)])


def after(v, *done):
    return lax.optimization_barrier((v, *done))[0]


def place_body(ids_ref, ax, ay, bx, by, *outs):
    me = ids_ref[1]
    w = ax.shape[3]
    for t, ref in enumerate((ax, ay, bx, by)):
        col = (t // 2) * w
        for i in range(2):
            for j in range(4):
                e = 4 * j + ((2 * i + t) if t < 2 else (i + 2 * (t - 2)))
                row = pl.multiple_of(lax.bitwise_xor(me, e) * 48, 16)
                start = 0
                for out in outs:
                    end = start + out.shape[1]
                    lo, hi = max(col, start), min(col + w, end)
                    if lo < hi:
                        out[pl.ds(row, 48), lo - start : hi - start] = ref[i, j, :, lo - col : hi - col]
                    start = end


def gather_z(shard):
    return [shard] + [hop(shard, 4 * e) for e in range(1, 4)]


def gather_one(pieces):
    z = jnp.stack(pieces, axis=0)
    w = z.shape[2] // 2
    a, b = z[:, :, :w], z[:, :, w:]
    return a, hop(a, 2), b, hop(b, 1)


def gather_two(a, ra, b, rb):
    a2, b2 = jnp.stack([a, ra], axis=0), jnp.stack([b, rb], axis=0)
    return a2, hop(a2, 1), b2, hop(b2, 2)


def gathered(ids, parts, *outs):
    return once(place_body, outs, (ids, *parts), "place")


def fold_one_body(ka, ra, kb, rb, oka, osa, okb, osb):
    for k, r, keep, send in ((ka, ra, oka, osa), (kb, rb, okb, osb)):
        t = (k[...].astype(F32) + r[...].astype(F32)).astype(BF)
        keep[...] = t[:4]
        send[...] = t[4:]


def fold_two_body(ka, ra, kb, rb, small, got, own, total, *sends):
    w = ka.shape[2]
    for k, r, cs in ((ka, ra, slice(0, w)), (kb, rb, slice(w, 2 * w))):
        t = k[...].astype(F32) + r[...].astype(F32)
        own[:, cs] = t[0]
        for e in range(3):
            sends[e][:, cs] = t[e + 1].astype(BF)
    v = small[...] + got[...]
    total[...] = v
    for send in sends:
        send[:, 2 * w :] = v.astype(BF)


def fold_one(ka, ra, kb, rb):
    piece = sds((4,) + ka.shape[1:])
    return once(fold_one_body, (piece,) * 4, (ka, ra, kb, rb), "fold_one", scalars=0)


def fold_two(*parts):
    w = 2 * parts[0].shape[2]
    outs = (sds((48, w), F32), sds((48, 128), F32)) + (sds((48, w + 128)),) * 3
    return once(fold_two_body, outs, parts, "fold_two", scalars=0)


def fold_ff_body(ka, ra, kb, rb, own, send):
    w = ka.shape[2]
    for k, r, cs in ((ka, ra, slice(0, w)), (kb, rb, slice(w, 2 * w))):
        t = (k[...].astype(F32) + r[...].astype(F32)).astype(BF)
        for z in range(2):
            own[z, :, cs] = t[2 * z]
            send[z, :, cs] = t[2 * z + 1]


def fold_at_body(*refs):
    ins, outs = refs[:8], refs[8:]
    for i in range(4):
        k, r = ins[2 * i], ins[2 * i + 1]
        kept, sent = outs[2 * (i // 2)], outs[2 * (i // 2) + 1]
        cs = slice((i % 2) * HI, (i % 2) * HI + HI)
        t = (k[...].astype(F32) + r[...].astype(F32)).astype(BF)
        kept[:, :, cs] = t[:4]
        sent[:, :, cs] = t[4:]


def fold_ff_two_body(own, got, keep, send):
    t = own[...].astype(F32) + got[...].astype(F32)
    keep[...] = t[0]
    send[...] = t[1].astype(BF)


def finish_ff_body(own, got, in_ref, out_ref):
    w = out_ref.shape[1]
    out_ref[...] = own[:, :w] + got[:, :w].astype(F32)
    in_ref[...] = own[:, w:] + got[:, w:].astype(F32)


def finish_body(own, total, a, b, c, *outs):
    def got(cs):
        return a[:, cs].astype(F32) + b[:, cs].astype(F32) + c[:, cs].astype(F32)

    for i, ref in enumerate(outs[:4]):
        cs = slice(i * HI, (i + 1) * HI)
        ref[...] = own[:, cs] + got(cs)
    at = 4 * HI
    split_small(total[...] + got(slice(at, at + 128)), *outs[4:])


def split_small(v, gain1, gain2, gpre, gpost):
    for i in range(6):
        gain1[i * 128 : (i + 1) * 128] = v[i]
        gain2[i * 128 : (i + 1) * 128] = v[8 + i]
    gpre[...] = v[16 : 16 + HEADS, :HEADS]
    gpost[...] = v[32:48].T[:HEADS, :HEADS]


def split_small_body(v, *outs):
    split_small(v[...], *outs)


def scatter_plain(ka, sa, kb, sb):
    w = ka.shape[2]
    flat = jnp.concatenate(
        [jnp.concatenate([k, s], axis=0).reshape(768, w) for k, s in ((ka, sa), (kb, sb))], axis=1
    )
    return lax.psum_scatter(flat.astype(F32), "dp", scatter_dimension=0, tiled=True)


def sum_all(v):
    n = lax.axis_size("dp")
    v = v + swap(v)
    bit = 1
    while bit < n:
        v = v + hop(v, bit)
        bit *= 2
    return v


def on_device(
    tokens, cotangent, segment_ids, norm1_gain, w_query, w_key, w_value, pre_mix, post_mix,
    w_output, norm2_gain, w_in, w_out,
):
    ids = jnp.stack([lax.axis_index("tensor"), lax.axis_index("dp")]).astype(jnp.int32)
    xor = lax.axis_size("dp") == 16
    low = lambda v: v.astype(BF)
    D = norm1_gain.shape[0]
    tie = lax.optimization_barrier
    gain1, gain2 = norm1_gain.reshape(1, D), norm2_gain.reshape(1, D)
    seg = segment_ids.reshape(1, SEQ)

    every = lambda v: lax.all_gather(v, "dp", axis=0, tiled=True)
    r, ff = w_in.shape
    shard_qk, shard_vo, shard_ff = once(
        cast_body, (sds((r, INNER)), sds((r, INNER + PART)), sds((r, 2 * ff - PART))),
        tuple(far(w) for w in (w_query, w_key, w_value, w_output.T, w_in, w_out.T)), "cast", scalars=0,
    )
    if xor:
        z_qk = gather_z(shard_qk)
    w_ff = every(shard_ff)
    x_oth, cot_oth = swap(tokens), swap(cotangent)
    act_loc, act_oth, actT, x_own, cot_own, cot_rest, cotT = once(
        prepare_body,
        (
            sds((HALF, D)), sds((HALF, D)), hbm((D, SEQ)), hbm((HALF, D)), hbm((HALF, D)),
            hbm((HALF, D)), hbm((D, SEQ)),
        ),
        (far(tokens), x_oth, far(cotangent), cot_oth, gain1), "prepare", scalars=0,
    )
    if xor:
        *z_qk, act_loc = tie((*z_qk, act_loc))
        a, ra, b, rb = gather_one(z_qk)
        z_vo = gather_z(after(shard_vo, *z_qk))
        qk_parts = gather_two(a, ra, b, rb)
        *z_vo, ax, ay, bx, by = tie((*z_vo, *qk_parts))
        a, ra, b, rb = gather_one(z_vo)
        (w_qk,) = gathered(ids, (ax, ay, bx, by), sds((D, INNER)))
    else:
        w_qk, w_vo = every(shard_qk), every(shard_vo)
        w_vo, w_part = w_vo[:, :INNER], w_vo[:, INNER:]
    q, qT, k, kT = once(
        project_qk_body,
        (hbm((HALF, INNER)), sds((INNER, HALF)), sds((SEQ, INNER)), hbm((INNER, SEQ))),
        (ids, act_loc, act_oth, w_qk, swap(w_qk)), "project_qk", flops=1.8e9,
    )
    if xor:
        ra, rb, k = tie((ra, rb, k))
        vo_parts = gather_two(a, ra, b, rb)
        k = after(k, vo_parts[0], vo_parts[2])
    pT = logits_softmax(ids, pre_mix, seg, k, qT)
    if xor:
        w_vo, w_part = gathered(ids, tie((*vo_parts, pT))[:4], sds((D, INNER)), hbm((D, PART)))
    vo_o = swap(w_vo)
    v, vT = once(
        project_v_body, (hbm((SEQ, INNER)), sds((INNER, SEQ))),
        (ids, act_loc, act_oth, w_vo, vo_o), "project_v", flops=1.2e9,
    )
    uT, heads = attend(ids, post_mix, vT, pT)
    mid, act2, act2T = once(
        middle_body, (hbm((HALF, D), F32), hbm((HALF, D)), hbm((D, HALF))),
        (x_own, heads, w_vo, vo_o, gain2), "middle", scalars=0, flops=6e8,
    )
    out_own, out_oth, ga_own, ga_oth, ka, sa, kb, sb = ffn(
        xor, ids, far(act2), far(swap(act2)), far(act2T), far(swap(act2T)), far(cot_own), far(cot_rest), far(cotT), far(w_ff), far(w_part)
    )
    if xor:
        ra, rb = hop(sa, 1), hop(sb, 2)
    stay, sent, gh, ghT, gain2_part, gwo, gwo_o = once(
        middle_back_body,
        (
            hbm((BLK, D), F32), hbm((BLK, D), F32), sds((HALF, INNER)), sds((INNER, HALF)),
            hbm((1, D), F32), sds((D, HI)), sds((D, HI)),
        ),
        (ga_own, swap(ga_oth), mid, cot_own, gain2, heads, w_vo, vo_o),
        "middle_back", scalars=0, flops=1.2e9,
    )
    got_sent, got_out, gwo_r = swap(sent), swap(out_oth), swap(gwo_o)
    gL, gv, gv_o, gpost = attend_back(ids, post_mix, v, ghT, gh, pT, uT)
    grads = (sds((8, 48, HI)),) * 4
    if xor:
        gv, gv_o, got_sent, got_out, gwo_r = tie((gv, gv_o, got_sent, got_out, gwo_r))
    gv, *vo = once(
        lambda *r: grad_vo_body(xor, *r), (hbm((SEQ, HI)),) + grads,
        (ids, actT, gv, swap(gv_o), gwo, gwo_r), "grad_vo",
        scratch=[pltpu.VMEM((D, HI), F32)], flops=6e8,
    )
    if xor:
        vo_ka, vo_sa, vo_kb, vo_sb = vo
        ra, rb = tie((ra, rb, vo_sa))[:2]
        ff_ka, ff_sa, ff_kb, ff_sb = fold_one(ka, ra, kb, rb)
        ff_ra, ff_rb = hop(ff_sa, 2), hop(ff_sb, 1)
        gL = after(gL, ff_sa, vo_sa)
    gq, gq_o, gk, gk_o, gpre = scores_back(ids, pre_mix, kT, qT, q, gL)
    if xor:
        ff_ra, ff_rb, gq, gq_o, gk_o = tie((ff_ra, ff_rb, gq, gq_o, gk_o))
        wide = ff_ka.shape[2] * 2
        ff_own, ff_send = once(
            fold_ff_body, (sds((2, 48, wide)),) * 2, (ff_ka, ff_ra, ff_kb, ff_rb), "fold_ff", scalars=0
        )
        ff_got = hop(ff_send, 4)
        vo_sa, vo_sb = tie((vo_sa, vo_sb, ff_send))[:2]
        vo_ra, vo_rb = hop(vo_sa, 1), hop(vo_sb, 2)
        gq, gk = tie((gq, gk, ff_send))[:2]
    gq, gk, *qk = once(
        lambda *r: grad_qk_body(xor, *r), (sds((SEQ, HI)),) * 2 + grads,
        (ids, actT, gq, swap(gq_o), gk, swap(gk_o)), "grad_qk",
        scratch=[pltpu.VMEM((D, HI), F32)], flops=1.2e9,
    )
    if xor:
        qk_ka, qk_sa, qk_kb, qk_sb = qk
        qk_ra, qk_rb = hop(qk_sa, 1), hop(qk_sb, 2)
        gq, vo_ra, vo_rb = tie((gq, vo_ra, vo_rb))
    ga_loc, ga_oth = once(
        act_back_body, (sds((HALF, D), F32), sds((HALF, D))), (gq, gk, gv, w_qk, w_vo),
        "act_back", scalars=0, flops=0.3e9, moved=1,
    )
    ga_got = swap(ga_oth)
    if xor:
        ff_own, ff_got = tie((ff_own, ff_got, ga_oth))[:2]
        ff_own, ff_send = once(
            fold_ff_two_body, (sds((48, wide), F32), sds((48, wide))), (ff_own, ff_got), "fold_ff_two", scalars=0,
            flops=2e9, moved=1,
        )
        ff_got = hop(ff_send, 8)
        qk_ra, qk_rb, ff_two = tie((qk_ra, qk_rb, ff_send))
        at_ka, at_sa, at_kb, at_sb = once(
            fold_at_body, (sds((4, 48, INNER)),) * 4,
            (qk_ka, qk_ra, vo_ka, vo_ra, qk_kb, qk_rb, vo_kb, vo_rb), "fold_at", scalars=0, flops=5e9,
        )
        at_ra, at_rb = hop(at_sa, 2), hop(at_sb, 1)
        ga_loc, ga_got = tie((ga_loc, ga_got, at_sa))[:2]
    grad_tokens, small = once(
        tokens_back_body, (sds((HALF, D)), sds((48, 128), F32)),
        (ga_loc, ga_got, tokens, gain1, stay, got_sent, gain2_part, gpre, gpost),
        "tokens_back", scalars=0,
    )
    r = w_in.shape[0]
    part = sds((r, HI), F32)
    small_outs = (sds((D,), F32),) * 2 + (sds((HEADS, HEADS), F32),) * 2
    if xor:
        got = swap(small)
        mid, small = tie((mid, small))
        out_stay, out_sent = once(
            output_body, (sds((BLK, D)), sds((BLK, D))), (mid, out_own, got_out), "output", scalars=0
        )
        out_got = swap(out_sent)
        small, got = tie((small, got, out_sent))[:2]
        small = small + got
        small = small + hop(small, 1)
        got = hop(small, 2)
        at_ra, at_rb, got, small, ff_got = tie((at_ra, at_rb, got, small, ff_got))
        at, total, *sends = fold_two(at_ka, at_ra, at_kb, at_rb, small, got)
        gots = [hop(sends[e], 4 * (e + 1)) for e in range(3)]
        out_got = tie((out_got, at))[0]
        (output,) = once(join_body, (sds((HALF, D)),), (out_stay, out_got), "join", scalars=0)
        grad_in, grad_out = once(
            finish_ff_body, (sds((r, ff), F32),) * 2, (ff_own, ff_got), "finish_ff", scalars=0
        )
        gots = tie((*gots, output, grad_in))[:3]
        grad_q, grad_v, grad_k, grad_o, *sums = once(
            finish_body, (part,) * 4 + small_outs, (at, total, *gots), "finish", scalars=0
        )
    else:
        grad_qk, grad_vo = scatter_plain(*qk), scatter_plain(*vo)
        grad_ffn = scatter_plain(ka, sa, kb, sb)
        grad_q, grad_k, grad_v, grad_o = grad_qk[:, :HI], grad_qk[:, HI:], grad_vo[:, :HI], grad_vo[:, HI:]
        grad_in, grad_out = grad_ffn[:, ff:], grad_ffn[:, :ff]
        sums = once(split_small_body, small_outs, (sum_all(small),), "split_small", scalars=0)
        out_stay, out_sent = once(
            output_body, (sds((BLK, D)), sds((BLK, D))), (mid, out_own, got_out), "output", scalars=0
        )
        output = jnp.concatenate([out_stay, swap(out_sent)], axis=0)
    return (
        output, grad_tokens, sums[0], grad_q, grad_k, grad_v, sums[2], sums[3],
        grad_o.T, sums[1], grad_in, grad_out.T,
    )


def solution(mesh):
    rows = P(("dp", "tensor"), None)
    w, wt = P("dp", "tensor"), P("tensor", "dp")
    return jax.shard_map(
        on_device,
        mesh=mesh,
        in_specs=(rows, rows, P("dp"), P(), w, w, w, P(), P(), wt, P(), w, wt),
        out_specs=(rows, rows, P(), w, w, w, P(), P(), wt, P(), w, wt),
        check_vma=False,
    )
```

```python
import math

import jax
import jax.numpy as jnp
from jax import lax
from jax.experimental import pallas as pl
from jax.experimental.pallas import tpu as pltpu
from jax.sharding import PartitionSpec as P

HEADS = 12
HD = 64
INNER = 768
HI = INNER // 2
SEQ = 1024
HALF = SEQ // 2
BLK = 256
EPSILON = 1e-06
LOG2E = 1.4426950408889634
BF = jnp.bfloat16
F32 = jnp.float32
HB1, HB2, HB3, HB4 = 3, 3, 3, 3
FT = 512
PART = 256


def dot(a, b):
    return jnp.dot(a, b, preferred_element_type=F32)


def dot_nt(a, b):
    return lax.dot_general(a, b, (((1,), (1,)), ((), ())), preferred_element_type=F32)


def smem():
    return pl.BlockSpec(memory_space=pltpu.SMEM)


def whole():
    return pl.BlockSpec(memory_space=pltpu.VMEM)


def full(s):
    return pl.BlockSpec(s, lambda *i: (0,) * len(s))


def params(mib=24):
    return pltpu.CompilerParams(vmem_limit_bytes=mib * 1024 * 1024)


def cost(flops, moved, exps=0):
    return pl.CostEstimate(flops=int(flops), bytes_accessed=int(moved), transcendentals=int(exps))


def sds(shape, dtype=BF):
    return jax.ShapeDtypeStruct(shape, dtype)


def once(body, outs, args, name, scalars=1, scratch=(), flops=0, moved=None):
    if moved is None:
        moved = sum(math.prod(a.shape) * a.dtype.itemsize for a in (*args, *outs))
    return pl.pallas_call(
        body,
        in_specs=[smem()] * scalars + [whole()] * (len(args) - scalars),
        out_specs=[whole()] * len(outs),
        out_shape=list(outs),
        scratch_shapes=list(scratch),
        compiler_params=params(),
        cost_estimate=cost(flops, moved),
        name=name,
    )(*args)


def per_core(ids_ref, run):
    for c in range(2):
        pl.when(ids_ref[0] == c)(lambda c=c: run(c))


def head(c, i):
    return (i + c * (HEADS // 2)) % HEADS


def spread(rep_ref, row, values):
    for g, value in enumerate(values):
        rep_ref[row : row + 1, g * HD : (g + 1) * HD] = jnp.full((1, HD), value, F32)


def hbm(shape, dtype=BF):
    return pltpu.HBM(shape, dtype)


def far(v):
    return pltpu.with_memory_space_constraint(v, pltpu.HBM)


def chunks(c):
    return (1, 4) if c == 0 else (3, 2)


def blocks_of(c):
    return (0, 3) if c == 0 else (2, 1)


def logits_body(ids_ref, pre_ref, seg_ref, k_ref, qT_ref, pT_ref, mask_ref):
    step = pl.program_id(0)

    def run(c):
        nj, bl = chunks(c), blocks_of(c)
        base = (0, nj[0] * BLK)

        @pl.when(step == 0)
        def _():
            seg = seg_ref[...].astype(F32)
            down = jnp.broadcast_to(seg, (8, SEQ)).T[:, :1]
            for b in range(2):
                qpos = lax.broadcasted_iota(jnp.int32, (BLK, BLK), 1) + bl[b] * BLK
                qseg = seg[:, bl[b] * BLK : (bl[b] + 1) * BLK]
                for j in range(nj[b]):
                    kpos = lax.broadcasted_iota(jnp.int32, (BLK, BLK), 0) + j * BLK
                    ok = (kpos <= qpos) & (down[j * BLK : (j + 1) * BLK] == qseg)
                    at = base[b] + j * BLK
                    mask_ref[at : at + BLK, :] = jnp.where(ok, 0.0, -1e30)

        for hh in range(HB1):
            h = step * HB1 + hh
            scale = [pre_ref[h, head(c, g)] * (0.125 * LOG2E) for g in range(HEADS)]
            for b in range(2):
                n = nj[b] * BLK
                qs = jnp.concatenate(
                    [
                        (
                            qT_ref[g * HD : (g + 1) * HD, b * BLK : (b + 1) * BLK].astype(F32)
                            * scale[g]
                        ).astype(BF)
                        for g in range(HEADS)
                    ],
                    axis=0,
                )
                s = dot(k_ref[:n, :], qs) + mask_ref[base[b] : base[b] + n, :]
                m = jnp.max(s, axis=0, keepdims=True)
                e = jnp.exp2(s - m)
                inv = 1.0 / jnp.sum(e, axis=0, keepdims=True)
                pT_ref[base[b] : base[b] + n, hh * BLK : (hh + 1) * BLK] = (e * inv).astype(BF)

    per_core(ids_ref, run)


def logits_softmax(ids, pre, seg, k, qT):
    return pl.pallas_call(
        logits_body,
        grid=(HEADS // HB1,),
        in_specs=[smem(), smem(), full((1, SEQ)), full((SEQ, INNER)), full((INNER, HALF))],
        out_specs=pl.BlockSpec((5 * BLK, HB1 * BLK), lambda h: (0, h)),
        out_shape=hbm((5 * BLK, HEADS * BLK)),
        scratch_shapes=[pltpu.VMEM((5 * BLK, BLK), F32)],
        compiler_params=params(),
        cost_estimate=cost(6.04e9, 10e6, 4e6),
        name="logits_softmax",
    )(ids, pre, seg, k, qT)


def attend_body(ids_ref, post_ref, vT_ref, pT_ref, uT_ref, h_ref, acc_ref):
    step = pl.program_id(0)

    def run(c):
        nj = chunks(c)
        base = (0, nj[0] * BLK)
        for b in range(2):
            n = nj[b] * BLK
            cs = slice(b * BLK, (b + 1) * BLK)
            us = []
            for hh in range(HB2):
                u = dot(vT_ref[:, :n], pT_ref[base[b] : base[b] + n, hh * BLK : (hh + 1) * BLK])
                uT_ref[hh * INNER : (hh + 1) * INNER, cs] = u.astype(BF)
                us.append(u)
            for k in range(HEADS):
                rs = slice(k * HD, (k + 1) * HD)
                t = us[0][rs, :] * post_ref[head(c, k), step * HB2]
                for hh in range(1, HB2):
                    t = t + us[hh][rs, :] * post_ref[head(c, k), step * HB2 + hh]
                acc_ref[rs, cs] += t

    @pl.when(step == 0)
    def _():
        acc_ref[...] = jnp.zeros_like(acc_ref)

    per_core(ids_ref, run)

    @pl.when(step == HEADS // HB2 - 1)
    def _():
        h_ref[...] = acc_ref[...].T.astype(BF)


def attend(ids, post, vT, pT):
    return pl.pallas_call(
        attend_body,
        grid=(HEADS // HB2,),
        in_specs=[smem(), smem(), full((INNER, SEQ)), pl.BlockSpec((5 * BLK, HB2 * BLK), lambda h: (0, h))],
        out_specs=[pl.BlockSpec((HB2 * INNER, HALF), lambda h: (h, 0)), full((HALF, INNER))],
        out_shape=[hbm((HEADS * INNER, HALF)), sds((HALF, INNER))],
        scratch_shapes=[pltpu.VMEM((INNER, HALF), F32)],
        compiler_params=params(),
        cost_estimate=cost(6.04e9, 20e6),
        name="attend",
    )(ids, post, vT, far(pT))


def split_rows(c, acc_ref, own_ref, oth_ref):
    for d in range(2):
        src = slice((c ^ d) * HALF, (c ^ d) * HALF + HALF)
        dst = slice(d * HALF, (d + 1) * HALF)
        own_ref[dst, :] = acc_ref[src, :HI].astype(BF)
        oth_ref[dst, :] = acc_ref[src, HI:].astype(BF)


def keep_sum(ref, h, k, b, g):
    g = g[:, :128] + g[:, 128:]
    ref[h, k : k + 1, :] = g if b == 0 else ref[h, k : k + 1, :] + g


def attend_back_body(
    ids_ref, post_ref, v_ref, ghT_ref, gh_ref, pT_ref, uT_ref,
    gL_ref, own_ref, oth_ref, gpost_ref, acc_ref, rep_ref,
):
    step = pl.program_id(0)

    def run(c):
        nj = chunks(c)
        base = (0, nj[0] * BLK)
        for hh in range(HB3):
            spread(rep_ref, hh, [post_ref[head(c, k), step * HB3 + hh] for k in range(HEADS)])
        for b in range(2):
            n = nj[b] * BLK
            cs = slice(b * BLK, (b + 1) * BLK)
            g2s = []
            for hh in range(HB3):
                h = step * HB3 + hh
                hs = slice(hh * BLK, (hh + 1) * BLK)
                r = jnp.zeros((1, BLK), F32)
                parts = []
                for k in range(HEADS):
                    gk = ghT_ref[k * HD : (k + 1) * HD, cs].astype(F32)
                    u = uT_ref[hh * INNER + k * HD : hh * INNER + (k + 1) * HD, cs].astype(F32)
                    g = jnp.sum(gk * u, axis=0, keepdims=True)
                    w = post_ref[head(c, k), h]
                    keep_sum(gpost_ref, hh, head(c, k), b, g)
                    r = r + g * w
                    parts.append((gk * w).astype(BF))
                gP = dot(v_ref[:n, :], jnp.concatenate(parts, axis=0))
                p = pT_ref[base[b] : base[b] + n, hs]
                gL_ref[base[b] : base[b] + n, hs] = (p.astype(F32) * (gP - r)).astype(BF)
                g2s.append((gh_ref[cs, :].astype(F32) * rep_ref[hh : hh + 1, :]).astype(BF))
            acc_ref[:n, :] += dot(pT_ref[base[b] : base[b] + n, :], jnp.concatenate(g2s, axis=0))

        @pl.when(step == HEADS // HB3 - 1)
        def _():
            split_rows(c, acc_ref, own_ref, oth_ref)

    @pl.when(step == 0)
    def _():
        acc_ref[...] = jnp.zeros_like(acc_ref)

    per_core(ids_ref, run)


def attend_back(ids, post, v, ghT, gh, pT, uT):
    return pl.pallas_call(
        attend_back_body,
        grid=(HEADS // HB3,),
        in_specs=[
            smem(), smem(), full((SEQ, INNER)), full((INNER, HALF)), full((HALF, INNER)),
            pl.BlockSpec((5 * BLK, HB3 * BLK), lambda h: (0, h)),
            pl.BlockSpec((HB3 * INNER, HALF), lambda h: (h, 0)),
        ],
        out_specs=[
            pl.BlockSpec((5 * BLK, HB3 * BLK), lambda h: (0, h)),
            full((SEQ, HI)), full((SEQ, HI)),
            pl.BlockSpec((HB3, HEADS, 128), lambda h: (h, 0, 0)),
        ],
        out_shape=[
            hbm((5 * BLK, HEADS * BLK)), sds((SEQ, HI)), sds((SEQ, HI)),
            hbm((HEADS, HEADS, 128), F32),
        ],
        scratch_shapes=[pltpu.VMEM((SEQ, INNER), F32), pltpu.VMEM((8, INNER), F32)],
        compiler_params=params(),
        cost_estimate=cost(12.1e9, 30e6),
        name="attend_back",
    )(ids, post, v, ghT, gh, far(pT), far(uT))


def scores_back_body(
    ids_ref, pre_ref, kT_ref, qT_ref, q_ref, gL_ref,
    gqa_ref, gqb_ref, own_ref, oth_ref, gpre_ref, accq_ref, acck_ref, rep_ref,
):
    step = pl.program_id(0)

    def run(c):
        nj = chunks(c)
        base = (0, nj[0] * BLK)
        scale = [
            [pre_ref[step * HB4 + hh, head(c, g)] * 0.125 for g in range(HEADS)] for hh in range(HB4)
        ]
        for hh in range(HB4):
            spread(rep_ref, hh, scale[hh])
        for b in range(2):
            n = nj[b] * BLK
            cs = slice(b * BLK, (b + 1) * BLK)
            ws, q2s = [], []
            for hh in range(HB4):
                ws.append(dot(kT_ref[:, :n], gL_ref[base[b] : base[b] + n, hh * BLK : (hh + 1) * BLK]))
                q2s.append((q_ref[cs, :].astype(F32) * rep_ref[hh : hh + 1, :]).astype(BF))
            for k in range(HEADS):
                rs = slice(k * HD, (k + 1) * HD)
                qk = qT_ref[rs, cs].astype(F32)
                t = None
                for hh in range(HB4):
                    w = ws[hh][rs, :]
                    g = jnp.sum(qk * w, axis=0, keepdims=True) * 0.125
                    keep_sum(gpre_ref, hh, head(c, k), b, g)
                    u = w * scale[hh][k]
                    t = u if t is None else t + u
                accq_ref[rs, cs] += t
            acck_ref[:n, :] += dot(gL_ref[base[b] : base[b] + n, :], jnp.concatenate(q2s, axis=0))

        @pl.when(step == HEADS // HB4 - 1)
        def _():
            split_rows(c, acck_ref, own_ref, oth_ref)

    @pl.when(step == 0)
    def _():
        accq_ref[...] = jnp.zeros_like(accq_ref)
        acck_ref[...] = jnp.zeros_like(acck_ref)

    per_core(ids_ref, run)

    @pl.when(step == HEADS // HB4 - 1)
    def _():
        gqa_ref[...] = accq_ref[:HI, :].T.astype(BF)
        gqb_ref[...] = accq_ref[HI:, :].T.astype(BF)


def scores_back(ids, pre, kT, qT, q, gL):
    return pl.pallas_call(
        scores_back_body,
        grid=(HEADS // HB4,),
        in_specs=[
            smem(), smem(), full((INNER, SEQ)), full((INNER, HALF)), full((HALF, INNER)),
            pl.BlockSpec((5 * BLK, HB4 * BLK), lambda h: (0, h)),
        ],
        out_specs=[
            full((HALF, HI)), full((HALF, HI)), full((SEQ, HI)), full((SEQ, HI)),
            pl.BlockSpec((HB4, HEADS, 128), lambda h: (h, 0, 0)),
        ],
        out_shape=[
            sds((HALF, HI)), sds((HALF, HI)), sds((SEQ, HI)), sds((SEQ, HI)),
            sds((HEADS, HEADS, 128), F32),
        ],
        scratch_shapes=[
            pltpu.VMEM((INNER, HALF), F32), pltpu.VMEM((SEQ, INNER), F32), pltpu.VMEM((8, INNER), F32),
        ],
        compiler_params=params(),
        cost_estimate=cost(12.1e9, 14e6),
        name="scores_back",
    )(ids, pre, kT, qT, q, far(gL))


def own_rows(loc, oth):
    return jnp.concatenate([loc[:BLK], oth[BLK:]], axis=0)


def project_qk_body(ids_ref, loc_ref, oth_ref, wa_ref, wb_ref, q_ref, qT_ref, k_ref, kT_ref):
    own = own_rows(loc_ref[...], oth_ref[...])
    for i, w in enumerate((wa_ref, wb_ref)):
        t = dot(own, w[:, :HI])
        cs = slice(i * HI, (i + 1) * HI)
        q_ref[:, cs] = t.astype(BF)
        qT_ref[cs, :] = t.T.astype(BF)
    project_rows(ids_ref, loc_ref, oth_ref, wa_ref, wb_ref, HI, k_ref, kT_ref)


def project_v_body(ids_ref, loc_ref, oth_ref, wa_ref, wb_ref, v_ref, vT_ref):
    project_rows(ids_ref, loc_ref, oth_ref, wa_ref, wb_ref, 0, v_ref, vT_ref)


def project_rows(ids_ref, loc_ref, oth_ref, wa_ref, wb_ref, col, k_ref, kT_ref):
    for d, rows in enumerate((loc_ref, oth_ref)):
        at = pl.multiple_of(lax.bitwise_xor(ids_ref[0], d) * HALF, HALF)
        for i, w in enumerate((wa_ref, wb_ref)):
            t = dot(rows[...], w[:, col : col + HI])
            cs = slice(i * HI, (i + 1) * HI)
            k_ref[pl.ds(at, HALF), cs] = t.astype(BF)
            kT_ref[cs, pl.ds(at, HALF)] = t.T.astype(BF)


def norm(v):
    inv = lax.rsqrt(jnp.mean(v * v, axis=-1, keepdims=True) + EPSILON)
    return v * inv, inv


def cast_body(q_ref, k_ref, v_ref, o_ref, in_ref, out_ref, qk_ref, vo_ref, ff_ref):
    qk_ref[:, :HI] = q_ref[...].astype(BF)
    qk_ref[:, HI:] = k_ref[...].astype(BF)
    vo_ref[:, :HI] = v_ref[...].astype(BF)
    vo_ref[:, HI:INNER] = o_ref[...].astype(BF)
    ff = in_ref.shape[1]
    ff_ref[:, :ff] = in_ref[...].astype(BF)
    ff_ref[:, ff:] = out_ref[:, : ff - PART].astype(BF)
    vo_ref[:, INNER:] = out_ref[:, ff - PART :].astype(BF)


def prepare_body(
    x_ref, xo_ref, c_ref, co_ref, gain_ref,
    loc_ref, oth_ref, actT_ref, own_ref, cown_ref, crest_ref, cT_ref,
):
    for src, dst, cs in ((x_ref, loc_ref, slice(0, HALF)), (xo_ref, oth_ref, slice(HALF, SEQ))):
        act = norm(src[...].astype(F32))[0] * gain_ref[...]
        dst[...] = act.astype(BF)
        actT_ref[:, cs] = act.T.astype(BF)
    own_ref[:BLK, :] = x_ref[:BLK, :]
    own_ref[BLK:, :] = xo_ref[BLK:, :]
    for dst, a, b, at in ((cown_ref, c_ref, co_ref, 0), (crest_ref, co_ref, c_ref, HALF)):
        dst[:BLK, :] = a[:BLK, :]
        dst[BLK:, :] = b[BLK:, :]
        cT_ref[:, at : at + BLK] = a[:BLK, :].astype(F32).T.astype(BF)
        cT_ref[:, at + BLK : at + HALF] = b[BLK:, :].astype(F32).T.astype(BF)


def middle_body(x_ref, h_ref, wa_ref, wb_ref, gain_ref, mid_ref, act_ref, actT_ref):
    mid = x_ref[...].astype(F32) + dot_nt(h_ref[:, :HI], wa_ref[:, HI:]) + dot_nt(h_ref[:, HI:], wb_ref[:, HI:])
    act = norm(mid)[0] * gain_ref[...]
    mid_ref[...] = mid
    act_ref[...] = act.astype(BF)
    actT_ref[...] = act.T.astype(BF)


def emit(me, scr_ref, cols, keep_ref, send_ref, outer_x):
    for e in range(16):
        x, y, z = e & 1, (e >> 1) & 1, e >> 2
        if me is None:
            ref, at, row = (keep_ref, send_ref)[e >> 3], e & 7, e * 48
        else:
            first, second = (x, y) if outer_x else (y, x)
            ref, at = (keep_ref, send_ref)[first], second * 4 + z
            row = pl.multiple_of(lax.bitwise_xor(me, e) * 48, 16)
        ref[at, :, cols] = scr_ref[pl.ds(row, 48), cols].astype(BF)


def gates(v):
    sq = v * v
    s = 0.5 * jnp.tanh(v * (0.7978845608028654 + 0.035677408136300125 * sq)) + 0.5
    slope = s + v * (1.5957691216057308 + 0.21406444881780075 * sq) * (s - s * s)
    return (v * s).astype(BF), slope


def ffn_body(
    xor, ids_ref, aown_ref, aoth_ref, aTown_ref, aToth_ref, cown_ref, coth_ref, cT_ref,
    win_ref, wouta_ref, woutb_ref, part_ref, outa_ref, outb_ref, gaa_ref, gab_ref, ka_ref, sa_ref, kb_ref, sb_ref,
    acco_ref, accg_ref, scr_ref,
):
    step = pl.program_id(0)
    last = pl.num_programs(0) - 1
    me = ids_ref[1] if xor else None

    @pl.when(step == 0)
    def _():
        acco_ref[...] = jnp.zeros_like(acco_ref)
        accg_ref[...] = jnp.zeros_like(accg_ref)

    win = win_ref[...]
    wout = jnp.concatenate(
        [wouta_ref[...], jnp.where(step == last, part_ref[...], woutb_ref[...])], axis=1
    )
    v0, v1 = dot(aown_ref[...], win), dot(aoth_ref[...], win)
    h0, s0 = gates(v0)
    g0 = dot(cown_ref[...], wout)
    h1, s1 = gates(v1)
    g1 = dot(coth_ref[...], wout)
    acco_ref[:HALF, :] += dot_nt(h0, wout)
    p0 = (g0.astype(BF).astype(F32) * s0).astype(BF)
    acco_ref[HALF:, :] += dot_nt(h1, wout)
    p1 = (g1.astype(BF).astype(F32) * s1).astype(BF)
    accg_ref[:HALF, :] += dot_nt(p0, win)
    accg_ref[HALF:, :] += dot_nt(p1, win)
    hid, gpre = (h0, h1), (p0, p1)
    scr_ref[...] = dot(cT_ref[:, :HALF], hid[0]) + dot(cT_ref[:, HALF:], hid[1])
    emit(me, scr_ref, slice(0, FT), ka_ref, sa_ref, True)
    scr_ref[...] = dot(aTown_ref[...], gpre[0]) + dot(aToth_ref[...], gpre[1])
    emit(me, scr_ref, slice(0, FT), kb_ref, sb_ref, False)

    @pl.when(step == last)
    def _():
        outa_ref[...] = acco_ref[:HALF, :]
        outb_ref[...] = acco_ref[HALF:, :].astype(BF)
        gaa_ref[...] = accg_ref[:HALF, :]
        gab_ref[...] = accg_ref[HALF:, :].astype(BF)


def ffn(xor, ids, aown, aoth, aTown, aToth, cown, coth, cT, w, part):
    width = (w.shape[1] + PART) // 2
    steps = width // FT
    tile = pl.BlockSpec((INNER, FT), lambda t: (0, t))
    end = w.shape[1] // PART - 1
    tile2 = pl.BlockSpec((INNER, PART), lambda t: (0, 2 * (steps + t)))
    tile3 = pl.BlockSpec((INNER, PART), lambda t: (0, jnp.minimum(2 * (steps + t) + 1, end)))
    grad = pl.BlockSpec((8, 48, FT), lambda t: (0, 0, t))
    half, halfT = full((HALF, INNER)), full((INNER, HALF))
    return pl.pallas_call(
        lambda *r: ffn_body(xor, *r),
        grid=(steps,),
        in_specs=[smem(), half, half, halfT, halfT, half, half, full((INNER, SEQ)), tile, tile2, tile3, full((INNER, PART))],
        out_specs=[half, half, half, half, grad, grad, grad, grad],
        out_shape=[
            sds((HALF, INNER), F32), sds((HALF, INNER)), sds((HALF, INNER), F32), sds((HALF, INNER)),
        ] + [sds((8, 48, width))] * 4,
        scratch_shapes=[
            pltpu.VMEM((SEQ, INNER), F32), pltpu.VMEM((SEQ, INNER), F32), pltpu.VMEM((INNER, FT), F32),
        ],
        compiler_params=params(44),
        cost_estimate=cost(14.5e9, 20e6, 1.6e6),
        name="ffn",
    )(ids, aown, aoth, aTown, aToth, cown, coth, cT, w, w, w, part)


def middle_back_body(
    ga_ref, gr_ref, mid_ref, cot_ref, gain_ref, h_ref, wa_ref, wb_ref,
    stay_ref, sent_ref, gh_ref, ghT_ref, gain_out, gwa_ref, gwb_ref,
):
    ga = ga_ref[...] + gr_ref[...].astype(F32)
    normed, inv = norm(mid_ref[...])
    scaled = ga * gain_ref[...]
    gm = cot_ref[...].astype(F32) + inv * (
        scaled - normed * jnp.mean(scaled * normed, axis=-1, keepdims=True)
    )
    gain_out[...] = jnp.sum(ga * normed, axis=0, keepdims=True)
    stay_ref[...] = gm[:BLK]
    sent_ref[...] = gm[BLK:]
    grad = gm.astype(BF)
    gT = gm.T.astype(BF)
    for i, (w, gw) in enumerate(((wa_ref, gwa_ref), (wb_ref, gwb_ref))):
        cs = slice(i * HI, (i + 1) * HI)
        t = dot(grad, w[:, HI:])
        gh_ref[:, cs] = t.astype(BF)
        ghT_ref[cs, :] = t.T.astype(BF)
        gw[...] = dot(gT, h_ref[:, cs]).astype(BF)


def joined(own, got):
    a, b = own.astype(F32), got.astype(F32)
    return jnp.concatenate([a[:HALF] + b[HALF:], a[HALF:] + b[:HALF]], axis=0).astype(BF)


def grad_vo_body(xor, ids_ref, aT_ref, gv_ref, rv_ref, go_ref, ro_ref, gv_out, ka, sa, kb, sb, scr):
    me = ids_ref[1] if xor else None
    gv = joined(gv_ref[...], rv_ref[...])
    gv_out[...] = gv
    scr[...] = dot(aT_ref[...], gv)
    emit(me, scr, slice(0, HI), ka, sa, True)
    scr[...] = go_ref[...].astype(F32) + ro_ref[...].astype(F32)
    emit(me, scr, slice(0, HI), kb, sb, False)


def grad_qk_body(xor, ids_ref, aT_ref, gq_ref, rq_ref, gk_ref, rk_ref, gq_out, gk_out, ka, sa, kb, sb, scr):
    me = ids_ref[1] if xor else None
    gq, rq = gq_ref[...], rq_ref[...]
    gq = jnp.concatenate([gq[:BLK], rq[BLK:], rq[:BLK], gq[BLK:]], axis=0)
    gq_out[...] = gq
    scr[...] = dot(aT_ref[...], gq)
    emit(me, scr, slice(0, HI), ka, sa, True)
    gk = joined(gk_ref[...], rk_ref[...])
    gk_out[...] = gk
    scr[...] = dot(aT_ref[...], gk)
    emit(me, scr, slice(0, HI), kb, sb, False)


def act_back_body(gq_ref, gk_ref, gv_ref, qk_ref, vo_ref, loc_ref, oth_ref):
    for rs, ref in ((slice(0, HALF), loc_ref), (slice(HALF, SEQ), oth_ref)):
        t = dot_nt(gq_ref[rs, :], qk_ref[:, :HI]) + dot_nt(gk_ref[rs, :], qk_ref[:, HI:])
        ref[...] = (t + dot_nt(gv_ref[rs, :], vo_ref[:, :HI])).astype(ref.dtype)


def output_body(mid_ref, own_ref, got_ref, stay_ref, sent_ref):
    out = (mid_ref[...] + own_ref[...] + got_ref[...].astype(F32)).astype(BF)
    stay_ref[...] = out[:BLK]
    sent_ref[...] = out[BLK:]


def join_body(stay_ref, got_ref, out_ref):
    out_ref[:BLK, :] = stay_ref[...]
    out_ref[BLK:, :] = got_ref[...]


def tokens_back_body(
    ga_ref, gr_ref, x_ref, gain_ref, stay_ref, got_ref, gain2_ref, gpre_ref, gpost_ref,
    out_ref, small_ref,
):
    ga = ga_ref[...] + gr_ref[...].astype(F32)
    normed, inv = norm(x_ref[...].astype(F32))
    scaled = ga * gain_ref[...]
    back = inv * (scaled - normed * jnp.mean(scaled * normed, axis=-1, keepdims=True))
    out_ref[:BLK, :] = (stay_ref[...] + back[:BLK]).astype(BF)
    out_ref[BLK:, :] = (got_ref[...] + back[BLK:]).astype(BF)
    gain1 = jnp.sum(ga * normed, axis=0, keepdims=True)
    small_ref[...] = jnp.zeros_like(small_ref)
    for i in range(6):
        cs = slice(i * 128, (i + 1) * 128)
        small_ref[i : i + 1, :] = gain1[:, cs]
        small_ref[8 + i : 9 + i, :] = gain2_ref[:, cs]
    small_ref[16 : 16 + HEADS, :HEADS] = jnp.sum(gpre_ref[...], axis=-1)
    small_ref[32 : 32 + HEADS, :HEADS] = jnp.sum(gpost_ref[...], axis=-1)


def swap(v):
    return lax.ppermute(v, "tensor", [(0, 1), (1, 0)])


def hop(v, mask):
    n = lax.axis_size("dp")
    return lax.ppermute(v, "dp", [(i, i ^ mask) for i in range(n)])


def after(v, *done):
    return lax.optimization_barrier((v, *done))[0]


def place_body(ids_ref, ax, ay, bx, by, *outs):
    me = ids_ref[1]
    w = ax.shape[3]
    for t, ref in enumerate((ax, ay, bx, by)):
        col = (t // 2) * w
        for i in range(2):
            for j in range(4):
                e = 4 * j + ((2 * i + t) if t < 2 else (i + 2 * (t - 2)))
                row = pl.multiple_of(lax.bitwise_xor(me, e) * 48, 16)
                start = 0
                for out in outs:
                    end = start + out.shape[1]
                    lo, hi = max(col, start), min(col + w, end)
                    if lo < hi:
                        out[pl.ds(row, 48), lo - start : hi - start] = ref[i, j, :, lo - col : hi - col]
                    start = end


def gather_z(shard):
    return [shard] + [hop(shard, 4 * e) for e in range(1, 4)]


def gather_one(pieces):
    z = jnp.stack(pieces, axis=0)
    w = z.shape[2] // 2
    a, b = z[:, :, :w], z[:, :, w:]
    return a, hop(a, 2), b, hop(b, 1)


def gather_two(a, ra, b, rb):
    a2, b2 = jnp.stack([a, ra], axis=0), jnp.stack([b, rb], axis=0)
    return a2, hop(a2, 1), b2, hop(b2, 2)


def gathered(ids, parts, *outs):
    return once(place_body, outs, (ids, *parts), "place")


def fold_one_body(ka, ra, kb, rb, oka, osa, okb, osb):
    for k, r, keep, send in ((ka, ra, oka, osa), (kb, rb, okb, osb)):
        t = (k[...].astype(F32) + r[...].astype(F32)).astype(BF)
        keep[...] = t[:4]
        send[...] = t[4:]


def fold_two_body(ka, ra, kb, rb, small, got, own, total, *sends):
    w = ka.shape[2]
    for k, r, cs in ((ka, ra, slice(0, w)), (kb, rb, slice(w, 2 * w))):
        t = k[...].astype(F32) + r[...].astype(F32)
        own[:, cs] = t[0]
        for e in range(3):
            sends[e][:, cs] = t[e + 1].astype(BF)
    v = (small[...] + got[...]).astype(BF)
    total[...] = v.astype(F32)
    for send in sends:
        send[:, 2 * w :] = v


def fold_one(ka, ra, kb, rb):
    piece = sds((4,) + ka.shape[1:])
    return once(fold_one_body, (piece,) * 4, (ka, ra, kb, rb), "fold_one", scalars=0)


def fold_two(*parts):
    w = 2 * parts[0].shape[2]
    outs = (sds((48, w), F32), sds((48, 128), F32)) + (sds((48, w + 128)),) * 3
    return once(fold_two_body, outs, parts, "fold_two", scalars=0)


def fold_ff_body(ka, ra, kb, rb, own, send):
    w = ka.shape[2]
    for k, r, cs in ((ka, ra, slice(0, w)), (kb, rb, slice(w, 2 * w))):
        t = (k[...].astype(F32) + r[...].astype(F32)).astype(BF)
        for z in range(2):
            own[z, :, cs] = t[2 * z]
            send[z, :, cs] = t[2 * z + 1]


def fold_at_body(*refs):
    ins, outs = refs[:8], refs[8:]
    for i in range(4):
        k, r = ins[2 * i], ins[2 * i + 1]
        kept, sent = outs[2 * (i // 2)], outs[2 * (i // 2) + 1]
        cs = slice((i % 2) * HI, (i % 2) * HI + HI)
        t = (k[...].astype(F32) + r[...].astype(F32)).astype(BF)
        kept[:, :, cs] = t[:4]
        sent[:, :, cs] = t[4:]


def fold_ff_two_body(own, got, keep, send):
    t = own[...].astype(F32) + got[...].astype(F32)
    keep[...] = t[0]
    send[...] = t[1].astype(BF)


def finish_ff_body(own, got, in_ref, out_ref):
    w = out_ref.shape[1]
    out_ref[...] = own[:, :w] + got[:, :w].astype(F32)
    in_ref[...] = own[:, w:] + got[:, w:].astype(F32)


def finish_body(own, total, a, b, c, *outs):
    def got(cs):
        return a[:, cs].astype(F32) + b[:, cs].astype(F32) + c[:, cs].astype(F32)

    for i, ref in enumerate(outs[:4]):
        cs = slice(i * HI, (i + 1) * HI)
        ref[...] = own[:, cs] + got(cs)
    at = 4 * HI
    cs = slice(at, at + 128)
    near = total[...] + a[:, cs].astype(F32)
    split_small(near + (b[:, cs].astype(F32) + c[:, cs].astype(F32)), *outs[4:])


def split_small(v, gain1, gain2, gpre, gpost):
    for i in range(6):
        gain1[i * 128 : (i + 1) * 128] = v[i]
        gain2[i * 128 : (i + 1) * 128] = v[8 + i]
    gpre[...] = v[16 : 16 + HEADS, :HEADS]
    gpost[...] = v[32:48].T[:HEADS, :HEADS]


def split_small_body(v, *outs):
    split_small(v[...], *outs)


def scatter_plain(ka, sa, kb, sb):
    w = ka.shape[2]
    flat = jnp.concatenate(
        [jnp.concatenate([k, s], axis=0).reshape(768, w) for k, s in ((ka, sa), (kb, sb))], axis=1
    )
    return lax.psum_scatter(flat.astype(F32), "dp", scatter_dimension=0, tiled=True)


def sum_all(v):
    n = lax.axis_size("dp")
    v = v + swap(v)
    bit = 1
    while bit < n:
        v = v + hop(v, bit)
        bit *= 2
    return v


def on_device(
    tokens, cotangent, segment_ids, norm1_gain, w_query, w_key, w_value, pre_mix, post_mix,
    w_output, norm2_gain, w_in, w_out,
):
    ids = jnp.stack([lax.axis_index("tensor"), lax.axis_index("dp")]).astype(jnp.int32)
    xor = lax.axis_size("dp") == 16
    low = lambda v: v.astype(BF)
    D = norm1_gain.shape[0]
    tie = lax.optimization_barrier
    gain1, gain2 = norm1_gain.reshape(1, D), norm2_gain.reshape(1, D)
    seg = segment_ids.reshape(1, SEQ)

    every = lambda v: lax.all_gather(v, "dp", axis=0, tiled=True)
    r, ff = w_in.shape
    shard_qk, shard_vo, shard_ff = once(
        cast_body, (sds((r, INNER)), sds((r, INNER + PART)), sds((r, 2 * ff - PART))),
        tuple(far(w) for w in (w_query, w_key, w_value, w_output.T, w_in, w_out.T)), "cast", scalars=0,
    )
    if xor:
        z_qk = gather_z(shard_qk)
    w_ff = every(shard_ff)
    x_oth, cot_oth = swap(tokens), swap(cotangent)
    act_loc, act_oth, actT, x_own, cot_own, cot_rest, cotT = once(
        prepare_body,
        (
            sds((HALF, D)), sds((HALF, D)), hbm((D, SEQ)), hbm((HALF, D)), hbm((HALF, D)),
            hbm((HALF, D)), hbm((D, SEQ)),
        ),
        (far(tokens), x_oth, far(cotangent), cot_oth, gain1), "prepare", scalars=0,
    )
    if xor:
        *z_qk, act_loc = tie((*z_qk, act_loc))
        a, ra, b, rb = gather_one(z_qk)
        z_vo = gather_z(after(shard_vo, *z_qk))
        qk_parts = gather_two(a, ra, b, rb)
        *z_vo, ax, ay, bx, by = tie((*z_vo, *qk_parts))
        a, ra, b, rb = gather_one(z_vo)
        (w_qk,) = gathered(ids, (ax, ay, bx, by), sds((D, INNER)))
    else:
        w_qk, w_vo = every(shard_qk), every(shard_vo)
        w_vo, w_part = w_vo[:, :INNER], w_vo[:, INNER:]
    q, qT, k, kT = once(
        project_qk_body,
        (hbm((HALF, INNER)), sds((INNER, HALF)), sds((SEQ, INNER)), hbm((INNER, SEQ))),
        (ids, act_loc, act_oth, w_qk, swap(w_qk)), "project_qk", flops=1.8e9,
    )
    if xor:
        ra, rb, k = tie((ra, rb, k))
        vo_parts = gather_two(a, ra, b, rb)
        k = after(k, vo_parts[0], vo_parts[2])
    pT = logits_softmax(ids, pre_mix, seg, k, qT)
    if xor:
        w_vo, w_part = gathered(ids, tie((*vo_parts, pT))[:4], sds((D, INNER)), hbm((D, PART)))
    vo_o = swap(w_vo)
    v, vT = once(
        project_v_body, (hbm((SEQ, INNER)), sds((INNER, SEQ))),
        (ids, act_loc, act_oth, w_vo, vo_o), "project_v", flops=1.2e9,
    )
    uT, heads = attend(ids, post_mix, vT, pT)
    mid, act2, act2T = once(
        middle_body, (hbm((HALF, D), F32), hbm((HALF, D)), hbm((D, HALF))),
        (x_own, heads, w_vo, vo_o, gain2), "middle", scalars=0, flops=6e8,
    )
    out_own, out_oth, ga_own, ga_oth, ka, sa, kb, sb = ffn(
        xor, ids, far(act2), far(swap(act2)), far(act2T), far(swap(act2T)), far(cot_own), far(cot_rest), far(cotT), far(w_ff), far(w_part)
    )
    if xor:
        ra, rb = hop(sa, 1), hop(sb, 2)
    stay, sent, gh, ghT, gain2_part, gwo, gwo_o = once(
        middle_back_body,
        (
            hbm((BLK, D), F32), hbm((BLK, D), F32), sds((HALF, INNER)), sds((INNER, HALF)),
            hbm((1, D), F32), sds((D, HI)), sds((D, HI)),
        ),
        (ga_own, swap(ga_oth), mid, cot_own, gain2, heads, w_vo, vo_o),
        "middle_back", scalars=0, flops=1.2e9,
    )
    got_sent, got_out, gwo_r = swap(sent), swap(out_oth), swap(gwo_o)
    gL, gv, gv_o, gpost = attend_back(ids, post_mix, v, ghT, gh, pT, uT)
    grads = (sds((8, 48, HI)),) * 4
    if xor:
        gv, gv_o, got_sent, got_out, gwo_r = tie((gv, gv_o, got_sent, got_out, gwo_r))
    gv, *vo = once(
        lambda *r: grad_vo_body(xor, *r), (hbm((SEQ, HI)),) + grads,
        (ids, actT, gv, swap(gv_o), gwo, gwo_r), "grad_vo",
        scratch=[pltpu.VMEM((D, HI), F32)], flops=6e8,
    )
    if xor:
        vo_ka, vo_sa, vo_kb, vo_sb = vo
        ra, rb = tie((ra, rb, vo_sa))[:2]
        ff_ka, ff_sa, ff_kb, ff_sb = fold_one(ka, ra, kb, rb)
        ff_ra, ff_rb = hop(ff_sa, 2), hop(ff_sb, 1)
        gL = after(gL, ff_sa, vo_sa)
    gq, gq_o, gk, gk_o, gpre = scores_back(ids, pre_mix, kT, qT, q, gL)
    if xor:
        ff_ra, ff_rb, gq, gq_o, gk_o = tie((ff_ra, ff_rb, gq, gq_o, gk_o))
        wide = ff_ka.shape[2] * 2
        ff_own, ff_send = once(
            fold_ff_body, (sds((2, 48, wide)),) * 2, (ff_ka, ff_ra, ff_kb, ff_rb), "fold_ff", scalars=0
        )
        ff_got = hop(ff_send, 4)
        vo_sa, vo_sb = tie((vo_sa, vo_sb, ff_send))[:2]
        vo_ra, vo_rb = hop(vo_sa, 1), hop(vo_sb, 2)
        gq, gk = tie((gq, gk, ff_send))[:2]
    gq, gk, *qk = once(
        lambda *r: grad_qk_body(xor, *r), (sds((SEQ, HI)),) * 2 + grads,
        (ids, actT, gq, swap(gq_o), gk, swap(gk_o)), "grad_qk",
        scratch=[pltpu.VMEM((D, HI), F32)], flops=1.2e9,
    )
    if xor:
        qk_ka, qk_sa, qk_kb, qk_sb = qk
        qk_ra, qk_rb = hop(qk_sa, 1), hop(qk_sb, 2)
        gq, vo_ra, vo_rb = tie((gq, vo_ra, vo_rb))
    ga_loc, ga_oth = once(
        act_back_body, (sds((HALF, D), F32), sds((HALF, D))), (gq, gk, gv, w_qk, w_vo),
        "act_back", scalars=0, flops=0.3e9, moved=1,
    )
    ga_got = swap(ga_oth)
    if xor:
        ff_own, ff_got = tie((ff_own, ff_got, ga_oth))[:2]
        ff_own, ff_send = once(
            fold_ff_two_body, (sds((48, wide), F32), sds((48, wide))), (ff_own, ff_got), "fold_ff_two", scalars=0,
            flops=2e9, moved=1,
        )
        ff_got = hop(ff_send, 8)
        qk_ra, qk_rb, ff_two = tie((qk_ra, qk_rb, ff_send))
        at_ka, at_sa, at_kb, at_sb = once(
            fold_at_body, (sds((4, 48, INNER)),) * 4,
            (qk_ka, qk_ra, vo_ka, vo_ra, qk_kb, qk_rb, vo_kb, vo_rb), "fold_at", scalars=0, flops=5e9,
        )
        at_ra, at_rb = hop(at_sa, 2), hop(at_sb, 1)
        ga_loc, ga_got = tie((ga_loc, ga_got, at_sa))[:2]
    grad_tokens, small = once(
        tokens_back_body, (sds((HALF, D)), sds((48, 128), F32)),
        (ga_loc, ga_got, tokens, gain1, stay, got_sent, gain2_part, gpre, gpost),
        "tokens_back", scalars=0,
    )
    r = w_in.shape[0]
    part = sds((r, HI), F32)
    small_outs = (sds((D,), F32),) * 2 + (sds((HEADS, HEADS), F32),) * 2
    if xor:
        got = swap(small)
        mid, small = tie((mid, small))
        out_stay, out_sent = once(
            output_body, (sds((BLK, D)), sds((BLK, D))), (mid, out_own, got_out), "output", scalars=0
        )
        out_got = swap(out_sent)
        small, got = tie((small, got, out_sent))[:2]
        small = small + got
        small = small + hop(small, 1)
        got = hop(small, 2)
        at_ra, at_rb, got, small, ff_got = tie((at_ra, at_rb, got, small, ff_got))
        at, total, *sends = fold_two(at_ka, at_ra, at_kb, at_rb, small, got)
        gots = [hop(sends[e], 4 * (e + 1)) for e in range(3)]
        out_got = tie((out_got, at))[0]
        (output,) = once(join_body, (sds((HALF, D)),), (out_stay, out_got), "join", scalars=0)
        grad_in, grad_out = once(
            finish_ff_body, (sds((r, ff), F32),) * 2, (ff_own, ff_got), "finish_ff", scalars=0
        )
        gots = tie((*gots, output, grad_in))[:3]
        grad_q, grad_v, grad_k, grad_o, *sums = once(
            finish_body, (part,) * 4 + small_outs, (at, total, *gots), "finish", scalars=0
        )
    else:
        grad_qk, grad_vo = scatter_plain(*qk), scatter_plain(*vo)
        grad_ffn = scatter_plain(ka, sa, kb, sb)
        grad_q, grad_k, grad_v, grad_o = grad_qk[:, :HI], grad_qk[:, HI:], grad_vo[:, :HI], grad_vo[:, HI:]
        grad_in, grad_out = grad_ffn[:, ff:], grad_ffn[:, :ff]
        sums = once(split_small_body, small_outs, (sum_all(small),), "split_small", scalars=0)
        out_stay, out_sent = once(
            output_body, (sds((BLK, D)), sds((BLK, D))), (mid, out_own, got_out), "output", scalars=0
        )
        output = jnp.concatenate([out_stay, swap(out_sent)], axis=0)
    return (
        output, grad_tokens, sums[0], grad_q, grad_k, grad_v, sums[2], sums[3],
        grad_o.T, sums[1], grad_in, grad_out.T,
    )


def solution(mesh):
    rows = P(("dp", "tensor"), None)
    w, wt = P("dp", "tensor"), P("tensor", "dp")
    return jax.shard_map(
        on_device,
        mesh=mesh,
        in_specs=(rows, rows, P("dp"), P(), w, w, w, P(), P(), wt, P(), w, wt),
        out_specs=(rows, rows, P(), w, w, w, P(), P(), wt, P(), w, wt),
        check_vma=False,
    )
```

```python
import math

import jax
import jax.numpy as jnp
from jax import lax
from jax.experimental import pallas as pl
from jax.experimental.pallas import tpu as pltpu
from jax.sharding import PartitionSpec as P

HEADS = 12
HD = 64
INNER = 768
HI = INNER // 2
SEQ = 1024
HALF = SEQ // 2
BLK = 256
EPSILON = 1e-06
LOG2E = 1.4426950408889634
BF = jnp.bfloat16
F32 = jnp.float32
HB1, HB2, HB3, HB4 = 3, 3, 3, 3
FT = 512
PART = 256


def dot(a, b):
    return jnp.dot(a, b, preferred_element_type=F32)


def dot_nt(a, b):
    return lax.dot_general(a, b, (((1,), (1,)), ((), ())), preferred_element_type=F32)


def smem():
    return pl.BlockSpec(memory_space=pltpu.SMEM)


def whole():
    return pl.BlockSpec(memory_space=pltpu.VMEM)


def full(s):
    return pl.BlockSpec(s, lambda *i: (0,) * len(s))


def params(mib=24):
    return pltpu.CompilerParams(vmem_limit_bytes=mib * 1024 * 1024)


def cost(flops, moved, exps=0):
    return pl.CostEstimate(flops=int(flops), bytes_accessed=int(moved), transcendentals=int(exps))


def sds(shape, dtype=BF):
    return jax.ShapeDtypeStruct(shape, dtype)


def once(body, outs, args, name, scalars=1, scratch=(), flops=0, moved=None):
    if moved is None:
        moved = sum(math.prod(a.shape) * a.dtype.itemsize for a in (*args, *outs))
    return pl.pallas_call(
        body,
        in_specs=[smem()] * scalars + [whole()] * (len(args) - scalars),
        out_specs=[whole()] * len(outs),
        out_shape=list(outs),
        scratch_shapes=list(scratch),
        compiler_params=params(),
        cost_estimate=cost(flops, moved),
        name=name,
    )(*args)


def per_core(ids_ref, run):
    for c in range(2):
        pl.when(ids_ref[0] == c)(lambda c=c: run(c))


def head(c, i):
    return (i + c * (HEADS // 2)) % HEADS


def spread(rep_ref, row, values):
    for g, value in enumerate(values):
        rep_ref[row : row + 1, g * HD : (g + 1) * HD] = jnp.full((1, HD), value, F32)


def hbm(shape, dtype=BF):
    return pltpu.HBM(shape, dtype)


def far(v):
    return pltpu.with_memory_space_constraint(v, pltpu.HBM)


def chunks(c):
    return (1, 4) if c == 0 else (3, 2)


def blocks_of(c):
    return (0, 3) if c == 0 else (2, 1)


def logits_body(ids_ref, pre_ref, seg_ref, k_ref, qT_ref, pT_ref, mask_ref):
    step = pl.program_id(0)

    def run(c):
        nj, bl = chunks(c), blocks_of(c)
        base = (0, nj[0] * BLK)

        @pl.when(step == 0)
        def _():
            seg = seg_ref[...].astype(F32)
            down = jnp.broadcast_to(seg, (8, SEQ)).T[:, :1]
            for b in range(2):
                qpos = lax.broadcasted_iota(jnp.int32, (BLK, BLK), 1) + bl[b] * BLK
                qseg = seg[:, bl[b] * BLK : (bl[b] + 1) * BLK]
                for j in range(nj[b]):
                    kpos = lax.broadcasted_iota(jnp.int32, (BLK, BLK), 0) + j * BLK
                    ok = (kpos <= qpos) & (down[j * BLK : (j + 1) * BLK] == qseg)
                    at = base[b] + j * BLK
                    mask_ref[at : at + BLK, :] = jnp.where(ok, 0.0, -1e30)

        for hh in range(HB1):
            h = step * HB1 + hh
            scale = [pre_ref[h, head(c, g)] * (0.125 * LOG2E) for g in range(HEADS)]
            for b in range(2):
                n = nj[b] * BLK
                qs = jnp.concatenate(
                    [
                        (
                            qT_ref[g * HD : (g + 1) * HD, b * BLK : (b + 1) * BLK].astype(F32)
                            * scale[g]
                        ).astype(BF)
                        for g in range(HEADS)
                    ],
                    axis=0,
                )
                s = dot(k_ref[:n, :], qs) + mask_ref[base[b] : base[b] + n, :]
                m = jnp.max(s, axis=0, keepdims=True)
                e = jnp.exp2(s - m)
                inv = 1.0 / jnp.sum(e, axis=0, keepdims=True)
                pT_ref[base[b] : base[b] + n, hh * BLK : (hh + 1) * BLK] = (e * inv).astype(BF)

    per_core(ids_ref, run)


def logits_softmax(ids, pre, seg, k, qT):
    return pl.pallas_call(
        logits_body,
        grid=(HEADS // HB1,),
        in_specs=[smem(), smem(), full((1, SEQ)), full((SEQ, INNER)), full((INNER, HALF))],
        out_specs=pl.BlockSpec((5 * BLK, HB1 * BLK), lambda h: (0, h)),
        out_shape=hbm((5 * BLK, HEADS * BLK)),
        scratch_shapes=[pltpu.VMEM((5 * BLK, BLK), F32)],
        compiler_params=params(),
        cost_estimate=cost(6.04e9, 10e6, 4e6),
        name="logits_softmax",
    )(ids, pre, seg, k, qT)


def attend_body(ids_ref, post_ref, vT_ref, pT_ref, uT_ref, h_ref, acc_ref):
    step = pl.program_id(0)

    def run(c):
        nj = chunks(c)
        base = (0, nj[0] * BLK)
        for b in range(2):
            n = nj[b] * BLK
            cs = slice(b * BLK, (b + 1) * BLK)
            us = []
            for hh in range(HB2):
                u = dot(vT_ref[:, :n], pT_ref[base[b] : base[b] + n, hh * BLK : (hh + 1) * BLK])
                uT_ref[hh * INNER : (hh + 1) * INNER, cs] = u.astype(BF)
                us.append(u)
            for k in range(HEADS):
                rs = slice(k * HD, (k + 1) * HD)
                t = us[0][rs, :] * post_ref[head(c, k), step * HB2]
                for hh in range(1, HB2):
                    t = t + us[hh][rs, :] * post_ref[head(c, k), step * HB2 + hh]
                acc_ref[rs, cs] += t

    @pl.when(step == 0)
    def _():
        acc_ref[...] = jnp.zeros_like(acc_ref)

    per_core(ids_ref, run)

    @pl.when(step == HEADS // HB2 - 1)
    def _():
        h_ref[...] = acc_ref[...].T.astype(BF)


def attend(ids, post, vT, pT):
    return pl.pallas_call(
        attend_body,
        grid=(HEADS // HB2,),
        in_specs=[smem(), smem(), full((INNER, SEQ)), pl.BlockSpec((5 * BLK, HB2 * BLK), lambda h: (0, h))],
        out_specs=[pl.BlockSpec((HB2 * INNER, HALF), lambda h: (h, 0)), full((HALF, INNER))],
        out_shape=[hbm((HEADS * INNER, HALF)), sds((HALF, INNER))],
        scratch_shapes=[pltpu.VMEM((INNER, HALF), F32)],
        compiler_params=params(),
        cost_estimate=cost(6.04e9, 20e6),
        name="attend",
    )(ids, post, vT, far(pT))


def split_rows(c, acc_ref, own_ref, oth_ref):
    for d in range(2):
        src = slice((c ^ d) * HALF, (c ^ d) * HALF + HALF)
        dst = slice(d * HALF, (d + 1) * HALF)
        own_ref[dst, :] = acc_ref[src, :HI].astype(BF)
        oth_ref[dst, :] = acc_ref[src, HI:].astype(BF)


def keep_sum(ref, h, k, b, g):
    g = g[:, :128] + g[:, 128:]
    ref[h, k] = g if b == 0 else ref[h, k] + g


def to_eight(v):
    return jnp.sum(v.reshape(HD // 8, 8, v.shape[1]), axis=0)


def attend_back_body(
    ids_ref, post_ref, v_ref, ghT_ref, gh_ref, pT_ref, uT_ref,
    gL_ref, own_ref, oth_ref, gpost_ref, acc_ref, rep_ref,
):
    step = pl.program_id(0)

    def run(c):
        nj = chunks(c)
        base = (0, nj[0] * BLK)
        for hh in range(HB3):
            spread(rep_ref, hh, [post_ref[head(c, k), step * HB3 + hh] for k in range(HEADS)])
        for b in range(2):
            n = nj[b] * BLK
            cs = slice(b * BLK, (b + 1) * BLK)
            g2s = []
            for hh in range(HB3):
                h = step * HB3 + hh
                hs = slice(hh * BLK, (hh + 1) * BLK)
                r = jnp.zeros((8, BLK), F32)
                parts = []
                for k in range(HEADS):
                    gk = ghT_ref[k * HD : (k + 1) * HD, cs].astype(F32)
                    u = uT_ref[hh * INNER + k * HD : hh * INNER + (k + 1) * HD, cs].astype(F32)
                    g = to_eight(gk * u)
                    w = post_ref[head(c, k), h]
                    keep_sum(gpost_ref, hh, head(c, k), b, g)
                    r = r + g * w
                    parts.append((gk * w).astype(BF))
                r = jnp.sum(r, axis=0, keepdims=True)
                gP = dot(v_ref[:n, :], jnp.concatenate(parts, axis=0))
                p = pT_ref[base[b] : base[b] + n, hs]
                gL_ref[base[b] : base[b] + n, hs] = (p.astype(F32) * (gP - r)).astype(BF)
                g2s.append((gh_ref[cs, :].astype(F32) * rep_ref[hh : hh + 1, :]).astype(BF))
            acc_ref[:n, :] += dot(pT_ref[base[b] : base[b] + n, :], jnp.concatenate(g2s, axis=0))

        @pl.when(step == HEADS // HB3 - 1)
        def _():
            split_rows(c, acc_ref, own_ref, oth_ref)

    @pl.when(step == 0)
    def _():
        acc_ref[...] = jnp.zeros_like(acc_ref)

    per_core(ids_ref, run)


def attend_back(ids, post, v, ghT, gh, pT, uT):
    return pl.pallas_call(
        attend_back_body,
        grid=(HEADS // HB3,),
        in_specs=[
            smem(), smem(), full((SEQ, INNER)), full((INNER, HALF)), full((HALF, INNER)),
            pl.BlockSpec((5 * BLK, HB3 * BLK), lambda h: (0, h)),
            pl.BlockSpec((HB3 * INNER, HALF), lambda h: (h, 0)),
        ],
        out_specs=[
            pl.BlockSpec((5 * BLK, HB3 * BLK), lambda h: (0, h)),
            full((SEQ, HI)), full((SEQ, HI)),
            pl.BlockSpec((HB3, HEADS, 8, 128), lambda h: (h, 0, 0, 0)),
        ],
        out_shape=[
            hbm((5 * BLK, HEADS * BLK)), sds((SEQ, HI)), sds((SEQ, HI)),
            hbm((HEADS, HEADS, 8, 128), F32),
        ],
        scratch_shapes=[pltpu.VMEM((SEQ, INNER), F32), pltpu.VMEM((8, INNER), F32)],
        compiler_params=params(),
        cost_estimate=cost(12.1e9, 30e6),
        name="attend_back",
    )(ids, post, v, ghT, gh, far(pT), far(uT))


def scores_back_body(
    ids_ref, pre_ref, kT_ref, qT_ref, q_ref, gL_ref,
    gqa_ref, gqb_ref, own_ref, oth_ref, gpre_ref, accq_ref, acck_ref, rep_ref,
):
    step = pl.program_id(0)

    def run(c):
        nj = chunks(c)
        base = (0, nj[0] * BLK)
        scale = [
            [pre_ref[step * HB4 + hh, head(c, g)] * 0.125 for g in range(HEADS)] for hh in range(HB4)
        ]
        for hh in range(HB4):
            spread(rep_ref, hh, scale[hh])
        for b in range(2):
            n = nj[b] * BLK
            cs = slice(b * BLK, (b + 1) * BLK)
            ws, q2s = [], []
            for hh in range(HB4):
                ws.append(dot(kT_ref[:, :n], gL_ref[base[b] : base[b] + n, hh * BLK : (hh + 1) * BLK]))
                q2s.append((q_ref[cs, :].astype(F32) * rep_ref[hh : hh + 1, :]).astype(BF))
            for k in range(HEADS):
                rs = slice(k * HD, (k + 1) * HD)
                qk = qT_ref[rs, cs].astype(F32)
                t = None
                for hh in range(HB4):
                    w = ws[hh][rs, :]
                    keep_sum(gpre_ref, hh, head(c, k), b, to_eight(qk * w))
                    u = w * scale[hh][k]
                    t = u if t is None else t + u
                accq_ref[rs, cs] += t
            acck_ref[:n, :] += dot(gL_ref[base[b] : base[b] + n, :], jnp.concatenate(q2s, axis=0))

        @pl.when(step == HEADS // HB4 - 1)
        def _():
            split_rows(c, acck_ref, own_ref, oth_ref)

    @pl.when(step == 0)
    def _():
        accq_ref[...] = jnp.zeros_like(accq_ref)
        acck_ref[...] = jnp.zeros_like(acck_ref)

    per_core(ids_ref, run)

    @pl.when(step == HEADS // HB4 - 1)
    def _():
        gqa_ref[...] = accq_ref[:HI, :].T.astype(BF)
        gqb_ref[...] = accq_ref[HI:, :].T.astype(BF)


def scores_back(ids, pre, kT, qT, q, gL):
    return pl.pallas_call(
        scores_back_body,
        grid=(HEADS // HB4,),
        in_specs=[
            smem(), smem(), full((INNER, SEQ)), full((INNER, HALF)), full((HALF, INNER)),
            pl.BlockSpec((5 * BLK, HB4 * BLK), lambda h: (0, h)),
        ],
        out_specs=[
            full((HALF, HI)), full((HALF, HI)), full((SEQ, HI)), full((SEQ, HI)),
            pl.BlockSpec((HB4, HEADS, 8, 128), lambda h: (h, 0, 0, 0)),
        ],
        out_shape=[
            sds((HALF, HI)), sds((HALF, HI)), sds((SEQ, HI)), sds((SEQ, HI)),
            sds((HEADS, HEADS, 8, 128), F32),
        ],
        scratch_shapes=[
            pltpu.VMEM((INNER, HALF), F32), pltpu.VMEM((SEQ, INNER), F32), pltpu.VMEM((8, INNER), F32),
        ],
        compiler_params=params(),
        cost_estimate=cost(12.1e9, 14e6),
        name="scores_back",
    )(ids, pre, kT, qT, q, far(gL))


def own_rows(loc, oth):
    return jnp.concatenate([loc[:BLK], oth[BLK:]], axis=0)


def project_qk_body(ids_ref, loc_ref, oth_ref, wa_ref, wb_ref, q_ref, qT_ref, k_ref, kT_ref):
    own = own_rows(loc_ref[...], oth_ref[...])
    for i, w in enumerate((wa_ref, wb_ref)):
        t = dot(own, w[:, :HI])
        cs = slice(i * HI, (i + 1) * HI)
        q_ref[:, cs] = t.astype(BF)
        qT_ref[cs, :] = t.T.astype(BF)
    project_rows(ids_ref, loc_ref, oth_ref, wa_ref, wb_ref, HI, k_ref, kT_ref)


def project_v_body(ids_ref, loc_ref, oth_ref, wa_ref, wb_ref, v_ref, vT_ref):
    project_rows(ids_ref, loc_ref, oth_ref, wa_ref, wb_ref, 0, v_ref, vT_ref)


def project_rows(ids_ref, loc_ref, oth_ref, wa_ref, wb_ref, col, k_ref, kT_ref):
    for d, rows in enumerate((loc_ref, oth_ref)):
        at = pl.multiple_of(lax.bitwise_xor(ids_ref[0], d) * HALF, HALF)
        for i, w in enumerate((wa_ref, wb_ref)):
            t = dot(rows[...], w[:, col : col + HI])
            cs = slice(i * HI, (i + 1) * HI)
            k_ref[pl.ds(at, HALF), cs] = t.astype(BF)
            kT_ref[cs, pl.ds(at, HALF)] = t.T.astype(BF)


def norm(v):
    inv = lax.rsqrt(jnp.mean(v * v, axis=-1, keepdims=True) + EPSILON)
    return v * inv, inv


def cast_body(q_ref, k_ref, v_ref, o_ref, in_ref, out_ref, qk_ref, vo_ref, ff_ref):
    qk_ref[:, :HI] = q_ref[...].astype(BF)
    qk_ref[:, HI:] = k_ref[...].astype(BF)
    vo_ref[:, :HI] = v_ref[...].astype(BF)
    vo_ref[:, HI:INNER] = o_ref[...].astype(BF)
    ff = in_ref.shape[1]
    ff_ref[:, :ff] = in_ref[...].astype(BF)
    ff_ref[:, ff:] = out_ref[:, : ff - PART].astype(BF)
    vo_ref[:, INNER:] = out_ref[:, ff - PART :].astype(BF)


def prepare_body(
    x_ref, xo_ref, c_ref, co_ref, gain_ref,
    loc_ref, oth_ref, actT_ref, own_ref, cown_ref, crest_ref, cT_ref,
):
    for src, dst, cs in ((x_ref, loc_ref, slice(0, HALF)), (xo_ref, oth_ref, slice(HALF, SEQ))):
        act = norm(src[...].astype(F32))[0] * gain_ref[...]
        dst[...] = act.astype(BF)
        actT_ref[:, cs] = act.T.astype(BF)
    own_ref[:BLK, :] = x_ref[:BLK, :]
    own_ref[BLK:, :] = xo_ref[BLK:, :]
    for dst, a, b, at in ((cown_ref, c_ref, co_ref, 0), (crest_ref, co_ref, c_ref, HALF)):
        dst[:BLK, :] = a[:BLK, :]
        dst[BLK:, :] = b[BLK:, :]
        cT_ref[:, at : at + BLK] = a[:BLK, :].astype(F32).T.astype(BF)
        cT_ref[:, at + BLK : at + HALF] = b[BLK:, :].astype(F32).T.astype(BF)


def middle_body(x_ref, h_ref, wa_ref, wb_ref, gain_ref, mid_ref, act_ref, actT_ref):
    mid = x_ref[...].astype(F32) + dot_nt(h_ref[:, :HI], wa_ref[:, HI:]) + dot_nt(h_ref[:, HI:], wb_ref[:, HI:])
    act = norm(mid)[0] * gain_ref[...]
    mid_ref[...] = mid
    act_ref[...] = act.astype(BF)
    actT_ref[...] = act.T.astype(BF)


def emit(me, scr_ref, cols, keep_ref, send_ref, outer_x):
    for e in range(16):
        x, y, z = e & 1, (e >> 1) & 1, e >> 2
        if me is None:
            ref, at, row = (keep_ref, send_ref)[e >> 3], e & 7, e * 48
        else:
            first, second = (x, y) if outer_x else (y, x)
            ref, at = (keep_ref, send_ref)[first], second * 4 + z
            row = pl.multiple_of(lax.bitwise_xor(me, e) * 48, 16)
        ref[at, :, cols] = scr_ref[pl.ds(row, 48), cols].astype(BF)


def gates(v):
    sq = v * v
    s = 0.5 * jnp.tanh(v * (0.7978845608028654 + 0.035677408136300125 * sq)) + 0.5
    slope = s + v * (1.5957691216057308 + 0.21406444881780075 * sq) * (s - s * s)
    return (v * s).astype(BF), slope


def ffn_body(
    xor, ids_ref, aown_ref, aoth_ref, aTown_ref, aToth_ref, cown_ref, coth_ref, cT_ref,
    win_ref, wouta_ref, woutb_ref, part_ref, outa_ref, outb_ref, gaa_ref, gab_ref, ka_ref, sa_ref, kb_ref, sb_ref,
    acco_ref, accg_ref, scr_ref,
):
    step = pl.program_id(0)
    last = pl.num_programs(0) - 1
    me = ids_ref[1] if xor else None

    @pl.when(step == 0)
    def _():
        acco_ref[...] = jnp.zeros_like(acco_ref)
        accg_ref[...] = jnp.zeros_like(accg_ref)

    win = win_ref[...]
    wout = jnp.concatenate(
        [wouta_ref[...], jnp.where(step == last, part_ref[...], woutb_ref[...])], axis=1
    )
    v0, v1 = dot(aown_ref[...], win), dot(aoth_ref[...], win)
    h0, s0 = gates(v0)
    g0 = dot(cown_ref[...], wout)
    h1, s1 = gates(v1)
    g1 = dot(coth_ref[...], wout)
    acco_ref[:HALF, :] += dot_nt(h0, wout)
    p0 = (g0.astype(BF).astype(F32) * s0).astype(BF)
    acco_ref[HALF:, :] += dot_nt(h1, wout)
    p1 = (g1.astype(BF).astype(F32) * s1).astype(BF)
    accg_ref[:HALF, :] += dot_nt(p0, win)
    accg_ref[HALF:, :] += dot_nt(p1, win)
    hid, gpre = (h0, h1), (p0, p1)
    scr_ref[...] = dot(cT_ref[:, :HALF], hid[0]) + dot(cT_ref[:, HALF:], hid[1])
    emit(me, scr_ref, slice(0, FT), ka_ref, sa_ref, True)
    scr_ref[...] = dot(aTown_ref[...], gpre[0]) + dot(aToth_ref[...], gpre[1])
    emit(me, scr_ref, slice(0, FT), kb_ref, sb_ref, False)

    @pl.when(step == last)
    def _():
        outa_ref[...] = acco_ref[:HALF, :]
        outb_ref[...] = acco_ref[HALF:, :].astype(BF)
        gaa_ref[...] = accg_ref[:HALF, :]
        gab_ref[...] = accg_ref[HALF:, :].astype(BF)


def ffn(xor, ids, aown, aoth, aTown, aToth, cown, coth, cT, w, part):
    width = (w.shape[1] + PART) // 2
    steps = width // FT
    tile = pl.BlockSpec((INNER, FT), lambda t: (0, t))
    end = w.shape[1] // PART - 1
    tile2 = pl.BlockSpec((INNER, PART), lambda t: (0, 2 * (steps + t)))
    tile3 = pl.BlockSpec((INNER, PART), lambda t: (0, jnp.minimum(2 * (steps + t) + 1, end)))
    grad = pl.BlockSpec((8, 48, FT), lambda t: (0, 0, t))
    half, halfT = full((HALF, INNER)), full((INNER, HALF))
    return pl.pallas_call(
        lambda *r: ffn_body(xor, *r),
        grid=(steps,),
        in_specs=[smem(), half, half, halfT, halfT, half, half, full((INNER, SEQ)), tile, tile2, tile3, full((INNER, PART))],
        out_specs=[half, half, half, half, grad, grad, grad, grad],
        out_shape=[
            sds((HALF, INNER), F32), sds((HALF, INNER)), sds((HALF, INNER), F32), sds((HALF, INNER)),
        ] + [sds((8, 48, width))] * 4,
        scratch_shapes=[
            pltpu.VMEM((SEQ, INNER), F32), pltpu.VMEM((SEQ, INNER), F32), pltpu.VMEM((INNER, FT), F32),
        ],
        compiler_params=params(44),
        cost_estimate=cost(14.5e9, 20e6, 1.6e6),
        name="ffn",
    )(ids, aown, aoth, aTown, aToth, cown, coth, cT, w, w, w, part)


def middle_back_body(
    ga_ref, gr_ref, mid_ref, cot_ref, gain_ref, h_ref, wa_ref, wb_ref,
    stay_ref, sent_ref, gh_ref, ghT_ref, gain_out, gwa_ref, gwb_ref,
):
    ga = ga_ref[...] + gr_ref[...].astype(F32)
    normed, inv = norm(mid_ref[...])
    scaled = ga * gain_ref[...]
    gm = cot_ref[...].astype(F32) + inv * (
        scaled - normed * jnp.mean(scaled * normed, axis=-1, keepdims=True)
    )
    gain_out[...] = jnp.sum(ga * normed, axis=0, keepdims=True)
    stay_ref[...] = gm[:BLK]
    sent_ref[...] = gm[BLK:]
    grad = gm.astype(BF)
    gT = gm.T.astype(BF)
    for i, (w, gw) in enumerate(((wa_ref, gwa_ref), (wb_ref, gwb_ref))):
        cs = slice(i * HI, (i + 1) * HI)
        t = dot(grad, w[:, HI:])
        gh_ref[:, cs] = t.astype(BF)
        ghT_ref[cs, :] = t.T.astype(BF)
        gw[...] = dot(gT, h_ref[:, cs]).astype(BF)


def joined(own, got):
    a, b = own.astype(F32), got.astype(F32)
    return jnp.concatenate([a[:HALF] + b[HALF:], a[HALF:] + b[:HALF]], axis=0).astype(BF)


def grad_vo_body(xor, ids_ref, aT_ref, gv_ref, rv_ref, go_ref, ro_ref, gv_out, ka, sa, kb, sb, scr):
    me = ids_ref[1] if xor else None
    gv = joined(gv_ref[...], rv_ref[...])
    gv_out[...] = gv
    scr[...] = dot(aT_ref[...], gv)
    emit(me, scr, slice(0, HI), ka, sa, True)
    scr[...] = go_ref[...].astype(F32) + ro_ref[...].astype(F32)
    emit(me, scr, slice(0, HI), kb, sb, False)


def grad_qk_body(xor, ids_ref, aT_ref, gq_ref, rq_ref, gk_ref, rk_ref, gq_out, gk_out, ka, sa, kb, sb, scr):
    me = ids_ref[1] if xor else None
    gq, rq = gq_ref[...], rq_ref[...]
    gq = jnp.concatenate([gq[:BLK], rq[BLK:], rq[:BLK], gq[BLK:]], axis=0)
    gq_out[...] = gq
    scr[...] = dot(aT_ref[...], gq)
    emit(me, scr, slice(0, HI), ka, sa, True)
    gk = joined(gk_ref[...], rk_ref[...])
    gk_out[...] = gk
    scr[...] = dot(aT_ref[...], gk)
    emit(me, scr, slice(0, HI), kb, sb, False)


def act_back_body(gq_ref, gk_ref, gv_ref, qk_ref, vo_ref, loc_ref, oth_ref):
    for rs, ref in ((slice(0, HALF), loc_ref), (slice(HALF, SEQ), oth_ref)):
        t = dot_nt(gq_ref[rs, :], qk_ref[:, :HI]) + dot_nt(gk_ref[rs, :], qk_ref[:, HI:])
        ref[...] = (t + dot_nt(gv_ref[rs, :], vo_ref[:, :HI])).astype(ref.dtype)


def output_body(mid_ref, own_ref, got_ref, stay_ref, sent_ref):
    out = (mid_ref[...] + own_ref[...] + got_ref[...].astype(F32)).astype(BF)
    stay_ref[...] = out[:BLK]
    sent_ref[...] = out[BLK:]


def join_body(stay_ref, got_ref, out_ref):
    out_ref[:BLK, :] = stay_ref[...]
    out_ref[BLK:, :] = got_ref[...]


def tokens_back_body(
    ga_ref, gr_ref, x_ref, gain_ref, stay_ref, got_ref, gain2_ref, gpre_ref, gpost_ref,
    out_ref, small_ref,
):
    ga = ga_ref[...] + gr_ref[...].astype(F32)
    normed, inv = norm(x_ref[...].astype(F32))
    scaled = ga * gain_ref[...]
    back = inv * (scaled - normed * jnp.mean(scaled * normed, axis=-1, keepdims=True))
    out_ref[:BLK, :] = (stay_ref[...] + back[:BLK]).astype(BF)
    out_ref[BLK:, :] = (got_ref[...] + back[BLK:]).astype(BF)
    gain1 = jnp.sum(ga * normed, axis=0, keepdims=True)
    small_ref[...] = jnp.zeros_like(small_ref)
    for i in range(6):
        cs = slice(i * 128, (i + 1) * 128)
        small_ref[i : i + 1, :] = gain1[:, cs]
        small_ref[8 + i : 9 + i, :] = gain2_ref[:, cs]
    small_ref[16 : 16 + HEADS, :HEADS] = jnp.sum(jnp.sum(gpre_ref[...], axis=2), axis=-1) * 0.125
    small_ref[32 : 32 + HEADS, :HEADS] = jnp.sum(jnp.sum(gpost_ref[...], axis=2), axis=-1)


def swap(v):
    return lax.ppermute(v, "tensor", [(0, 1), (1, 0)])


def hop(v, mask):
    n = lax.axis_size("dp")
    return lax.ppermute(v, "dp", [(i, i ^ mask) for i in range(n)])


def after(v, *done):
    return lax.optimization_barrier((v, *done))[0]


def place_body(ids_ref, ax, ay, bx, by, *outs):
    me = ids_ref[1]
    w = ax.shape[3]
    for t, ref in enumerate((ax, ay, bx, by)):
        col = (t // 2) * w
        for i in range(2):
            for j in range(4):
                e = 4 * j + ((2 * i + t) if t < 2 else (i + 2 * (t - 2)))
                row = pl.multiple_of(lax.bitwise_xor(me, e) * 48, 16)
                start = 0
                for out in outs:
                    end = start + out.shape[1]
                    lo, hi = max(col, start), min(col + w, end)
                    if lo < hi:
                        out[pl.ds(row, 48), lo - start : hi - start] = ref[i, j, :, lo - col : hi - col]
                    start = end


def gather_z(shard):
    return [shard] + [hop(shard, 4 * e) for e in range(1, 4)]


def gather_one(pieces):
    z = jnp.stack(pieces, axis=0)
    w = z.shape[2] // 2
    a, b = z[:, :, :w], z[:, :, w:]
    return a, hop(a, 2), b, hop(b, 1)


def gather_two(a, ra, b, rb):
    a2, b2 = jnp.stack([a, ra], axis=0), jnp.stack([b, rb], axis=0)
    return a2, hop(a2, 1), b2, hop(b2, 2)


def gathered(ids, parts, *outs):
    return once(place_body, outs, (ids, *parts), "place")


def fold_one_body(ka, ra, kb, rb, oka, osa, okb, osb):
    for k, r, keep, send in ((ka, ra, oka, osa), (kb, rb, okb, osb)):
        t = (k[...].astype(F32) + r[...].astype(F32)).astype(BF)
        keep[...] = t[:4]
        send[...] = t[4:]


def fold_two_body(ka, ra, kb, rb, small, got, own, total, *sends):
    w = ka.shape[2]
    for k, r, cs in ((ka, ra, slice(0, w)), (kb, rb, slice(w, 2 * w))):
        t = k[...].astype(F32) + r[...].astype(F32)
        own[:, cs] = t[0]
        for e in range(3):
            sends[e][:, cs] = t[e + 1].astype(BF)
    v = (small[...] + got[...]).astype(BF)
    total[...] = v.astype(F32)
    for send in sends:
        send[:, 2 * w :] = v


def fold_one(ka, ra, kb, rb):
    piece = sds((4,) + ka.shape[1:])
    return once(fold_one_body, (piece,) * 4, (ka, ra, kb, rb), "fold_one", scalars=0)


def fold_two(*parts):
    w = 2 * parts[0].shape[2]
    outs = (sds((48, w), F32), sds((48, 128), F32)) + (sds((48, w + 128)),) * 3
    return once(fold_two_body, outs, parts, "fold_two", scalars=0)


def fold_ff_body(ka, ra, kb, rb, own, send):
    w = ka.shape[2]
    for k, r, cs in ((ka, ra, slice(0, w)), (kb, rb, slice(w, 2 * w))):
        t = (k[...].astype(F32) + r[...].astype(F32)).astype(BF)
        for z in range(2):
            own[z, :, cs] = t[2 * z]
            send[z, :, cs] = t[2 * z + 1]


def fold_at_body(*refs):
    ins, outs = refs[:8], refs[8:]
    for i in range(4):
        k, r = ins[2 * i], ins[2 * i + 1]
        kept, sent = outs[2 * (i // 2)], outs[2 * (i // 2) + 1]
        cs = slice((i % 2) * HI, (i % 2) * HI + HI)
        t = (k[...].astype(F32) + r[...].astype(F32)).astype(BF)
        kept[:, :, cs] = t[:4]
        sent[:, :, cs] = t[4:]


def fold_ff_two_body(own, got, keep, send):
    t = own[...].astype(F32) + got[...].astype(F32)
    keep[...] = t[0]
    send[...] = t[1].astype(BF)


def finish_ff_body(own, got, in_ref, out_ref):
    w = out_ref.shape[1]
    out_ref[...] = own[:, :w] + got[:, :w].astype(F32)
    in_ref[...] = own[:, w:] + got[:, w:].astype(F32)


def finish_body(own, total, a, b, c, *outs):
    def got(cs):
        return a[:, cs].astype(F32) + b[:, cs].astype(F32) + c[:, cs].astype(F32)

    for i, ref in enumerate(outs[:4]):
        cs = slice(i * HI, (i + 1) * HI)
        ref[...] = own[:, cs] + got(cs)
    at = 4 * HI
    cs = slice(at, at + 128)
    near = total[...] + a[:, cs].astype(F32)
    split_small(near + (b[:, cs].astype(F32) + c[:, cs].astype(F32)), *outs[4:])


def split_small(v, gain1, gain2, gpre, gpost):
    for i in range(6):
        gain1[i * 128 : (i + 1) * 128] = v[i]
        gain2[i * 128 : (i + 1) * 128] = v[8 + i]
    gpre[...] = v[16 : 16 + HEADS, :HEADS]
    gpost[...] = v[32:48].T[:HEADS, :HEADS]


def split_small_body(v, *outs):
    split_small(v[...], *outs)


def scatter_plain(ka, sa, kb, sb):
    w = ka.shape[2]
    flat = jnp.concatenate(
        [jnp.concatenate([k, s], axis=0).reshape(768, w) for k, s in ((ka, sa), (kb, sb))], axis=1
    )
    return lax.psum_scatter(flat.astype(F32), "dp", scatter_dimension=0, tiled=True)


def sum_all(v):
    n = lax.axis_size("dp")
    v = v + swap(v)
    bit = 1
    while bit < n:
        v = v + hop(v, bit)
        bit *= 2
    return v


def on_device(
    tokens, cotangent, segment_ids, norm1_gain, w_query, w_key, w_value, pre_mix, post_mix,
    w_output, norm2_gain, w_in, w_out,
):
    ids = jnp.stack([lax.axis_index("tensor"), lax.axis_index("dp")]).astype(jnp.int32)
    xor = lax.axis_size("dp") == 16
    low = lambda v: v.astype(BF)
    D = norm1_gain.shape[0]
    tie = lax.optimization_barrier
    gain1, gain2 = norm1_gain.reshape(1, D), norm2_gain.reshape(1, D)
    seg = segment_ids.reshape(1, SEQ)

    every = lambda v: lax.all_gather(v, "dp", axis=0, tiled=True)
    r, ff = w_in.shape
    shard_qk, shard_vo, shard_ff = once(
        cast_body, (sds((r, INNER)), sds((r, INNER + PART)), sds((r, 2 * ff - PART))),
        tuple(far(w) for w in (w_query, w_key, w_value, w_output.T, w_in, w_out.T)), "cast", scalars=0,
    )
    if xor:
        z_qk = gather_z(shard_qk)
    w_ff = every(shard_ff)
    x_oth, cot_oth = swap(tokens), swap(cotangent)
    act_loc, act_oth, actT, x_own, cot_own, cot_rest, cotT = once(
        prepare_body,
        (
            sds((HALF, D)), sds((HALF, D)), hbm((D, SEQ)), hbm((HALF, D)), hbm((HALF, D)),
            hbm((HALF, D)), hbm((D, SEQ)),
        ),
        (far(tokens), x_oth, far(cotangent), cot_oth, gain1), "prepare", scalars=0,
    )
    if xor:
        *z_qk, act_loc = tie((*z_qk, act_loc))
        a, ra, b, rb = gather_one(z_qk)
        z_vo = gather_z(after(shard_vo, *z_qk))
        qk_parts = gather_two(a, ra, b, rb)
        *z_vo, ax, ay, bx, by = tie((*z_vo, *qk_parts))
        a, ra, b, rb = gather_one(z_vo)
        (w_qk,) = gathered(ids, (ax, ay, bx, by), sds((D, INNER)))
    else:
        w_qk, w_vo = every(shard_qk), every(shard_vo)
        w_vo, w_part = w_vo[:, :INNER], w_vo[:, INNER:]
    q, qT, k, kT = once(
        project_qk_body,
        (hbm((HALF, INNER)), sds((INNER, HALF)), sds((SEQ, INNER)), hbm((INNER, SEQ))),
        (ids, act_loc, act_oth, w_qk, swap(w_qk)), "project_qk", flops=1.8e9,
    )
    if xor:
        ra, rb, k = tie((ra, rb, k))
        vo_parts = gather_two(a, ra, b, rb)
        k = after(k, vo_parts[0], vo_parts[2])
    pT = logits_softmax(ids, pre_mix, seg, k, qT)
    if xor:
        w_vo, w_part = gathered(ids, tie((*vo_parts, pT))[:4], sds((D, INNER)), hbm((D, PART)))
    vo_o = swap(w_vo)
    v, vT = once(
        project_v_body, (hbm((SEQ, INNER)), sds((INNER, SEQ))),
        (ids, act_loc, act_oth, w_vo, vo_o), "project_v", flops=1.2e9,
    )
    uT, heads = attend(ids, post_mix, vT, pT)
    mid, act2, act2T = once(
        middle_body, (hbm((HALF, D), F32), hbm((HALF, D)), hbm((D, HALF))),
        (x_own, heads, w_vo, vo_o, gain2), "middle", scalars=0, flops=6e8,
    )
    out_own, out_oth, ga_own, ga_oth, ka, sa, kb, sb = ffn(
        xor, ids, far(act2), far(swap(act2)), far(act2T), far(swap(act2T)), far(cot_own), far(cot_rest), far(cotT), far(w_ff), far(w_part)
    )
    if xor:
        ra, rb = hop(sa, 1), hop(sb, 2)
    stay, sent, gh, ghT, gain2_part, gwo, gwo_o = once(
        middle_back_body,
        (
            hbm((BLK, D), F32), hbm((BLK, D), F32), sds((HALF, INNER)), sds((INNER, HALF)),
            hbm((1, D), F32), sds((D, HI)), sds((D, HI)),
        ),
        (ga_own, swap(ga_oth), mid, cot_own, gain2, heads, w_vo, vo_o),
        "middle_back", scalars=0, flops=1.2e9,
    )
    got_sent, got_out, gwo_r = swap(sent), swap(out_oth), swap(gwo_o)
    gL, gv, gv_o, gpost = attend_back(ids, post_mix, v, ghT, gh, pT, uT)
    grads = (sds((8, 48, HI)),) * 4
    if xor:
        gv, gv_o, got_sent, got_out, gwo_r = tie((gv, gv_o, got_sent, got_out, gwo_r))
    gv, *vo = once(
        lambda *r: grad_vo_body(xor, *r), (hbm((SEQ, HI)),) + grads,
        (ids, actT, gv, swap(gv_o), gwo, gwo_r), "grad_vo",
        scratch=[pltpu.VMEM((D, HI), F32)], flops=6e8,
    )
    if xor:
        vo_ka, vo_sa, vo_kb, vo_sb = vo
        ra, rb = tie((ra, rb, vo_sa))[:2]
        ff_ka, ff_sa, ff_kb, ff_sb = fold_one(ka, ra, kb, rb)
        ff_ra, ff_rb = hop(ff_sa, 2), hop(ff_sb, 1)
        gL = after(gL, ff_sa, vo_sa)
    gq, gq_o, gk, gk_o, gpre = scores_back(ids, pre_mix, kT, qT, q, gL)
    if xor:
        ff_ra, ff_rb, gq, gq_o, gk_o = tie((ff_ra, ff_rb, gq, gq_o, gk_o))
        wide = ff_ka.shape[2] * 2
        ff_own, ff_send = once(
            fold_ff_body, (sds((2, 48, wide)),) * 2, (ff_ka, ff_ra, ff_kb, ff_rb), "fold_ff", scalars=0
        )
        ff_got = hop(ff_send, 4)
        vo_sa, vo_sb = tie((vo_sa, vo_sb, ff_send))[:2]
        vo_ra, vo_rb = hop(vo_sa, 1), hop(vo_sb, 2)
        gq, gk = tie((gq, gk, ff_send))[:2]
    gq, gk, *qk = once(
        lambda *r: grad_qk_body(xor, *r), (sds((SEQ, HI)),) * 2 + grads,
        (ids, actT, gq, swap(gq_o), gk, swap(gk_o)), "grad_qk",
        scratch=[pltpu.VMEM((D, HI), F32)], flops=1.2e9,
    )
    if xor:
        qk_ka, qk_sa, qk_kb, qk_sb = qk
        qk_ra, qk_rb = hop(qk_sa, 1), hop(qk_sb, 2)
        gq, vo_ra, vo_rb = tie((gq, vo_ra, vo_rb))
    ga_loc, ga_oth = once(
        act_back_body, (sds((HALF, D), F32), sds((HALF, D))), (gq, gk, gv, w_qk, w_vo),
        "act_back", scalars=0, flops=0.3e9, moved=1,
    )
    ga_got = swap(ga_oth)
    if xor:
        ff_own, ff_got = tie((ff_own, ff_got, ga_oth))[:2]
        ff_own, ff_send = once(
            fold_ff_two_body, (sds((48, wide), F32), sds((48, wide))), (ff_own, ff_got), "fold_ff_two", scalars=0,
            flops=2e9, moved=1,
        )
        ff_got = hop(ff_send, 8)
        qk_ra, qk_rb, ff_two = tie((qk_ra, qk_rb, ff_send))
        at_ka, at_sa, at_kb, at_sb = once(
            fold_at_body, (sds((4, 48, INNER)),) * 4,
            (qk_ka, qk_ra, vo_ka, vo_ra, qk_kb, qk_rb, vo_kb, vo_rb), "fold_at", scalars=0, flops=5e9,
        )
        at_ra, at_rb = hop(at_sa, 2), hop(at_sb, 1)
        ga_loc, ga_got = tie((ga_loc, ga_got, at_sa))[:2]
    grad_tokens, small = once(
        tokens_back_body, (sds((HALF, D)), sds((48, 128), F32)),
        (ga_loc, ga_got, tokens, gain1, stay, got_sent, gain2_part, gpre, gpost),
        "tokens_back", scalars=0,
    )
    r = w_in.shape[0]
    part = sds((r, HI), F32)
    small_outs = (sds((D,), F32),) * 2 + (sds((HEADS, HEADS), F32),) * 2
    if xor:
        got = swap(small)
        mid, small = tie((mid, small))
        out_stay, out_sent = once(
            output_body, (sds((BLK, D)), sds((BLK, D))), (mid, out_own, got_out), "output", scalars=0
        )
        out_got = swap(out_sent)
        small, got = tie((small, got, out_sent))[:2]
        small = small + got
        small = small + hop(small, 1)
        got = hop(small, 2)
        at_ra, at_rb, got, small, ff_got = tie((at_ra, at_rb, got, small, ff_got))
        at, total, *sends = fold_two(at_ka, at_ra, at_kb, at_rb, small, got)
        gots = [hop(sends[e], 4 * (e + 1)) for e in range(3)]
        out_got = tie((out_got, at))[0]
        (output,) = once(join_body, (sds((HALF, D)),), (out_stay, out_got), "join", scalars=0)
        grad_in, grad_out = once(
            finish_ff_body, (sds((r, ff), F32),) * 2, (ff_own, ff_got), "finish_ff", scalars=0
        )
        gots = tie((*gots, output, grad_in))[:3]
        grad_q, grad_v, grad_k, grad_o, *sums = once(
            finish_body, (part,) * 4 + small_outs, (at, total, *gots), "finish", scalars=0
        )
    else:
        grad_qk, grad_vo = scatter_plain(*qk), scatter_plain(*vo)
        grad_ffn = scatter_plain(ka, sa, kb, sb)
        grad_q, grad_k, grad_v, grad_o = grad_qk[:, :HI], grad_qk[:, HI:], grad_vo[:, :HI], grad_vo[:, HI:]
        grad_in, grad_out = grad_ffn[:, ff:], grad_ffn[:, :ff]
        sums = once(split_small_body, small_outs, (sum_all(small),), "split_small", scalars=0)
        out_stay, out_sent = once(
            output_body, (sds((BLK, D)), sds((BLK, D))), (mid, out_own, got_out), "output", scalars=0
        )
        output = jnp.concatenate([out_stay, swap(out_sent)], axis=0)
    return (
        output, grad_tokens, sums[0], grad_q, grad_k, grad_v, sums[2], sums[3],
        grad_o.T, sums[1], grad_in, grad_out.T,
    )


def solution(mesh):
    rows = P(("dp", "tensor"), None)
    w, wt = P("dp", "tensor"), P("tensor", "dp")
    return jax.shard_map(
        on_device,
        mesh=mesh,
        in_specs=(rows, rows, P("dp"), P(), w, w, w, P(), P(), wt, P(), w, wt),
        out_specs=(rows, rows, P(), w, w, w, P(), P(), wt, P(), w, wt),
        check_vma=False,
    )
```
